32 devices in a mesh: groups: 2 (over y), seq: 4 (over z), head: 2 (over x), sub: 2 (over core).
Axes of the slice: x: 2, y: 2, z: 4, core: 2. Of those that a mesh axis runs over, the one named last changes fastest.
Arguments:
- inputs: bfloat16 [16384, 1536], P(('groups', 'seq'), ('head', 'sub')), parts along dimension 0, may hold values from -6 to 6
- b_proj: bfloat16 [16384, 128], P(('groups', 'seq')), parts along dimension 0, may hold values from -0.109375 to 0.109375
- c_proj: bfloat16 [16384, 128], P(('groups', 'seq')), parts along dimension 0, may hold values from -6 to 6
- step_codes: int32 [24, 16384], P(('head', 'sub'), ('groups', 'seq')), parts along dimension 1, may hold values from 0 to 3
- gate_codes: int32 [16384], P(('groups', 'seq')), parts along dimension 0, may hold values from 0 to 2
- decay_rates: float32 [24], P(('head', 'sub')), may hold values from 1.8310547e-05 to 0.12
- skip_gain: float32 [24], P(('head', 'sub')), may hold values from 0.5 to 1.5
- conv_weight: float32 [4, 1536], P(None, ('head', 'sub')), may hold values from -3 to 3
- out_cotangent: bfloat16 [16384, 1536], P(('groups', 'seq'), ('head', 'sub')), parts along dimension 0, may hold values from -6 to 6
Outputs:
- layer_out: bfloat16 [16384, 1536], P(('groups', 'seq'), ('head', 'sub')), parts along dimension 0
- input_grad: bfloat16 [16384, 1536], P(('groups', 'seq'), ('head', 'sub')), parts along dimension 0
- conv_grad: float32 [8, 1536], P('groups', ('head', 'sub')), parts along dimension 0
The draws below stay inside these ranges and needn't reach their ends.
There are 2 independent parts, one for each index of `groups`. The reference program is written for one: setup_inputs(seed, part) draws one part's arguments, and reference() takes and returns one part's arrays. A program takes and returns all parts, laid end to end along the dimension named above; an argument that names none is the same for every part. Nothing has to cross between parts.
All inputs are finite; a program needn't handle non-finite values.
Results may differ from the reference program's by a relative error of at most 0.0062.
Values may be sent and summed in bfloat16 or wider, within the bound.
No kernel may reach another device: no remote copies, remote signals or barrier semaphores. Data moves between devices by JAX's collectives and lax.ppermute only.
A program may use at most 64 MiB of HBM per device.

```python
import math
import jax
import jax.numpy as jnp
from jax import lax

HEADS = 24
HEAD_DIM = 64
STATE = 128
CONV = 4
BLOCK = 512
TOK_DEV = 2048
TOKENS = 8192
CHANNELS = 1536


def draw_decay_rates(key, part):
    slow_key = jax.random.fold_in(key, 1)
    fast_key = jax.random.fold_in(key, 2)
    pick_key = jax.random.fold_in(key, 3)
    slow_rate = jnp.exp(jax.random.uniform(slow_key, (HEADS,), jnp.float32, math.log(0.15), math.log(0.8))) / TOKENS
    fast_rate = jnp.exp(jax.random.uniform(fast_key, (HEADS,), jnp.float32, math.log(0.07), math.log(0.12)))
    chosen = jax.random.bernoulli(pick_key, 0.5, (HEADS,))
    return jnp.where(chosen, fast_rate, slow_rate).astype(jnp.float32)


def draw_step_codes(key, part):
    base_key = jax.random.fold_in(key, 4)
    jitter_key = jax.random.fold_in(key, 5)
    device_count = TOKENS // TOK_DEV
    base_code = jax.random.randint(base_key, (HEADS, device_count, 1), 0, 2, dtype=jnp.int32)
    jitter = jax.random.randint(jitter_key, (HEADS, device_count, TOK_DEV), 0, 3, dtype=jnp.int32)
    return (base_code + jitter).reshape(HEADS, TOKENS).astype(jnp.int32)


def draw_gate_codes(key, part):
    place_key = jax.random.fold_in(key, 6)
    level_key = jax.random.fold_in(key, 7)
    places = jax.random.randint(place_key, (2,), 0, TOKENS, dtype=jnp.int32)
    levels = jnp.stack([jnp.int32(2), jax.random.randint(level_key, (), 1, 3, dtype=jnp.int32)])
    hits = jnp.arange(TOKENS, dtype=jnp.int32)[:, None] == places[None, :]
    return jnp.max(jnp.where(hits, levels[None, :], 0), axis=1).astype(jnp.int32)


def block_scale(stream_key, extent, pieces, low, high):
    def one(axis_at, blocks):
        heights = jax.random.uniform(jax.random.fold_in(jax.random.fold_in(stream_key, 6), axis_at), (blocks,), jnp.float32, low / len(pieces), high / len(pieces))
        return jnp.repeat(jnp.exp(heights), extent[axis_at] // blocks).reshape((-1,) + (1,) * (len(extent) - axis_at - 1))

    level = one(*pieces[0])
    for cut in pieces[1:]:
        level = level * one(*cut)
    return level


def scatter_about(own_key, dims, width, bound, shards=(), held_as=jnp.bfloat16):
    loudness = block_scale(own_key, dims, shards, -0.22, 0.18) if shards else 1.0
    values = jax.random.normal(own_key, dims, jnp.float32) * width * loudness
    return jnp.minimum(jnp.maximum(values, -bound), bound).astype(held_as)


def setup_inputs(seed: int = 0, part: int = 0) -> dict:
    seeds = jax.random.split(jax.random.key(seed), 10)
    part_keys = jax.random.split(jax.random.fold_in(seeds[9], part), 10)
    return {
        "inputs": scatter_about(part_keys[0], (TOKENS, CHANNELS), 1.0, 6.0, ((0, 4), (1, 4))),
        "b_proj": scatter_about(part_keys[1], (TOKENS, STATE), (0.7 * TOKENS ** -0.5), 0.109375, ((0, 4),)),
        "c_proj": scatter_about(part_keys[2], (TOKENS, STATE), 1.0, 6.0, ((0, 4),)),
        "step_codes": draw_step_codes(jax.random.fold_in(jax.random.fold_in(seeds[9], part), 71), part),
        "gate_codes": draw_gate_codes(jax.random.fold_in(jax.random.fold_in(seeds[9], part), 71), part),
        "decay_rates": draw_decay_rates(jax.random.fold_in(seeds[9], 71), part),
        "skip_gain": jnp.clip(0.5 + 1.0 * jax.random.uniform(seeds[6], (HEADS,), jnp.float32) ** block_scale(seeds[6], (HEADS,), ((0, 4),), -0.2, 0.2), 0.5, 1.5),
        "conv_weight": scatter_about(seeds[7], (CONV, CHANNELS), CONV ** -0.5, 3.0, ((1, 4),), jnp.float32),
        "out_cotangent": scatter_about(part_keys[8], (TOKENS, CHANNELS), 1.0, 6.0, ((0, 4), (1, 4))),
    }


def rounded(values):
    return lax.optimization_barrier(values.astype(jnp.bfloat16)).astype(jnp.float32)


def block_weights(c_block, b_block, cum_block, step_block):
    scores = jnp.dot(c_block, b_block.T, preferred_element_type=jnp.float32)
    spread = cum_block[:, :, None] - cum_block[:, None, :]
    causal = jnp.arange(BLOCK)[:, None] >= jnp.arange(BLOCK)[None, :]
    decays = jnp.exp(jnp.where(causal[None], spread, -jnp.inf))
    return rounded(scores[None] * decays * step_block[:, None, :])


def reference(inputs, b_proj, c_proj, step_codes, gate_codes, decay_rates, skip_gain, conv_weight, out_cotangent):
    highest = lax.Precision.HIGHEST
    padded = jnp.concatenate([jnp.zeros((CONV - 1, CHANNELS), inputs.dtype), inputs], axis=0)
    preact = jnp.zeros((TOKENS, CHANNELS), jnp.float32)
    for offset in range(CONV):
        preact = preact + conv_weight[offset] * padded[offset:offset + TOKENS].astype(jnp.float32)
    mixed_in = jax.nn.silu(preact).astype(jnp.bfloat16)
    step_size = jnp.exp2(-step_codes.astype(jnp.float32))
    log_decay = -decay_rates[:, None] * step_size + jnp.log(1.0 - gate_codes.astype(jnp.float32) / 4.0)[None, :]
    block_count = TOKENS // BLOCK
    cum_decay = jnp.cumsum(log_decay.reshape(HEADS, block_count, BLOCK), axis=-1).transpose(1, 0, 2)
    step_blocks = step_size.reshape(HEADS, block_count, BLOCK).transpose(1, 0, 2)
    mixed_blocks = mixed_in.reshape(block_count, BLOCK, HEADS, HEAD_DIM).astype(jnp.float32)
    grad_blocks = out_cotangent.reshape(block_count, BLOCK, HEADS, HEAD_DIM).astype(jnp.float32)
    b_blocks = b_proj.reshape(block_count, BLOCK, STATE)
    c_blocks = c_proj.reshape(block_count, BLOCK, STATE)

    def forward_block(carry_state, block_data):
        mixed_b, b_block, c_block, cum_block, step_block = block_data
        weights = block_weights(c_block, b_block, cum_block, step_block)
        inner_part = jnp.einsum('hts,shp->thp', weights, mixed_b, precision=highest)
        carried = jnp.einsum('tn,hpn->thp', c_block.astype(jnp.float32), rounded(carry_state), precision=highest)
        carried = carried * jnp.exp(cum_block).T[:, :, None]
        result = skip_gain[None, :, None] * mixed_b + inner_part + carried
        block_total = cum_block[:, -1]
        scaled = rounded(mixed_b * (jnp.exp(block_total[:, None] - cum_block) * step_block).T[:, :, None])
        fresh_state = jnp.einsum('thp,tn->hpn', scaled, b_block.astype(jnp.float32), precision=highest)
        return jnp.exp(block_total)[:, None, None] * carry_state + fresh_state, result.astype(jnp.bfloat16)

    def backward_block(adjoint, block_data):
        grad_b, b_block, c_block, cum_block, step_block = block_data
        weights = block_weights(c_block, b_block, cum_block, step_block)
        inner_part = jnp.einsum('hst,shp->thp', weights, grad_b, precision=highest)
        block_total = cum_block[:, -1]
        factor = (step_block * jnp.exp(block_total[:, None] - cum_block)).T
        carried = jnp.einsum('tn,hpn->thp', b_block.astype(jnp.float32), rounded(adjoint), precision=highest)
        carried = carried * factor[:, :, None]
        result = skip_gain[None, :, None] * grad_b + inner_part + carried
        scaled = rounded(grad_b * jnp.exp(cum_block).T[:, :, None])
        fresh_adjoint = jnp.einsum('thp,tn->hpn', scaled, c_block.astype(jnp.float32), precision=highest)
        return jnp.exp(block_total)[:, None, None] * adjoint + fresh_adjoint, result

    zero_state = jnp.zeros((HEADS, HEAD_DIM, STATE), jnp.float32)
    unused_state, layer_out = lax.scan(forward_block, zero_state, (mixed_blocks, b_blocks, c_blocks, cum_decay, step_blocks))
    unused_adjoint, grad_in = lax.scan(backward_block, zero_state, (grad_blocks, b_blocks, c_blocks, cum_decay, step_blocks), reverse=True)
    grad_in = grad_in.reshape(TOKENS, CHANNELS)
    gate_value = jax.nn.sigmoid(preact)
    grad_pre = grad_in * gate_value * (1.0 + preact * (1.0 - gate_value))
    extended = jnp.concatenate([grad_pre, jnp.zeros((CONV - 1, CHANNELS), jnp.float32)], axis=0)
    input_grad = jnp.zeros((TOKENS, CHANNELS), jnp.float32)
    for offset in range(CONV):
        shift_from = CONV - 1 - offset
        input_grad = input_grad + conv_weight[offset] * extended[shift_from:shift_from + TOKENS]
    tap_sums = [jnp.sum(grad_pre * padded[offset:offset + TOKENS].astype(jnp.float32), axis=0) for offset in range(CONV)]
    conv_grad = jnp.stack(tap_sums) * TOKENS ** -0.5
    return layer_out.reshape(TOKENS, CHANNELS), input_grad.astype(jnp.bfloat16), conv_grad
```

```python
import functools

import jax
import jax.numpy as jnp
from jax import lax
from jax.experimental import pallas as pl
from jax.experimental.pallas import tpu as pltpu
from jax.sharding import PartitionSpec as P

CHUNK = 128
STEP_ROWS = 512
LOG_ONE = -0.2876820724517809
LOG_TWO = -0.6931471805599453
F32 = jnp.float32
BF16 = jnp.bfloat16
HIGHEST = lax.Precision.HIGHEST
VMEM_LIMIT = 48 * 1024 * 1024


def dot(a, b, dims, precision=None):
    return lax.dot_general(a, b, (dims, ((), ())), preferred_element_type=F32, precision=precision)


def per_lane(scalars, count, channels):
    width = channels // count
    lane = lax.broadcasted_iota(jnp.int32, (1, channels), 1)
    row = jnp.zeros((1, channels), F32)
    for head in range(count):
        inside = (lane >= head * width) & (lane < (head + 1) * width)
        row = jnp.where(inside, scalars[head], row)
    return row


def split_two(value):
    high = value.astype(BF16)
    low = (value - high.astype(F32)).astype(BF16)
    return jnp.concatenate([high.astype(F32), low.astype(F32)], axis=0).astype(BF16)


def spread_matrix(count, channels):
    width = channels // count
    row = lax.broadcasted_iota(jnp.int32, (16, channels), 0)
    lane = lax.broadcasted_iota(jnp.int32, (16, channels), 1)
    return jnp.where((row % 8) == lane // width, 1.0, 0.0).astype(BF16)


def spread(pair, onehot):
    return dot(pair, onehot, ((0,), (0,)))


def adjoint_kernel(
    heads, rates, codes, gates, grad, c_proj, near_out, far_out, logs_out, pay_out,
    steps, front, total,
):
    rows = codes.shape[1]
    channels = grad.shape[1]
    chunks = rows // CHUNK
    step = pl.program_id(0)

    @pl.when(step == 0)
    def prepare():
        steps[...] = jnp.zeros_like(steps)
        steps[0:heads, :] = jnp.exp2(-codes[...].astype(F32))
        gate = gates[...]
        steps[6:7, :] = jnp.where(gate == 1, 1.0, 0.0).astype(F32)
        steps[7:8, :] = jnp.where(gate == 2, 1.0, 0.0).astype(F32)
        stacked = jnp.concatenate(
            [steps[:, j * CHUNK : (j + 1) * CHUNK] for j in range(chunks)], axis=0
        ).astype(BF16)
        low = lax.broadcasted_iota(jnp.int32, (CHUNK, CHUNK), 0)
        high = lax.broadcasted_iota(jnp.int32, (CHUNK, CHUNK), 1)
        upper = jnp.where(low <= high, 1.0, 0.0).astype(BF16)
        sums = dot(stacked, upper, ((1,), (0,)))
        sub = lax.broadcasted_iota(jnp.int32, (8, CHUNK), 0)
        rate = jnp.zeros((8, CHUNK), F32)
        for head in range(heads):
            rate = jnp.where(sub == head, rates[head], rate)
        cums, mids, befores = [], [], []
        before = jnp.zeros((8, 1), F32)
        for j in range(chunks):
            part = sums[8 * j : 8 * j + 8, :]
            cum = LOG_ONE * part[6:7, :] + LOG_TWO * part[7:8, :] - rate * part
            cums.append(cum)
            mids.append(cum[:, CHUNK // 2 - 1 : CHUNK // 2])
            befores.append(before)
            before = before + cum[:, CHUNK - 1 : CHUNK]
        for j in range(chunks):
            at = slice(j * CHUNK, (j + 1) * CHUNK)
            size = steps[:, at]
            near_out[0:16, at] = split_two(jnp.exp(cums[j] - mids[j]))
            near_out[16:32, at] = split_two(jnp.exp(mids[j] - cums[j]) * size)
            front[:, at] = split_two(jnp.exp(befores[j] + cums[j]))
            far_out[:, at] = split_two(jnp.exp(before - befores[j] - cums[j]) * size)
        pick = lax.broadcasted_iota(jnp.int32, (8, CHUNK), 0)
        place = lax.broadcasted_iota(jnp.int32, (8, CHUNK), 1)
        chosen = jnp.where((pick == 0) | ((pick == 1) & (place < CHUNK // 2)), 1.0, 0.0)
        flat = dot(chosen.astype(BF16), stacked, ((1,), (1,)))
        owner = lax.broadcasted_iota(jnp.int32, (chunks, 8 * chunks), 1) // 8
        chunk_at = lax.broadcasted_iota(jnp.int32, (chunks, 8 * chunks), 0)
        lane_rate = per_lane(rates, heads, channels)
        kind = lax.broadcasted_iota(jnp.int32, (8 * chunks, channels), 0) % 8
        lane_head = lax.broadcasted_iota(jnp.int32, (8 * chunks, channels), 1) // (
            channels // heads
        )
        mixer = jnp.where(kind == lane_head, -lane_rate, 0.0)
        mixer = jnp.where(kind == 6, LOG_ONE, jnp.where(kind == 7, LOG_TWO, mixer))
        table = []
        for which in range(2):
            own = jnp.where(owner == chunk_at, flat[which : which + 1, :], 0.0)
            table.append(dot(own, mixer, ((1,), (0,)), HIGHEST))
        logs_out[0] = jnp.exp(table[0])
        logs_out[1] = jnp.exp(table[1])
        logs_out[2] = jnp.exp(table[0] - table[1])
        decay = jnp.exp(jnp.sum(table[0], axis=0, keepdims=True))
        first = decay.astype(BF16).astype(F32)
        second = (decay - first).astype(BF16).astype(F32)
        third = decay - first - second
        row = lax.broadcasted_iota(jnp.int32, (16, channels), 0)
        tail = jnp.where(
            row == 0, first, jnp.where(row == 1, second, jnp.where(row == 2, third, 0.0))
        )
        pay_out[128:144, :] = tail.astype(BF16)
        total[...] = jnp.zeros_like(total)

    onehot = spread_matrix(heads, channels)
    here = pl.multiple_of(step * STEP_ROWS, STEP_ROWS)
    scale = spread(front[:, pl.ds(here, STEP_ROWS)], onehot)
    scaled = (grad[...].astype(F32) * scale).astype(BF16)
    total[...] += dot(c_proj[...], scaled, ((0,), (0,)))

    @pl.when(step == pl.num_programs(0) - 1)
    def finish():
        pay_out[0:128, :] = total[...].astype(BF16)


def state_kernel(
    heads, parts, taps, far, inputs, halo, b_proj, adjoint_pay, mixed_out, slope_out, *rest
):
    pays, (window, total) = rest[: parts - 1], rest[parts - 1 :]
    channels = inputs.shape[1]
    step = pl.program_id(0)

    @pl.when(step == 0)
    def first():
        window[0:16, :] = halo[...].astype(F32)
        total[...] = jnp.zeros_like(total)

    @pl.when(step > 0)
    def later():
        window[0:16, :] = window[STEP_ROWS : STEP_ROWS + 16, :]

    window[16 : STEP_ROWS + 16, :] = inputs[...].astype(F32)
    onehot = spread_matrix(heads, channels)
    scaled = []
    for q in range(STEP_ROWS // CHUNK):
        at = q * CHUNK
        preact = taps[0:1, :] * window[13 + at : 13 + at + CHUNK, :]
        for k in range(1, 4):
            preact = preact + taps[k : k + 1, :] * window[13 + k + at : 13 + k + at + CHUNK, :]
        sigma = 1.0 / (1.0 + jnp.exp(-preact))
        mixed = preact * sigma
        slope_out[at : at + CHUNK, :] = sigma + mixed * (1.0 - sigma)
        mixed_out[at : at + CHUNK, :] = mixed.astype(BF16)
        scale = spread(far[:, at : at + CHUNK], onehot)
        scaled.append((mixed * scale).astype(BF16))
    total[...] += dot(b_proj[...], jnp.concatenate(scaled, axis=0), ((0,), (0,)))

    @pl.when(step == pl.num_programs(0) - 1)
    def finish():
        me = lax.axis_index("seq")
        state = total[...].astype(BF16)
        for distance in range(1, parts):
            forward = me + distance < parts

            @pl.when(forward)
            def send_state():
                pays[distance - 1][0:128, :] = state
                pays[distance - 1][128:144, :] = adjoint_pay[128:144, :]

            @pl.when(jnp.logical_not(forward))
            def send_adjoint():
                pays[distance - 1][...] = adjoint_pay[...]


def merged(parts, pays, forward):
    me = lax.axis_index("seq")
    running = jnp.zeros((128, pays[0].shape[1]), F32)
    for distance in range(parts - 1, 0, -1):
        held = pays[distance - 1] if forward else pays[parts - distance - 1]
        there = (me >= distance) if forward else (me + distance < parts)
        decay = (
            held[128:129, :].astype(F32) + held[129:130, :].astype(F32)
        ) + held[130:131, :].astype(F32)
        running = jnp.where(there, held[0:128, :].astype(F32) + decay * running, 0.0)
    return running


def gradient_kernel(
    heads, parts, gains, taps, near, logs, grad, slope, inputs, halo, b_proj, c_proj, *rest
):
    pays = rest[: parts - 1]
    grad_out, tail_out, edge_out, running, window, sums = rest[parts - 1 :]
    channels = inputs.shape[1]
    step = pl.program_id(0)
    last = pl.num_programs(0) - 1

    @pl.when(step == 0)
    def first():
        running[...] = merged(parts, pays, False)
        window[STEP_ROWS : STEP_ROWS + 8, :] = jnp.zeros((8, channels), F32)
        sums[...] = jnp.zeros_like(sums)

    @pl.when(step > 0)
    def later():
        window[STEP_ROWS : STEP_ROWS + 8, :] = window[0:8, :]

    onehot = spread_matrix(heads, channels)
    gain = per_lane(gains, heads, channels)
    row = lax.broadcasted_iota(jnp.int32, (CHUNK, CHUNK), 0)
    col = lax.broadcasted_iota(jnp.int32, (CHUNK, CHUNK), 1)
    keep = row <= col
    per_step = STEP_ROWS // CHUNK
    adjoint = running[...]
    partial = [jnp.zeros((8, channels), F32) for _ in range(4)]
    for q in range(per_step - 1, -1, -1):
        at = q * CHUNK
        chunk = (last - step) * per_step + q
        both = slice(at, at + CHUNK)
        behind = spread(near[0:16, both], onehot)
        ahead = spread(near[16:32, both], onehot)
        whole = logs[0, pl.ds(chunk, 1), :]
        middle = logs[1, pl.ds(chunk, 1), :]
        rest_of = logs[2, pl.ds(chunk, 1), :]
        grad_f = grad[both, :].astype(F32)
        scaled = (grad_f * behind).astype(BF16)
        low = (adjoint * rest_of).astype(BF16)
        b_block = b_proj[both, :]
        c_block = c_proj[both, :]
        scores = dot(b_block, c_block, ((1,), (1,)))
        scores = jnp.where(keep, scores, 0.0).astype(BF16)
        inner = dot(
            jnp.concatenate([scores, b_block], axis=1),
            jnp.concatenate([scaled, low], axis=0),
            ((1,), (0,)),
        )
        grad_pre = (gain * grad_f + ahead * inner) * slope[both, :]
        window[both, :] = grad_pre
        adjoint = whole * adjoint + middle * dot(c_block, scaled, ((0,), (0,)))
        x = inputs[both, :].astype(F32)
        result = taps[3:4, :] * grad_pre
        partial[3] = partial[3] + (grad_pre * x).reshape(CHUNK // 8, 8, channels).sum(axis=0)
        for k in range(3):
            moved = window[at + 3 - k : at + 3 - k + CHUNK, :]
            result = result + taps[k : k + 1, :] * moved
            partial[k] = partial[k] + (moved * x).reshape(CHUNK // 8, 8, channels).sum(axis=0)
        grad_out[both, :] = result.astype(BF16)
        if q == per_step - 1:

            @pl.when(step == 0)
            def keep_edge():
                edge_out[...] = result[CHUNK - 8 :, :]

    running[...] = adjoint
    for k in range(4):
        sums[8 * k : 8 * k + 8, :] += partial[k]

    @pl.when(step == last)
    def finish():
        tail_out[...] = jnp.zeros_like(tail_out)
        for k in range(4):
            tap = jnp.sum(sums[8 * k : 8 * k + 8, :], axis=0, keepdims=True)
            for j in range(k, 3):
                tap = tap + window[j - k : j - k + 1, :] * halo[13 + j : 14 + j, :].astype(F32)
            tail_out[k : k + 1, :] = tap
        tail_out[4:7, :] = window[0:3, :]


def output_kernel(heads, parts, gains, near, logs, mixed, b_proj, c_proj, *rest):
    pays = rest[: parts - 1]
    out, running = rest[parts - 1 :]
    channels = mixed.shape[1]
    step = pl.program_id(0)

    @pl.when(step == 0)
    def first():
        running[...] = merged(parts, pays, True)

    onehot = spread_matrix(heads, channels)
    gain = per_lane(gains, heads, channels)
    row = lax.broadcasted_iota(jnp.int32, (CHUNK, CHUNK), 0)
    col = lax.broadcasted_iota(jnp.int32, (CHUNK, CHUNK), 1)
    keep = row >= col
    per_step = STEP_ROWS // CHUNK
    state = running[...]
    for q in range(per_step):
        at = q * CHUNK
        chunk = step * per_step + q
        both = slice(at, at + CHUNK)
        behind = spread(near[0:16, both], onehot)
        ahead = spread(near[16:32, both], onehot)
        whole = logs[0, pl.ds(chunk, 1), :]
        middle = logs[1, pl.ds(chunk, 1), :]
        rest_of = logs[2, pl.ds(chunk, 1), :]
        mixed_f = mixed[both, :].astype(F32)
        scaled = (mixed_f * ahead).astype(BF16)
        low = (state * middle).astype(BF16)
        b_block = b_proj[both, :]
        c_block = c_proj[both, :]
        scores = dot(c_block, b_block, ((1,), (1,)))
        scores = jnp.where(keep, scores, 0.0).astype(BF16)
        inner = dot(
            jnp.concatenate([scores, c_block], axis=1),
            jnp.concatenate([scaled, low], axis=0),
            ((1,), (0,)),
        )
        out[both, :] = (gain * mixed_f + behind * inner).astype(BF16)
        state = whole * state + rest_of * dot(b_block, scaled, ((0,), (0,)))
    running[...] = state


def finish_kernel(parts, scale, taps, tail, edge, *rest):
    others = rest[: parts - 1]
    unused, grad_out, conv_out = rest[parts - 1 :]
    total = tail[0:4, :]
    for other in others:
        total = total + other[0:4, :]
    conv_out[...] = total * scale
    me = lax.axis_index("seq")
    after = jnp.where(me + 1 < parts, others[parts - 2][...], 0.0)
    channels = tail.shape[1]
    row = lax.broadcasted_iota(jnp.int32, (8, channels), 0)
    result = edge[...]
    for r in range(3):
        extra = jnp.zeros((1, channels), F32)
        for k in range(r + 1):
            extra = extra + taps[k : k + 1, :] * after[4 + r - k : 5 + r - k, :]
        result = jnp.where(row == 5 + r, result + extra, result)
    grad_out[0:8, :] = unused[0:8, :]
    grad_out[8:16, :] = result.astype(BF16)


def rotated(block, axis, distance):
    size = lax.axis_size(axis)
    return lax.ppermute(block, axis, [(i, (i + distance) % size) for i in range(size)])


def shards(
    inputs,
    b_proj,
    c_proj,
    step_codes,
    gate_codes,
    decay_rates,
    skip_gain,
    conv_weight,
    out_cotangent,
):
    rows, channels = inputs.shape
    heads = decay_rates.shape[0]
    parts = lax.axis_size("seq")
    grid = rows // STEP_ROWS
    chunks = rows // CHUNK

    def call(kernel, grid_size, in_specs, out_specs, out_shape, scratch, flops, nbytes, aliases=None):
        return pl.pallas_call(
            kernel,
            grid=(grid_size,),
            in_specs=in_specs,
            out_specs=out_specs,
            out_shape=out_shape,
            scratch_shapes=scratch,
            input_output_aliases=aliases or {},
            compiler_params=pltpu.CompilerParams(
                dimension_semantics=("arbitrary",), vmem_limit_bytes=VMEM_LIMIT
            ),
            cost_estimate=pl.CostEstimate(
                flops=flops, bytes_accessed=nbytes, transcendentals=rows * channels
            ),
        )

    def full(*shape):
        return pl.BlockSpec(shape, lambda i: (0,) * len(shape))

    def tall(width, back=False):
        return pl.BlockSpec(
            (STEP_ROWS, width), (lambda i: (grid - 1 - i, 0)) if back else (lambda i: (i, 0))
        )

    def wide(height, back=False):
        return pl.BlockSpec(
            (height, STEP_ROWS), (lambda i: (0, grid - 1 - i)) if back else (lambda i: (0, i))
        )

    scalars = pl.BlockSpec(memory_space=pltpu.SMEM)
    shape = jax.ShapeDtypeStruct
    big = rows * channels

    halo_from = [(i, i + 1) for i in range(parts - 1)]
    halo = lax.ppermute(inputs[rows - 16 :], "seq", halo_from)

    near, far, logs, adjoint_pay = call(
        functools.partial(adjoint_kernel, heads),
        grid,
        [scalars, full(heads, rows), full(1, rows), tall(channels), tall(128)],
        [full(32, rows), full(16, rows), full(3, chunks, channels), full(144, channels)],
        [
            shape((32, rows), BF16),
            shape((16, rows), BF16),
            shape((3, chunks, channels), F32),
            shape((144, channels), BF16),
        ],
        [
            pltpu.VMEM((8, rows), F32),
            pltpu.VMEM((16, rows), BF16),
            pltpu.VMEM((128, channels), F32),
        ],
        2 * big * 128,
        big * 3,
    )(decay_rates, step_codes, gate_codes.reshape(1, rows), out_cotangent, c_proj)

    outs = call(
        functools.partial(state_kernel, heads, parts),
        grid,
        [full(4, channels), wide(16), tall(channels), full(16, channels), tall(128), full(144, channels)],
        [tall(channels), tall(channels)] + [full(144, channels)] * (parts - 1),
        [shape((rows, channels), BF16), shape((rows, channels), F32)]
        + [shape((144, channels), BF16)] * (parts - 1),
        [pltpu.VMEM((STEP_ROWS + 16, channels), F32), pltpu.VMEM((128, channels), F32)],
        2 * big * 128,
        big * 9,
    )(conv_weight, far, inputs, halo, b_proj, adjoint_pay)
    mixed, slope, sends = outs[0], outs[1], outs[2:]
    pays = [rotated(send, "seq", distance + 1) for distance, send in enumerate(sends)]

    grad_rows, tail, edge = call(
        functools.partial(gradient_kernel, heads, parts),
        grid,
        [
            scalars,
            full(4, channels),
            wide(32, True),
            full(3, chunks, channels),
            tall(channels, True),
            tall(channels, True),
            tall(channels, True),
            full(16, channels),
            tall(128, True),
            tall(128, True),
        ]
        + [full(144, channels)] * (parts - 1),
        [tall(channels, True), full(8, channels), full(8, channels)],
        [shape((rows, channels), BF16), shape((8, channels), F32), shape((8, channels), F32)],
        [
            pltpu.VMEM((128, channels), F32),
            pltpu.VMEM((STEP_ROWS + 8, channels), F32),
            pltpu.VMEM((32, channels), F32),
        ],
        6 * big * 128,
        big * 10,
    )(
        skip_gain, conv_weight, near, logs, out_cotangent, slope, inputs, halo, b_proj, c_proj,
        *pays,
    )
    tails = [rotated(tail, "seq", distance) for distance in range(1, parts)]

    layer_out = call(
        functools.partial(output_kernel, heads, parts),
        grid,
        [scalars, wide(32), full(3, chunks, channels), tall(channels), tall(128), tall(128)]
        + [full(144, channels)] * (parts - 1),
        tall(channels),
        shape((rows, channels), BF16),
        [pltpu.VMEM((128, channels), F32)],
        6 * big * 128,
        big * 4,
    )(skip_gain, near, logs, mixed, b_proj, c_proj, *pays)

    scale = float((rows * parts) ** -0.5)
    last_rows = pl.BlockSpec((16, channels), lambda i: (rows // 16 - 1, 0))
    input_grad, conv_grad = call(
        functools.partial(finish_kernel, parts, scale),
        1,
        [full(4, channels), full(8, channels), full(8, channels)]
        + [full(8, channels)] * (parts - 1)
        + [last_rows],
        [last_rows, full(4, channels)],
        [shape((rows, channels), BF16), shape((4, channels), F32)],
        [],
        1000,
        1000,
        {parts + 2: 0},
    )(conv_weight, tail, edge, *tails, grad_rows)
    return layer_out, input_grad, conv_grad


def solution(mesh):
    in_specs = (
        P(("groups", "seq"), ("head", "sub")),
        P(("groups", "seq"), None),
        P(("groups", "seq"), None),
        P(("head", "sub"), ("groups", "seq")),
        P(("groups", "seq")),
        P(("head", "sub")),
        P(("head", "sub")),
        P(None, ("head", "sub")),
        P(("groups", "seq"), ("head", "sub")),
    )
    out_specs = (
        P(("groups", "seq"), ("head", "sub")),
        P(("groups", "seq"), ("head", "sub")),
        P("groups", ("head", "sub")),
    )
    return jax.shard_map(shards, mesh=mesh, in_specs=in_specs, out_specs=out_specs, check_vma=False)
```

```python
import functools

import jax
import jax.numpy as jnp
from jax import lax
from jax.experimental import pallas as pl
from jax.experimental.pallas import tpu as pltpu
from jax.sharding import PartitionSpec as P

CHUNK = 128
STATE = 128
STEP_ROWS = 512
LOG_ONE = -0.2876820724517809
LOG_TWO = -0.6931471805599453
F32 = jnp.float32
BF16 = jnp.bfloat16
HIGHEST = lax.Precision.HIGHEST
VMEM_LIMIT = 20 * 1024 * 1024


def dot(a, b, dims, precision=None):
    return lax.dot_general(a, b, (dims, ((), ())), preferred_element_type=F32, precision=precision)


def per_lane(scalars, count, channels):
    width = channels // count
    lane = lax.broadcasted_iota(jnp.int32, (1, channels), 1)
    row = jnp.zeros((1, channels), F32)
    for head in range(count):
        inside = (lane >= head * width) & (lane < (head + 1) * width)
        row = jnp.where(inside, scalars[head], row)
    return row


def split_two(value):
    high = value.astype(BF16)
    low = (value - high.astype(F32)).astype(BF16)
    return jnp.concatenate([high.astype(F32), low.astype(F32)], axis=0).astype(BF16)


def spread_matrix(count, channels):
    width = channels // count
    row = lax.broadcasted_iota(jnp.int32, (16, channels), 0)
    lane = lax.broadcasted_iota(jnp.int32, (16, channels), 1)
    return jnp.where((row % 8) == lane // width, 1.0, 0.0).astype(BF16)


def spread(pair, onehot):
    return dot(pair, onehot, ((0,), (0,)))


def adjoint_kernel(
    heads, rates_hbm, codes_hbm, gates_hbm, grad_hbm, c_hbm,
    near_out, far_out, front_out, logs_out, scaled_out, low_out, pay_out,
    rates, codes, gates, grad, c_proj, steps, fresh, small_sem, grad_sem, c_sem,
):
    rows, channels = grad.shape
    chunks = rows // CHUNK
    pieces = rows // STEP_ROWS
    small = [
        pltpu.make_async_copy(source, target, small_sem.at[i])
        for i, (source, target) in enumerate(
            ((rates_hbm, rates), (codes_hbm, codes), (gates_hbm, gates))
        )
    ]
    large = []
    for copy in small:
        copy.start()
    for piece in range(pieces):
        at = pl.ds(piece * STEP_ROWS, STEP_ROWS)
        large.append(pltpu.make_async_copy(grad_hbm.at[at], grad.at[at], grad_sem.at[piece]))
        large.append(pltpu.make_async_copy(c_hbm.at[at], c_proj.at[at], c_sem.at[piece]))
    for copy in large:
        copy.start()
    for copy in small:
        copy.wait()

    steps[...] = jnp.zeros_like(steps)
    steps[0:heads, :] = jnp.exp2(-codes[...].astype(F32))
    gate = gates[...]
    steps[6:7, :] = jnp.where(gate == 1, 1.0, 0.0).astype(F32)
    steps[7:8, :] = jnp.where(gate == 2, 1.0, 0.0).astype(F32)
    stacked = jnp.concatenate(
        [steps[:, j * CHUNK : (j + 1) * CHUNK] for j in range(chunks)], axis=0
    ).astype(BF16)
    row = lax.broadcasted_iota(jnp.int32, (CHUNK, CHUNK), 0)
    col = lax.broadcasted_iota(jnp.int32, (CHUNK, CHUNK), 1)
    upper = jnp.where(row <= col, 1.0, 0.0).astype(BF16)
    sums = dot(stacked, upper, ((1,), (0,)))
    sub = lax.broadcasted_iota(jnp.int32, (8, CHUNK), 0)
    rate = jnp.zeros((8, CHUNK), F32)
    for head in range(heads):
        rate = jnp.where(sub == head, rates[head], rate)
    cums, mids, befores = [], [], []
    before = jnp.zeros((8, 1), F32)
    for j in range(chunks):
        part = sums[8 * j : 8 * j + 8, :]
        cum = LOG_ONE * part[6:7, :] + LOG_TWO * part[7:8, :] - rate * part
        cums.append(cum)
        mids.append(cum[:, CHUNK // 2 - 1 : CHUNK // 2])
        befores.append(before)
        before = before + cum[:, CHUNK - 1 : CHUNK]
    for j in range(chunks):
        at = slice(j * CHUNK, (j + 1) * CHUNK)
        size = steps[:, at]
        near_out[0:16, at] = split_two(jnp.exp(cums[j] - mids[j]))
        near_out[16:32, at] = split_two(jnp.exp(mids[j] - cums[j]) * size)
        front_out[:, at] = split_two(jnp.exp(befores[j] + cums[j]))
        far_out[:, at] = split_two(jnp.exp(before - befores[j] - cums[j]) * size)
    pick = lax.broadcasted_iota(jnp.int32, (8, CHUNK), 0)
    place = lax.broadcasted_iota(jnp.int32, (8, CHUNK), 1)
    chosen = jnp.where((pick == 0) | ((pick == 1) & (place < CHUNK // 2)), 1.0, 0.0)
    flat = dot(chosen.astype(BF16), stacked, ((1,), (1,)))
    owner = lax.broadcasted_iota(jnp.int32, (chunks, 8 * chunks), 1) // 8
    chunk_at = lax.broadcasted_iota(jnp.int32, (chunks, 8 * chunks), 0)
    lane_rate = per_lane(rates, heads, channels)
    kind = lax.broadcasted_iota(jnp.int32, (8 * chunks, channels), 0) % 8
    lane_head = lax.broadcasted_iota(jnp.int32, (8 * chunks, channels), 1) // (channels // heads)
    mixer = jnp.where(kind == lane_head, -lane_rate, 0.0)
    mixer = jnp.where(kind == 6, LOG_ONE, jnp.where(kind == 7, LOG_TWO, mixer))
    table = []
    for which in range(2):
        own = jnp.where(owner == chunk_at, flat[which : which + 1, :], 0.0)
        table.append(dot(own, mixer, ((1,), (0,)), HIGHEST))
    whole = jnp.exp(table[0])
    middle = jnp.exp(table[1])
    rest_of = jnp.exp(table[0] - table[1])
    logs_out[0] = whole
    logs_out[1] = middle
    logs_out[2] = rest_of
    decay = jnp.exp(jnp.sum(table[0], axis=0, keepdims=True))
    first = decay.astype(BF16).astype(F32)
    second = (decay - first).astype(BF16).astype(F32)
    third = decay - first - second
    row = lax.broadcasted_iota(jnp.int32, (16, channels), 0)
    tail = jnp.where(
        row == 0, first, jnp.where(row == 1, second, jnp.where(row == 2, third, 0.0))
    )
    pay_out[STATE : STATE + 16, :] = tail.astype(BF16)

    onehot = spread_matrix(heads, channels)
    for piece in range(pieces):
        large[2 * piece].wait()
        large[2 * piece + 1].wait()
        for j in range(piece * STEP_ROWS // CHUNK, (piece + 1) * STEP_ROWS // CHUNK):
            both = slice(j * CHUNK, (j + 1) * CHUNK)
            scale = spread(near_out[0:16, both], onehot)
            scaled = (grad[both, :].astype(F32) * scale).astype(BF16)
            scaled_out[both, :] = scaled
            fresh[both, :] = dot(c_proj[both, :], scaled, ((0,), (0,)))
    for lanes in lane_tiles(channels):
        adjoint = jnp.zeros((STATE, lanes.stop - lanes.start), F32)
        for j in range(chunks - 1, -1, -1):
            both = slice(j * CHUNK, (j + 1) * CHUNK)
            low_out[both, lanes] = (adjoint * rest_of[j : j + 1, lanes]).astype(BF16)
            adjoint = whole[j : j + 1, lanes] * adjoint + (
                middle[j : j + 1, lanes] * fresh[both, lanes]
            )
        pay_out[0:STATE, lanes] = adjoint.astype(BF16)


def lane_tiles(channels):
    return [slice(at, min(at + 128, channels)) for at in range(0, channels, 128)]


def state_kernel(
    heads, parts, taps, near, logs, inputs, halo, b_proj, adjoint_pay,
    window, mixed_out, sigma_out, scaled_out, low_out, *rest
):
    pays, fresh = rest[: parts - 1], rest[parts - 1]
    rows, channels = inputs.shape
    chunks = rows // CHUNK
    window[0:16, :] = halo[...].astype(F32)
    onehot = spread_matrix(heads, channels)
    for j in range(chunks):
        at = j * CHUNK
        both = slice(at, at + CHUNK)
        window[16 + at : 16 + at + CHUNK, :] = inputs[both, :].astype(F32)
        preact = taps[0:1, :] * window[13 + at : 13 + at + CHUNK, :]
        for k in range(1, 4):
            preact = preact + taps[k : k + 1, :] * window[13 + k + at : 13 + k + at + CHUNK, :]
        sigma = 0.5 * jnp.tanh(0.5 * preact) + 0.5
        mixed = preact * sigma
        sigma_out[both, :] = sigma
        mixed_out[both, :] = mixed
        scale = spread(near[16:32, both], onehot)
        scaled = (mixed * scale).astype(BF16)
        scaled_out[both, :] = scaled
        fresh[both, :] = dot(b_proj[both, :], scaled, ((0,), (0,)))
    me = lax.axis_index("seq")
    for lanes in lane_tiles(channels):
        state = jnp.zeros((STATE, lanes.stop - lanes.start), F32)
        for j in range(chunks):
            both = slice(j * CHUNK, (j + 1) * CHUNK)
            low_out[both, lanes] = (state * logs[1, j : j + 1, lanes]).astype(BF16)
            state = logs[0, j : j + 1, lanes] * state + (
                logs[2, j : j + 1, lanes] * fresh[both, lanes]
            )
        state = state.astype(BF16)
        for distance in range(1, parts):
            forward = me + distance < parts
            pays[distance - 1][0:STATE, lanes] = jnp.where(
                forward, state, adjoint_pay[0:STATE, lanes]
            )
    for pay in pays:
        pay[STATE : STATE + 16, :] = adjoint_pay[STATE : STATE + 16, :]


def merged(parts, pays, forward):
    me = lax.axis_index("seq")
    running = jnp.zeros((STATE, pays[0].shape[1]), F32)
    for distance in range(parts - 1, 0, -1):
        held = pays[distance - 1] if forward else pays[parts - distance - 1]
        there = (me >= distance) if forward else (me + distance < parts)
        decay = (
            held[STATE : STATE + 1, :].astype(F32) + held[STATE + 1 : STATE + 2, :].astype(F32)
        ) + held[STATE + 2 : STATE + 3, :].astype(F32)
        running = jnp.where(there, held[0:STATE, :].astype(F32) + decay * running, 0.0)
    return running.astype(BF16)


def inner_kernel(
    heads, gains, near, far, grad, mixed, sigma, b_proj, c_proj,
    mixed_scaled, mixed_low, grad_scaled, grad_low,
    base_out, grad_base, grad_weight, ahead_scores, behind_scores,
):
    rows, channels = grad.shape
    chunks = rows // CHUNK
    row = lax.broadcasted_iota(jnp.int32, (CHUNK, CHUNK), 0)
    col = lax.broadcasted_iota(jnp.int32, (CHUNK, CHUNK), 1)
    for j in range(chunks):
        both = slice(j * CHUNK, (j + 1) * CHUNK)
        b_block = b_proj[both, :]
        c_block = c_proj[both, :]
        ahead = dot(c_block, b_block, ((1,), (1,)))
        ahead_scores[both, :] = jnp.where(row >= col, ahead, 0.0).astype(BF16)
        behind = dot(b_block, c_block, ((1,), (1,)))
        behind_scores[both, :] = jnp.where(row <= col, behind, 0.0).astype(BF16)
    onehot = spread_matrix(heads, channels)
    gain = per_lane(gains, heads, channels)
    for j in range(chunks):
        both = slice(j * CHUNK, (j + 1) * CHUNK)
        inner = dot(
            jnp.concatenate([behind_scores[both, :], b_proj[both, :]], axis=1),
            jnp.concatenate([grad_scaled[both, :], grad_low[both, :]], axis=0),
            ((1,), (0,)),
        )
        slope = sigma[both, :] + mixed[both, :] * (1.0 - sigma[both, :])
        inner = gain * grad[both, :].astype(F32) + spread(near[16:32, both], onehot) * inner
        grad_base[both, :] = slope * inner
        grad_weight[both, :] = slope * spread(far[:, both], onehot)
    for j in range(chunks):
        both = slice(j * CHUNK, (j + 1) * CHUNK)
        inner = dot(
            jnp.concatenate([ahead_scores[both, :], c_proj[both, :]], axis=1),
            jnp.concatenate([mixed_scaled[both, :], mixed_low[both, :]], axis=0),
            ((1,), (0,)),
        )
        base_out[both, :] = gain * mixed[both, :] + spread(near[0:16, both], onehot) * inner


def gradient_kernel(parts, taps, base, weight, inputs, b_proj, *rest):
    pays = rest[: parts - 1]
    grad_hbm, tail_out, edge_out, window, result_rows, sems = rest[parts - 1 :]
    rows, channels = base.shape
    chunks = rows // CHUNK
    adjoint = merged(parts, pays, False)
    window[rows : rows + 8, :] = jnp.zeros((8, channels), F32)
    partial = [jnp.zeros((8, channels), F32) for _ in range(4)]
    copies = []
    for j in range(chunks - 1, -1, -1):
        at = j * CHUNK
        both = slice(at, at + CHUNK)
        grad_pre = base[both, :] + weight[both, :] * dot(b_proj[both, :], adjoint, ((1,), (0,)))
        window[both, :] = grad_pre
        x = inputs[16 + at : 16 + at + CHUNK, :]
        result = taps[3:4, :] * grad_pre
        partial[3] = partial[3] + (grad_pre * x).reshape(CHUNK // 8, 8, channels).sum(axis=0)
        for k in range(3):
            moved = window[at + 3 - k : at + 3 - k + CHUNK, :]
            result = result + taps[k : k + 1, :] * moved
            partial[k] = partial[k] + (moved * x).reshape(CHUNK // 8, 8, channels).sum(axis=0)
        result_rows[both, :] = result.astype(BF16)
        if j == chunks - 1:
            edge_out[...] = result[CHUNK - 16 :, :]
        if at % STEP_ROWS == 0:
            place = pl.ds(at, STEP_ROWS)
            copy = pltpu.make_async_copy(
                result_rows.at[place], grad_hbm.at[place], sems.at[at // STEP_ROWS]
            )
            copy.start()
            copies.append(copy)
    for k in range(4):
        tap = jnp.sum(partial[k], axis=0, keepdims=True)
        for j in range(k, 3):
            tap = tap + window[j - k : j - k + 1, :] * inputs[13 + j : 14 + j, :]
        tail_out[k : k + 1, :] = tap
    tail_out[4:7, :] = window[0:3, :]
    tail_out[7:8, :] = jnp.zeros((1, channels), F32)
    for copy in copies:
        copy.wait()


def output_kernel(heads, parts, front, base, c_proj, *rest):
    pays = rest[: parts - 1]
    out_hbm, result_rows, sems = rest[parts - 1 :]
    rows, channels = base.shape
    chunks = rows // CHUNK
    state = merged(parts, pays, True)
    onehot = spread_matrix(heads, channels)
    copies = []
    for j in range(chunks):
        both = slice(j * CHUNK, (j + 1) * CHUNK)
        carried = dot(c_proj[both, :], state, ((1,), (0,)))
        result = base[both, :] + spread(front[:, both], onehot) * carried
        result_rows[both, :] = result.astype(BF16)
        if (j + 1) * CHUNK % STEP_ROWS == 0:
            at = (j + 1) * CHUNK - STEP_ROWS
            place = pl.ds(at, STEP_ROWS)
            copy = pltpu.make_async_copy(
                result_rows.at[place], out_hbm.at[place], sems.at[at // STEP_ROWS]
            )
            copy.start()
            copies.append(copy)
    for copy in copies:
        copy.wait()


def finish_kernel(parts, scale, taps, tail, edge, *rest):
    others = rest[: parts - 1]
    unused, grad_hbm, conv_out, rows_low, sem = rest[parts - 1 :]
    channels = tail.shape[1]
    me = lax.axis_index("seq")
    after = jnp.where(me + 1 < parts, others[parts - 2][...], 0.0)
    row = lax.broadcasted_iota(jnp.int32, (16, channels), 0)
    result = edge[...]
    for r in range(3):
        extra = jnp.zeros((1, channels), F32)
        for k in range(r + 1):
            extra = extra + taps[k : k + 1, :] * after[4 + r - k : 5 + r - k, :]
        result = jnp.where(row == 13 + r, result + extra, result)
    rows_low[...] = result.astype(BF16)
    rows = grad_hbm.shape[0]
    copy = pltpu.make_async_copy(rows_low, grad_hbm.at[pl.ds(rows - 16, 16)], sem)
    copy.start()
    total = tail[0:4, :]
    for other in others:
        total = total + other[0:4, :]
    conv_out[...] = total * scale
    copy.wait()


def rotated(block, axis, distance):
    size = lax.axis_size(axis)
    return lax.ppermute(block, axis, [(i, (i + distance) % size) for i in range(size)])


def shards(
    inputs,
    b_proj,
    c_proj,
    step_codes,
    gate_codes,
    decay_rates,
    skip_gain,
    conv_weight,
    out_cotangent,
):
    rows, channels = inputs.shape
    heads = decay_rates.shape[0]
    parts = lax.axis_size("seq")
    chunks = rows // CHUNK
    pieces = rows // STEP_ROWS
    hbm = pl.BlockSpec(memory_space=pltpu.HBM)
    vmem = pl.BlockSpec(memory_space=pltpu.VMEM)
    smem = pl.BlockSpec(memory_space=pltpu.SMEM)
    shape = jax.ShapeDtypeStruct
    dma = pltpu.SemaphoreType.DMA
    big = rows * channels

    def call(kernel, in_specs, out_specs, out_shape, scratch, products, aliases=None):
        return pl.pallas_call(
            kernel,
            in_specs=in_specs,
            out_specs=out_specs,
            out_shape=out_shape,
            scratch_shapes=scratch,
            input_output_aliases=aliases or {},
            compiler_params=pltpu.CompilerParams(vmem_limit_bytes=VMEM_LIMIT),
            cost_estimate=pl.CostEstimate(
                flops=products * 2 * big * 128, bytes_accessed=6 * big, transcendentals=big
            ),
        )

    def stay(array):
        return pltpu.with_memory_space_constraint(array, pltpu.HBM)

    halo_from = [(i, i + 1) for i in range(parts - 1)]
    halo = lax.ppermute(inputs[rows - 16 :], "seq", halo_from)
    pay = shape((STATE + 16, channels), BF16)
    narrow = shape((rows, channels), BF16)
    broad = shape((rows, channels), F32)

    near, far, front, logs, grad_scaled, grad_low, adjoint_pay = call(
        functools.partial(adjoint_kernel, heads),
        [hbm] * 5,
        [vmem] * 7,
        [
            shape((32, rows), BF16),
            shape((16, rows), BF16),
            shape((16, rows), BF16),
            shape((3, chunks, channels), F32),
            narrow,
            narrow,
            pay,
        ],
        [
            pltpu.SMEM((heads,), F32),
            pltpu.VMEM((heads, rows), jnp.int32),
            pltpu.VMEM((1, rows), jnp.int32),
            pltpu.VMEM((rows, channels), BF16),
            pltpu.VMEM((rows, 128), BF16),
            pltpu.VMEM((8, rows), F32),
            pltpu.VMEM((rows, channels), F32),
            dma((3,)),
            dma((pieces,)),
            dma((pieces,)),
        ],
        2,
    )(
        stay(decay_rates),
        stay(step_codes),
        stay(gate_codes.reshape(1, rows)),
        stay(out_cotangent),
        stay(c_proj),
    )

    outs = call(
        functools.partial(state_kernel, heads, parts),
        [vmem] * 7,
        [vmem] * (4 + parts),
        [shape((rows + 16, channels), F32), broad, broad, narrow, narrow] + [pay] * (parts - 1),
        [pltpu.VMEM((rows, channels), F32)],
        2,
    )(conv_weight, near, logs, inputs, halo, b_proj, adjoint_pay)
    wide_inputs, mixed, sigma, mixed_scaled, mixed_low = outs[:5]
    pays = [rotated(send, "seq", distance + 1) for distance, send in enumerate(outs[5:])]

    base, grad_base, grad_weight = call(
        functools.partial(inner_kernel, heads),
        [smem] + [vmem] * 11,
        [vmem] * 3,
        [broad] * 3,
        [pltpu.VMEM((rows, CHUNK), BF16), pltpu.VMEM((rows, CHUNK), BF16)],
        6,
    )(
        skip_gain, near, far, out_cotangent, mixed, sigma, b_proj, c_proj,
        mixed_scaled, mixed_low, grad_scaled, grad_low,
    )

    grad_rows, tail, edge = call(
        functools.partial(gradient_kernel, parts),
        [vmem] * (4 + parts),
        [hbm, vmem, vmem],
        [narrow, shape((8, channels), F32), shape((16, channels), F32)],
        [pltpu.VMEM((rows + 8, channels), F32), pltpu.VMEM((rows, channels), BF16), dma((pieces,))],
        2,
    )(conv_weight, grad_base, grad_weight, wide_inputs, b_proj, *pays)
    tails = [rotated(tail, "seq", distance) for distance in range(1, parts)]

    layer_out = call(
        functools.partial(output_kernel, heads, parts),
        [vmem] * (2 + parts),
        hbm,
        narrow,
        [pltpu.VMEM((rows, channels), BF16), dma((pieces,))],
        2,
    )(front, base, c_proj, *pays)

    scale = float((rows * parts) ** -0.5)
    input_grad, conv_grad = call(
        functools.partial(finish_kernel, parts, scale),
        [vmem] * (2 + parts) + [hbm],
        [hbm, vmem],
        [narrow, shape((4, channels), F32)],
        [pltpu.VMEM((16, channels), BF16), dma],
        0,
        {parts + 2: 0},
    )(conv_weight, tail, edge, *tails, grad_rows)
    return layer_out, input_grad, conv_grad


def solution(mesh):
    in_specs = (
        P(("groups", "seq"), ("head", "sub")),
        P(("groups", "seq"), None),
        P(("groups", "seq"), None),
        P(("head", "sub"), ("groups", "seq")),
        P(("groups", "seq")),
        P(("head", "sub")),
        P(("head", "sub")),
        P(None, ("head", "sub")),
        P(("groups", "seq"), ("head", "sub")),
    )
    out_specs = (
        P(("groups", "seq"), ("head", "sub")),
        P(("groups", "seq"), ("head", "sub")),
        P("groups", ("head", "sub")),
    )
    return jax.shard_map(shards, mesh=mesh, in_specs=in_specs, out_specs=out_specs, check_vma=False)
```

```python
import functools

import jax
import jax.numpy as jnp
from jax import lax
from jax.experimental import pallas as pl
from jax.experimental.pallas import tpu as pltpu
from jax.sharding import PartitionSpec as P

CHUNK = 128
STATE = 128
STEP_ROWS = 512
LOG_ONE = -0.2876820724517809
LOG_TWO = -0.6931471805599453
F32 = jnp.float32
BF16 = jnp.bfloat16
HIGHEST = lax.Precision.HIGHEST
VMEM_LIMIT = 20 * 1024 * 1024


def dot(a, b, dims, precision=None):
    return lax.dot_general(a, b, (dims, ((), ())), preferred_element_type=F32, precision=precision)


def per_lane(scalars, count, channels):
    width = channels // count
    lane = lax.broadcasted_iota(jnp.int32, (1, channels), 1)
    row = jnp.zeros((1, channels), F32)
    for head in range(count):
        inside = (lane >= head * width) & (lane < (head + 1) * width)
        row = jnp.where(inside, scalars[head], row)
    return row


def split_two(value):
    high = value.astype(BF16)
    low = (value - high.astype(F32)).astype(BF16)
    return jnp.concatenate([high.astype(F32), low.astype(F32)], axis=0).astype(BF16)


def spread_matrix(count, channels):
    width = channels // count
    row = lax.broadcasted_iota(jnp.int32, (16, channels), 0)
    lane = lax.broadcasted_iota(jnp.int32, (16, channels), 1)
    return jnp.where((row % 8) == lane // width, 1.0, 0.0).astype(BF16)


def spread(pair, onehot):
    return dot(pair, onehot, ((0,), (0,)))


def adjoint_kernel(
    heads, rates_hbm, codes_hbm, gates_hbm, grad_hbm, c_hbm,
    near_out, far_out, front_out, logs_out, pay_out,
    rates, codes, gates, grad, c_proj, steps, small_sem, grad_sem, c_sem,
):
    rows, channels = grad.shape
    chunks = rows // CHUNK
    pieces = rows // STEP_ROWS
    small = [
        pltpu.make_async_copy(source, target, small_sem.at[i])
        for i, (source, target) in enumerate(
            ((rates_hbm, rates), (codes_hbm, codes), (gates_hbm, gates))
        )
    ]
    large = []
    for copy in small:
        copy.start()
    for piece in range(pieces):
        at = pl.ds(piece * STEP_ROWS, STEP_ROWS)
        large.append(pltpu.make_async_copy(grad_hbm.at[at], grad.at[at], grad_sem.at[piece]))
        large.append(pltpu.make_async_copy(c_hbm.at[at], c_proj.at[at], c_sem.at[piece]))
    for copy in large:
        copy.start()
    for copy in small:
        copy.wait()

    steps[...] = jnp.zeros_like(steps)
    steps[0:heads, :] = jnp.exp2(-codes[...].astype(F32))
    gate = gates[...]
    steps[6:7, :] = jnp.where(gate == 1, 1.0, 0.0).astype(F32)
    steps[7:8, :] = jnp.where(gate == 2, 1.0, 0.0).astype(F32)
    stacked = jnp.concatenate(
        [steps[:, j * CHUNK : (j + 1) * CHUNK] for j in range(chunks)], axis=0
    ).astype(BF16)
    row = lax.broadcasted_iota(jnp.int32, (CHUNK, CHUNK), 0)
    col = lax.broadcasted_iota(jnp.int32, (CHUNK, CHUNK), 1)
    upper = jnp.where(row <= col, 1.0, 0.0).astype(BF16)
    sums = dot(stacked, upper, ((1,), (0,)))
    sub = lax.broadcasted_iota(jnp.int32, (8, CHUNK), 0)
    rate = jnp.zeros((8, CHUNK), F32)
    for head in range(heads):
        rate = jnp.where(sub == head, rates[head], rate)
    cums, mids, befores = [], [], []
    before = jnp.zeros((8, 1), F32)
    for j in range(chunks):
        part = sums[8 * j : 8 * j + 8, :]
        cum = LOG_ONE * part[6:7, :] + LOG_TWO * part[7:8, :] - rate * part
        cums.append(cum)
        mids.append(cum[:, CHUNK // 2 - 1 : CHUNK // 2])
        befores.append(before)
        before = before + cum[:, CHUNK - 1 : CHUNK]
    for j in range(chunks):
        at = slice(j * CHUNK, (j + 1) * CHUNK)
        size = steps[:, at]
        near_out[0:16, at] = split_two(jnp.exp(cums[j] - mids[j]))
        near_out[16:32, at] = split_two(jnp.exp(mids[j] - cums[j]) * size)
        front_out[:, at] = split_two(jnp.exp(befores[j] + cums[j]))
        far_out[:, at] = split_two(jnp.exp(before - befores[j] - cums[j]) * size)
    pick = lax.broadcasted_iota(jnp.int32, (8, CHUNK), 0)
    place = lax.broadcasted_iota(jnp.int32, (8, CHUNK), 1)
    chosen = jnp.where((pick == 0) | ((pick == 1) & (place < CHUNK // 2)), 1.0, 0.0)
    flat = dot(chosen.astype(BF16), stacked, ((1,), (1,)))
    owner = lax.broadcasted_iota(jnp.int32, (chunks, 8 * chunks), 1) // 8
    chunk_at = lax.broadcasted_iota(jnp.int32, (chunks, 8 * chunks), 0)
    lane_rate = per_lane(rates, heads, channels)
    kind = lax.broadcasted_iota(jnp.int32, (8 * chunks, channels), 0) % 8
    lane_head = lax.broadcasted_iota(jnp.int32, (8 * chunks, channels), 1) // (channels // heads)
    mixer = jnp.where(kind == lane_head, -lane_rate, 0.0)
    mixer = jnp.where(kind == 6, LOG_ONE, jnp.where(kind == 7, LOG_TWO, mixer))
    table = []
    for which in range(2):
        own = jnp.where(owner == chunk_at, flat[which : which + 1, :], 0.0)
        table.append(dot(own, mixer, ((1,), (0,)), HIGHEST))
    whole = jnp.exp(table[0])
    middle = jnp.exp(table[1])
    rest_of = jnp.exp(table[0] - table[1])
    logs_out[0] = whole
    logs_out[1] = middle
    logs_out[2] = rest_of
    decay = jnp.exp(jnp.sum(table[0], axis=0, keepdims=True))
    first = decay.astype(BF16).astype(F32)
    second = (decay - first).astype(BF16).astype(F32)
    third = decay - first - second
    row = lax.broadcasted_iota(jnp.int32, (16, channels), 0)
    tail = jnp.where(
        row == 0, first, jnp.where(row == 1, second, jnp.where(row == 2, third, 0.0))
    )
    pay_out[STATE : STATE + 16, :] = tail.astype(BF16)

    onehot = spread_matrix(heads, channels)
    total = jnp.zeros((STATE, channels), F32)
    for piece in range(pieces):
        both = slice(piece * STEP_ROWS, (piece + 1) * STEP_ROWS)
        scale = spread(front_out[:, both], onehot)
        large[2 * piece].wait()
        large[2 * piece + 1].wait()
        scaled = (grad[both, :].astype(F32) * scale).astype(BF16)
        total = total + dot(c_proj[both, :], scaled, ((0,), (0,)))
    pay_out[0:STATE, :] = total.astype(BF16)


def lane_tiles(channels):
    return [slice(at, min(at + 128, channels)) for at in range(0, channels, 128)]


def state_kernel(
    heads, parts, taps, far, inputs, halo, b_proj, adjoint_pay, mixed_out, sigma_out, *pays
):
    rows, channels = inputs.shape
    pieces = rows // STEP_ROWS
    me = lax.axis_index("seq")
    before = jnp.where(me > 0, halo[...].astype(F32), 0.0).astype(BF16)
    onehot = spread_matrix(heads, channels)
    row = lax.broadcasted_iota(jnp.int32, (3 * CHUNK, CHUNK + 16), 0)
    col = lax.broadcasted_iota(jnp.int32, (3 * CHUNK, CHUNK + 16), 1)
    shift = jnp.where(col == row % CHUNK + 13 + row // CHUNK, 1.0, 0.0).astype(BF16)
    total = jnp.zeros((STATE, channels), F32)
    for piece in range(pieces):
        scaled = []
        for at in range(piece * STEP_ROWS, (piece + 1) * STEP_ROWS, CHUNK):
            both = slice(at, at + CHUNK)
            if at == 0:
                block = jnp.concatenate([before, inputs[both, :]], axis=0)
            else:
                block = inputs[at - 16 : at + CHUNK, :]
            moved = dot(shift, block, ((1,), (0,)))
            preact = taps[3:4, :] * inputs[both, :].astype(F32)
            for k in range(3):
                preact = preact + taps[k : k + 1, :] * moved[k * CHUNK : (k + 1) * CHUNK, :]
            sigma = 0.5 * jnp.tanh(0.5 * preact) + 0.5
            mixed = preact * sigma
            sigma_out[both, :] = sigma
            mixed_out[both, :] = mixed
            scaled.append((mixed * spread(far[:, both], onehot)).astype(BF16))
        both = slice(piece * STEP_ROWS, (piece + 1) * STEP_ROWS)
        total = total + dot(b_proj[both, :], jnp.concatenate(scaled, axis=0), ((0,), (0,)))
    state = total.astype(BF16)
    for distance in range(1, parts):
        pay = pays[distance - 1]
        pay[0:STATE, :] = jnp.where(me + distance < parts, state, adjoint_pay[0:STATE, :])
        pay[STATE : STATE + 16, :] = adjoint_pay[STATE : STATE + 16, :]


def merged(parts, pays, forward):
    me = lax.axis_index("seq")
    running = jnp.zeros((STATE, pays[0].shape[1]), F32)
    for distance in range(parts - 1, 0, -1):
        held = pays[distance - 1] if forward else pays[parts - distance - 1]
        there = (me >= distance) if forward else (me + distance < parts)
        decay = (
            held[STATE : STATE + 1, :].astype(F32) + held[STATE + 1 : STATE + 2, :].astype(F32)
        ) + held[STATE + 2 : STATE + 3, :].astype(F32)
        running = jnp.where(there, held[0:STATE, :].astype(F32) + decay * running, 0.0)
    return running.astype(BF16)


def inner_kernel(
    heads, gains, near, far, logs, grad, mixed, sigma, b_proj, c_proj,
    base_out, grad_base, grad_weight,
    ahead_scores, behind_scores, mixed_scaled, mixed_low, grad_scaled, grad_low,
    mixed_fresh, grad_fresh,
):
    rows, channels = grad.shape
    chunks = rows // CHUNK
    blocks = [slice(j * CHUNK, (j + 1) * CHUNK) for j in range(chunks)]
    row = lax.broadcasted_iota(jnp.int32, (CHUNK, CHUNK), 0)
    col = lax.broadcasted_iota(jnp.int32, (CHUNK, CHUNK), 1)
    onehot = spread_matrix(heads, channels)
    gain = per_lane(gains, heads, channels)
    for both in blocks:
        scale = spread(near[0:16, both], onehot)
        grad_scaled[both, :] = (grad[both, :].astype(F32) * scale).astype(BF16)
    for both in blocks:
        scale = spread(near[16:32, both], onehot)
        mixed_scaled[both, :] = (mixed[both, :] * scale).astype(BF16)
    for both in blocks:
        grad_fresh[both, :] = dot(c_proj[both, :], grad_scaled[both, :], ((0,), (0,)))
    for both in blocks:
        mixed_fresh[both, :] = dot(b_proj[both, :], mixed_scaled[both, :], ((0,), (0,)))
    for both in blocks:
        ahead = dot(c_proj[both, :], b_proj[both, :], ((1,), (1,)))
        ahead_scores[both, :] = jnp.where(row >= col, ahead, 0.0).astype(BF16)
    for both in blocks:
        behind = dot(b_proj[both, :], c_proj[both, :], ((1,), (1,)))
        behind_scores[both, :] = jnp.where(row <= col, behind, 0.0).astype(BF16)
    for lanes in lane_tiles(channels):
        adjoint = jnp.zeros((STATE, lanes.stop - lanes.start), F32)
        for j in range(chunks - 1, -1, -1):
            grad_low[blocks[j], lanes] = (adjoint * logs[2, j : j + 1, lanes]).astype(BF16)
            adjoint = logs[0, j : j + 1, lanes] * adjoint + (
                logs[1, j : j + 1, lanes] * grad_fresh[blocks[j], lanes]
            )
        state = jnp.zeros((STATE, lanes.stop - lanes.start), F32)
        for j in range(chunks):
            mixed_low[blocks[j], lanes] = (state * logs[1, j : j + 1, lanes]).astype(BF16)
            state = logs[0, j : j + 1, lanes] * state + (
                logs[2, j : j + 1, lanes] * mixed_fresh[blocks[j], lanes]
            )
    for both in blocks:
        inner = dot(
            jnp.concatenate([behind_scores[both, :], b_proj[both, :]], axis=1),
            jnp.concatenate([grad_scaled[both, :], grad_low[both, :]], axis=0),
            ((1,), (0,)),
        )
        slope = sigma[both, :] + mixed[both, :] * (1.0 - sigma[both, :])
        inner = gain * grad[both, :].astype(F32) + spread(near[16:32, both], onehot) * inner
        grad_base[both, :] = slope * inner
        grad_weight[both, :] = slope * spread(far[:, both], onehot)
    for both in blocks:
        inner = dot(
            jnp.concatenate([ahead_scores[both, :], c_proj[both, :]], axis=1),
            jnp.concatenate([mixed_scaled[both, :], mixed_low[both, :]], axis=0),
            ((1,), (0,)),
        )
        base_out[both, :] = gain * mixed[both, :] + spread(near[0:16, both], onehot) * inner


def gradient_kernel(parts, taps, base, weight, inputs, halo, b_proj, *rest):
    pays = rest[: parts - 1]
    grad_out, tail_out, edge_out, window = rest[parts - 1 :]
    rows, channels = base.shape
    chunks = rows // CHUNK
    adjoint = merged(parts, pays, False)
    me = lax.axis_index("seq")
    window[rows : rows + 16, :] = jnp.zeros((16, channels), BF16)
    row = lax.broadcasted_iota(jnp.int32, (3 * CHUNK, CHUNK + 16), 0)
    col = lax.broadcasted_iota(jnp.int32, (3 * CHUNK, CHUNK + 16), 1)
    shift = jnp.where(col == row % CHUNK + 3 - row // CHUNK, 1.0, 0.0).astype(BF16)
    partial = [jnp.zeros((8, channels), F32) for _ in range(4)]
    for j in range(chunks - 1, -1, -1):
        at = j * CHUNK
        both = slice(at, at + CHUNK)
        grad_pre = base[both, :] + weight[both, :] * dot(b_proj[both, :], adjoint, ((1,), (0,)))
        window[both, :] = grad_pre.astype(BF16)
        moved = dot(shift, window[at : at + CHUNK + 16, :], ((1,), (0,)))
        x = inputs[both, :].astype(F32)
        result = taps[3:4, :] * grad_pre
        partial[3] = partial[3] + (grad_pre * x).reshape(CHUNK // 8, 8, channels).sum(axis=0)
        for k in range(3):
            part = moved[k * CHUNK : (k + 1) * CHUNK, :]
            result = result + taps[k : k + 1, :] * part
            partial[k] = partial[k] + (part * x).reshape(CHUNK // 8, 8, channels).sum(axis=0)
        grad_out[both, :] = result.astype(BF16)
        if j == chunks - 1:
            edge_out[...] = result[CHUNK - 16 :, :]
        if j == 0:
            first = grad_pre[0:8, :]
    before = jnp.where(me > 0, halo[...].astype(F32), 0.0)
    for k in range(4):
        tap = jnp.sum(partial[k], axis=0, keepdims=True)
        for j in range(k, 3):
            tap = tap + first[j - k : j - k + 1, :] * before[13 + j : 14 + j, :]
        tail_out[k : k + 1, :] = tap
    tail_out[4:7, :] = first[0:3, :]
    tail_out[7:8, :] = jnp.zeros((1, channels), F32)


def output_kernel(heads, parts, front, base, c_proj, grad_rows, *rest):
    pays = rest[: parts - 1]
    out_hbm, grad_hbm, result_rows, sems, grad_sem = rest[parts - 1 :]
    rows, channels = base.shape
    grad_copy = pltpu.make_async_copy(grad_rows, grad_hbm, grad_sem)
    grad_copy.start()
    state = merged(parts, pays, True)
    onehot = spread_matrix(heads, channels)
    copies = []
    for piece in range(rows // STEP_ROWS):
        for at in range(piece * STEP_ROWS, (piece + 1) * STEP_ROWS, CHUNK):
            both = slice(at, at + CHUNK)
            carried = dot(c_proj[both, :], state, ((1,), (0,)))
            result = base[both, :] + spread(front[:, both], onehot) * carried
            result_rows[both, :] = result.astype(BF16)
        place = pl.ds(piece * STEP_ROWS, STEP_ROWS)
        copy = pltpu.make_async_copy(result_rows.at[place], out_hbm.at[place], sems.at[piece])
        copy.start()
        copies.append(copy)
    for copy in copies:
        copy.wait()
    grad_copy.wait()


def finish_kernel(parts, scale, taps, tail, edge, *rest):
    others = rest[: parts - 1]
    unused, grad_hbm, conv_out, rows_low, sem = rest[parts - 1 :]
    channels = tail.shape[1]
    me = lax.axis_index("seq")
    after = jnp.where(me + 1 < parts, others[parts - 2][...], 0.0)
    row = lax.broadcasted_iota(jnp.int32, (16, channels), 0)
    result = edge[...]
    for r in range(3):
        extra = jnp.zeros((1, channels), F32)
        for k in range(r + 1):
            extra = extra + taps[k : k + 1, :] * after[4 + r - k : 5 + r - k, :]
        result = jnp.where(row == 13 + r, result + extra, result)
    rows_low[...] = result.astype(BF16)
    rows = grad_hbm.shape[0]
    copy = pltpu.make_async_copy(rows_low, grad_hbm.at[pl.ds(rows - 16, 16)], sem)
    copy.start()
    total = tail[0:4, :]
    for other in others:
        total = total + other[0:4, :]
    conv_out[...] = total * scale
    copy.wait()


def rotated(block, axis, distance):
    size = lax.axis_size(axis)
    return lax.ppermute(block, axis, [(i, (i + distance) % size) for i in range(size)])


def shards(
    inputs,
    b_proj,
    c_proj,
    step_codes,
    gate_codes,
    decay_rates,
    skip_gain,
    conv_weight,
    out_cotangent,
):
    rows, channels = inputs.shape
    heads = decay_rates.shape[0]
    parts = lax.axis_size("seq")
    chunks = rows // CHUNK
    pieces = rows // STEP_ROWS
    hbm = pl.BlockSpec(memory_space=pltpu.HBM)
    vmem = pl.BlockSpec(memory_space=pltpu.VMEM)
    smem = pl.BlockSpec(memory_space=pltpu.SMEM)
    shape = jax.ShapeDtypeStruct
    dma = pltpu.SemaphoreType.DMA
    big = rows * channels

    def call(kernel, in_specs, out_specs, out_shape, scratch, products, aliases=None):
        return pl.pallas_call(
            kernel,
            in_specs=in_specs,
            out_specs=out_specs,
            out_shape=out_shape,
            scratch_shapes=scratch,
            input_output_aliases=aliases or {},
            compiler_params=pltpu.CompilerParams(vmem_limit_bytes=VMEM_LIMIT),
            cost_estimate=pl.CostEstimate(
                flops=products * 2 * big * 128, bytes_accessed=6 * big, transcendentals=big
            ),
        )

    def stay(array):
        return pltpu.with_memory_space_constraint(array, pltpu.HBM)

    halo = rotated(inputs[rows - 16 :], "seq", 1)
    pay = shape((STATE + 16, channels), BF16)
    narrow = shape((rows, channels), BF16)
    broad = shape((rows, channels), F32)

    near, far, front, logs, adjoint_pay = call(
        functools.partial(adjoint_kernel, heads),
        [hbm] * 5,
        [vmem] * 5,
        [
            shape((32, rows), BF16),
            shape((16, rows), BF16),
            shape((16, rows), BF16),
            shape((3, chunks, channels), F32),
            pay,
        ],
        [
            pltpu.SMEM((heads,), F32),
            pltpu.VMEM((heads, rows), jnp.int32),
            pltpu.VMEM((1, rows), jnp.int32),
            pltpu.VMEM((rows, channels), BF16),
            pltpu.VMEM((rows, 128), BF16),
            pltpu.VMEM((8, rows), F32),
            dma((3,)),
            dma((pieces,)),
            dma((pieces,)),
        ],
        2,
    )(
        stay(decay_rates),
        stay(step_codes),
        stay(gate_codes.reshape(1, rows)),
        stay(out_cotangent),
        stay(c_proj),
    )

    outs = call(
        functools.partial(state_kernel, heads, parts),
        [vmem] * 6,
        [vmem] * (1 + parts),
        [broad, broad] + [pay] * (parts - 1),
        [],
        2,
    )(conv_weight, far, inputs, halo, b_proj, adjoint_pay)
    mixed, sigma = outs[:2]
    pays = [rotated(send, "seq", distance + 1) for distance, send in enumerate(outs[2:])]

    tile = pltpu.VMEM((rows, CHUNK), BF16)
    low = pltpu.VMEM((rows, channels), BF16)
    high = pltpu.VMEM((rows, channels), F32)
    base, grad_base, grad_weight = call(
        functools.partial(inner_kernel, heads),
        [smem] + [vmem] * 8,
        [vmem] * 3,
        [broad] * 3,
        [tile, tile, low, low, low, low, high, high],
        10,
    )(skip_gain, near, far, logs, out_cotangent, mixed, sigma, b_proj, c_proj)

    grad_rows, tail, edge = call(
        functools.partial(gradient_kernel, parts),
        [vmem] * (5 + parts),
        [vmem] * 3,
        [narrow, shape((8, channels), F32), shape((16, channels), F32)],
        [pltpu.VMEM((rows + 16, channels), BF16)],
        2,
    )(conv_weight, grad_base, grad_weight, inputs, halo, b_proj, *pays)
    tails = [rotated(tail, "seq", distance) for distance in range(1, parts)]

    layer_out, grad_rows = call(
        functools.partial(output_kernel, heads, parts),
        [vmem] * (3 + parts),
        [hbm, hbm],
        [narrow, narrow],
        [pltpu.VMEM((rows, channels), BF16), dma((pieces,)), dma],
        2,
    )(front, base, c_proj, grad_rows, *pays)

    scale = float((rows * parts) ** -0.5)
    input_grad, conv_grad = call(
        functools.partial(finish_kernel, parts, scale),
        [vmem] * (2 + parts) + [hbm],
        [hbm, vmem],
        [narrow, shape((4, channels), F32)],
        [pltpu.VMEM((16, channels), BF16), dma],
        0,
        {parts + 2: 0},
    )(conv_weight, tail, edge, *tails, grad_rows)
    return layer_out, input_grad, conv_grad


def solution(mesh):
    in_specs = (
        P(("groups", "seq"), ("head", "sub")),
        P(("groups", "seq"), None),
        P(("groups", "seq"), None),
        P(("head", "sub"), ("groups", "seq")),
        P(("groups", "seq")),
        P(("head", "sub")),
        P(("head", "sub")),
        P(None, ("head", "sub")),
        P(("groups", "seq"), ("head", "sub")),
    )
    out_specs = (
        P(("groups", "seq"), ("head", "sub")),
        P(("groups", "seq"), ("head", "sub")),
        P("groups", ("head", "sub")),
    )
    return jax.shard_map(shards, mesh=mesh, in_specs=in_specs, out_specs=out_specs, check_vma=False)
```

```python
import functools

import jax
import jax.numpy as jnp
from jax import lax
from jax.experimental import pallas as pl
from jax.experimental.pallas import tpu as pltpu
from jax.sharding import PartitionSpec as P

CHUNK = 128
STATE = 128
STEP_ROWS = 512
LOG_ONE = -0.2876820724517809
LOG_TWO = -0.6931471805599453
F32 = jnp.float32
BF16 = jnp.bfloat16
HIGHEST = lax.Precision.HIGHEST
VMEM_LIMIT = 20 * 1024 * 1024


def dot(a, b, dims, precision=None):
    return lax.dot_general(a, b, (dims, ((), ())), preferred_element_type=F32, precision=precision)


def per_lane(scalars, count, channels):
    width = channels // count
    lane = lax.broadcasted_iota(jnp.int32, (1, channels), 1)
    row = jnp.zeros((1, channels), F32)
    for head in range(count):
        inside = (lane >= head * width) & (lane < (head + 1) * width)
        row = jnp.where(inside, scalars[head], row)
    return row


def split_two(value):
    high = value.astype(BF16)
    low = (value - high.astype(F32)).astype(BF16)
    return jnp.concatenate([high.astype(F32), low.astype(F32)], axis=0).astype(BF16)


def spread_matrix(count, channels):
    width = channels // count
    row = lax.broadcasted_iota(jnp.int32, (16, channels), 0)
    lane = lax.broadcasted_iota(jnp.int32, (16, channels), 1)
    return jnp.where((row % 8) == lane // width, 1.0, 0.0).astype(BF16)


def spread(pair, onehot):
    return dot(pair, onehot, ((0,), (0,)))


def adjoint_kernel(
    heads, rates_hbm, codes_hbm, gates_hbm, grad_hbm, c_hbm,
    near_out, far_out, front_out, logs_out, pay_out,
    rates, codes, gates, grad, c_proj, steps, small_sem, grad_sem, c_sem,
):
    rows, channels = grad.shape
    chunks = rows // CHUNK
    pieces = rows // STEP_ROWS
    small = [
        pltpu.make_async_copy(source, target, small_sem.at[i])
        for i, (source, target) in enumerate(
            ((rates_hbm, rates), (codes_hbm, codes), (gates_hbm, gates))
        )
    ]
    large = []
    for copy in small:
        copy.start()
    for piece in range(pieces):
        at = pl.ds(piece * STEP_ROWS, STEP_ROWS)
        large.append(pltpu.make_async_copy(grad_hbm.at[at], grad.at[at], grad_sem.at[piece]))
        large.append(pltpu.make_async_copy(c_hbm.at[at], c_proj.at[at], c_sem.at[piece]))
    for copy in large:
        copy.start()
    for copy in small:
        copy.wait()

    steps[...] = jnp.zeros_like(steps)
    steps[0:heads, :] = jnp.exp2(-codes[...].astype(F32))
    gate = gates[...]
    steps[6:7, :] = jnp.where(gate == 1, 1.0, 0.0).astype(F32)
    steps[7:8, :] = jnp.where(gate == 2, 1.0, 0.0).astype(F32)
    stacked = jnp.concatenate(
        [steps[:, j * CHUNK : (j + 1) * CHUNK] for j in range(chunks)], axis=0
    ).astype(BF16)
    row = lax.broadcasted_iota(jnp.int32, (CHUNK, CHUNK), 0)
    col = lax.broadcasted_iota(jnp.int32, (CHUNK, CHUNK), 1)
    upper = jnp.where(row <= col, 1.0, 0.0).astype(BF16)
    sums = dot(stacked, upper, ((1,), (0,)))
    sub = lax.broadcasted_iota(jnp.int32, (8, CHUNK), 0)
    rate = jnp.zeros((8, CHUNK), F32)
    for head in range(heads):
        rate = jnp.where(sub == head, rates[head], rate)
    cums, mids, befores = [], [], []
    before = jnp.zeros((8, 1), F32)
    for j in range(chunks):
        part = sums[8 * j : 8 * j + 8, :]
        cum = LOG_ONE * part[6:7, :] + LOG_TWO * part[7:8, :] - rate * part
        cums.append(cum)
        mids.append(cum[:, CHUNK // 2 - 1 : CHUNK // 2])
        befores.append(before)
        before = before + cum[:, CHUNK - 1 : CHUNK]
    for j in range(chunks):
        at = slice(j * CHUNK, (j + 1) * CHUNK)
        size = steps[:, at]
        near_out[0:16, at] = split_two(jnp.exp(cums[j] - mids[j]))
        near_out[16:32, at] = split_two(jnp.exp(mids[j] - cums[j]) * size)
        front_out[:, at] = split_two(jnp.exp(befores[j] + cums[j]))
        far_out[:, at] = split_two(jnp.exp(before - befores[j] - cums[j]) * size)
    pick = lax.broadcasted_iota(jnp.int32, (8, CHUNK), 0)
    place = lax.broadcasted_iota(jnp.int32, (8, CHUNK), 1)
    chosen = jnp.where((pick == 0) | ((pick == 1) & (place < CHUNK // 2)), 1.0, 0.0)
    flat = dot(chosen.astype(BF16), stacked, ((1,), (1,)))
    owner = lax.broadcasted_iota(jnp.int32, (chunks, 8 * chunks), 1) // 8
    chunk_at = lax.broadcasted_iota(jnp.int32, (chunks, 8 * chunks), 0)
    lane_rate = per_lane(rates, heads, channels)
    kind = lax.broadcasted_iota(jnp.int32, (8 * chunks, channels), 0) % 8
    lane_head = lax.broadcasted_iota(jnp.int32, (8 * chunks, channels), 1) // (channels // heads)
    mixer = jnp.where(kind == lane_head, -lane_rate, 0.0)
    mixer = jnp.where(kind == 6, LOG_ONE, jnp.where(kind == 7, LOG_TWO, mixer))
    table = []
    for which in range(2):
        own = jnp.where(owner == chunk_at, flat[which : which + 1, :], 0.0)
        table.append(dot(own, mixer, ((1,), (0,)), HIGHEST))
    whole = jnp.exp(table[0])
    middle = jnp.exp(table[1])
    rest_of = jnp.exp(table[0] - table[1])
    logs_out[0] = whole
    logs_out[1] = middle
    logs_out[2] = rest_of
    decay = jnp.exp(jnp.sum(table[0], axis=0, keepdims=True))
    first = decay.astype(BF16).astype(F32)
    second = (decay - first).astype(BF16).astype(F32)
    third = decay - first - second
    row = lax.broadcasted_iota(jnp.int32, (16, channels), 0)
    tail = jnp.where(
        row == 0, first, jnp.where(row == 1, second, jnp.where(row == 2, third, 0.0))
    )
    pay_out[STATE : STATE + 16, :] = tail.astype(BF16)

    onehot = spread_matrix(heads, channels)
    for copy in large:
        copy.wait()
    for piece in range(pieces):
        both = slice(piece * STEP_ROWS, (piece + 1) * STEP_ROWS)
        scale = spread(front_out[:, both], onehot)
        grad[both, :] = (grad[both, :].astype(F32) * scale).astype(BF16)
    pay_out[0:STATE, :] = dot(c_proj[...], grad[...], ((0,), (0,))).astype(BF16)


def lane_tiles(channels):
    return [slice(at, min(at + 128, channels)) for at in range(0, channels, 128)]


def state_kernel(
    heads, parts, taps, far, inputs, halo, b_proj, adjoint_pay, mixed_out, sigma_out, *rest
):
    pays, scaled = rest[: parts - 1], rest[parts - 1]
    rows, channels = inputs.shape
    me = lax.axis_index("seq")
    before = jnp.where(me > 0, halo[...].astype(F32), 0.0).astype(BF16)
    onehot = spread_matrix(heads, channels)
    row = lax.broadcasted_iota(jnp.int32, (3 * CHUNK, CHUNK + 16), 0)
    col = lax.broadcasted_iota(jnp.int32, (3 * CHUNK, CHUNK + 16), 1)
    shift = jnp.where(col == row % CHUNK + 13 + row // CHUNK, 1.0, 0.0).astype(BF16)
    for at in range(0, rows, CHUNK):
        both = slice(at, at + CHUNK)
        if at == 0:
            block = jnp.concatenate([before, inputs[both, :]], axis=0)
        else:
            block = inputs[at - 16 : at + CHUNK, :]
        moved = dot(shift, block, ((1,), (0,)))
        preact = taps[3:4, :] * inputs[both, :].astype(F32)
        for k in range(3):
            preact = preact + taps[k : k + 1, :] * moved[k * CHUNK : (k + 1) * CHUNK, :]
        sigma = 0.5 * jnp.tanh(0.5 * preact) + 0.5
        mixed = preact * sigma
        sigma_out[both, :] = sigma
        mixed_out[both, :] = mixed
        scaled[both, :] = (mixed * spread(far[:, both], onehot)).astype(BF16)
    state = dot(b_proj[...], scaled[...], ((0,), (0,))).astype(BF16)
    for distance in range(1, parts):
        pay = pays[distance - 1]
        pay[0:STATE, :] = jnp.where(me + distance < parts, state, adjoint_pay[0:STATE, :])
        pay[STATE : STATE + 16, :] = adjoint_pay[STATE : STATE + 16, :]


def merged(parts, pays, forward):
    me = lax.axis_index("seq")
    running = jnp.zeros((STATE, pays[0].shape[1]), F32)
    for distance in range(parts - 1, 0, -1):
        held = pays[distance - 1] if forward else pays[parts - distance - 1]
        there = (me >= distance) if forward else (me + distance < parts)
        decay = (
            held[STATE : STATE + 1, :].astype(F32) + held[STATE + 1 : STATE + 2, :].astype(F32)
        ) + held[STATE + 2 : STATE + 3, :].astype(F32)
        running = jnp.where(there, held[0:STATE, :].astype(F32) + decay * running, 0.0)
    return running.astype(BF16)


def inner_kernel(
    heads, gains, near, far, logs, grad, mixed, sigma, b_proj, c_proj,
    base_out, grad_base, grad_weight,
    ahead_scores, behind_scores, mixed_scaled, mixed_low, grad_scaled, grad_low,
    mixed_fresh, grad_fresh,
):
    rows, channels = grad.shape
    chunks = rows // CHUNK
    blocks = [slice(j * CHUNK, (j + 1) * CHUNK) for j in range(chunks)]
    row = lax.broadcasted_iota(jnp.int32, (CHUNK, CHUNK), 0)
    col = lax.broadcasted_iota(jnp.int32, (CHUNK, CHUNK), 1)
    onehot = spread_matrix(heads, channels)
    gain = per_lane(gains, heads, channels)
    for both in blocks:
        scale = spread(near[0:16, both], onehot)
        grad_scaled[both, :] = (grad[both, :].astype(F32) * scale).astype(BF16)
    for both in blocks:
        scale = spread(near[16:32, both], onehot)
        mixed_scaled[both, :] = (mixed[both, :] * scale).astype(BF16)
    for both in blocks:
        grad_fresh[both, :] = dot(c_proj[both, :], grad_scaled[both, :], ((0,), (0,)))
    for both in blocks:
        mixed_fresh[both, :] = dot(b_proj[both, :], mixed_scaled[both, :], ((0,), (0,)))
    for both in blocks:
        ahead = dot(c_proj[both, :], b_proj[both, :], ((1,), (1,)))
        ahead_scores[both, :] = jnp.where(row >= col, ahead, 0.0).astype(BF16)
    for both in blocks:
        behind = dot(b_proj[both, :], c_proj[both, :], ((1,), (1,)))
        behind_scores[both, :] = jnp.where(row <= col, behind, 0.0).astype(BF16)
    for lanes in lane_tiles(channels):
        adjoint = jnp.zeros((STATE, lanes.stop - lanes.start), F32)
        for j in range(chunks - 1, -1, -1):
            grad_low[blocks[j], lanes] = (adjoint * logs[2, j : j + 1, lanes]).astype(BF16)
            adjoint = logs[0, j : j + 1, lanes] * adjoint + (
                logs[1, j : j + 1, lanes] * grad_fresh[blocks[j], lanes]
            )
        state = jnp.zeros((STATE, lanes.stop - lanes.start), F32)
        for j in range(chunks):
            mixed_low[blocks[j], lanes] = (state * logs[1, j : j + 1, lanes]).astype(BF16)
            state = logs[0, j : j + 1, lanes] * state + (
                logs[2, j : j + 1, lanes] * mixed_fresh[blocks[j], lanes]
            )
    for both in blocks:
        inner = dot(
            jnp.concatenate([behind_scores[both, :], b_proj[both, :]], axis=1),
            jnp.concatenate([grad_scaled[both, :], grad_low[both, :]], axis=0),
            ((1,), (0,)),
        )
        slope = sigma[both, :] + mixed[both, :] * (1.0 - sigma[both, :])
        inner = gain * grad[both, :].astype(F32) + spread(near[16:32, both], onehot) * inner
        grad_base[both, :] = slope * inner
        grad_weight[both, :] = slope * spread(far[:, both], onehot)
    for both in blocks:
        inner = dot(
            jnp.concatenate([ahead_scores[both, :], c_proj[both, :]], axis=1),
            jnp.concatenate([mixed_scaled[both, :], mixed_low[both, :]], axis=0),
            ((1,), (0,)),
        )
        base_out[both, :] = gain * mixed[both, :] + spread(near[0:16, both], onehot) * inner


def gradient_kernel(parts, taps, base, weight, inputs, halo, b_proj, *rest):
    pays = rest[: parts - 1]
    grad_out, tail_out, edge_out, window, exact = rest[parts - 1 :]
    rows, channels = base.shape
    chunks = rows // CHUNK
    adjoint = merged(parts, pays, False)
    me = lax.axis_index("seq")
    window[rows : rows + 16, :] = jnp.zeros((16, channels), BF16)
    row = lax.broadcasted_iota(jnp.int32, (3 * CHUNK, CHUNK + 16), 0)
    col = lax.broadcasted_iota(jnp.int32, (3 * CHUNK, CHUNK + 16), 1)
    shift = jnp.where(col == row % CHUNK + 3 - row // CHUNK, 1.0, 0.0).astype(BF16)
    partial = [jnp.zeros((8, channels), F32) for _ in range(4)]
    for j in range(chunks):
        both = slice(j * CHUNK, (j + 1) * CHUNK)
        grad_pre = base[both, :] + weight[both, :] * dot(b_proj[both, :], adjoint, ((1,), (0,)))
        window[both, :] = grad_pre.astype(BF16)
        exact[both, :] = grad_pre
    for j in range(chunks):
        at = j * CHUNK
        both = slice(at, at + CHUNK)
        grad_pre = exact[both, :]
        moved = dot(shift, window[at : at + CHUNK + 16, :], ((1,), (0,)))
        x = inputs[both, :].astype(F32)
        result = taps[3:4, :] * grad_pre
        partial[3] = partial[3] + (grad_pre * x).reshape(CHUNK // 8, 8, channels).sum(axis=0)
        for k in range(3):
            part = moved[k * CHUNK : (k + 1) * CHUNK, :]
            result = result + taps[k : k + 1, :] * part
            partial[k] = partial[k] + (part * x).reshape(CHUNK // 8, 8, channels).sum(axis=0)
        grad_out[both, :] = result.astype(BF16)
        if j == chunks - 1:
            edge_out[...] = result[CHUNK - 16 :, :]
    first = exact[0:8, :]
    before = jnp.where(me > 0, halo[...].astype(F32), 0.0)
    for k in range(4):
        tap = jnp.sum(partial[k], axis=0, keepdims=True)
        for j in range(k, 3):
            tap = tap + first[j - k : j - k + 1, :] * before[13 + j : 14 + j, :]
        tail_out[k : k + 1, :] = tap
    tail_out[4:7, :] = first[0:3, :]
    tail_out[7:8, :] = jnp.zeros((1, channels), F32)


def output_kernel(heads, parts, front, base, c_proj, grad_rows, *rest):
    pays = rest[: parts - 1]
    out_hbm, grad_hbm, result_rows, sems, grad_sem = rest[parts - 1 :]
    rows, channels = base.shape
    grad_copy = pltpu.make_async_copy(grad_rows, grad_hbm, grad_sem)
    grad_copy.start()
    state = merged(parts, pays, True)
    onehot = spread_matrix(heads, channels)
    copies = []
    for piece in range(rows // STEP_ROWS):
        for at in range(piece * STEP_ROWS, (piece + 1) * STEP_ROWS, CHUNK):
            both = slice(at, at + CHUNK)
            carried = dot(c_proj[both, :], state, ((1,), (0,)))
            result = base[both, :] + spread(front[:, both], onehot) * carried
            result_rows[both, :] = result.astype(BF16)
        place = pl.ds(piece * STEP_ROWS, STEP_ROWS)
        copy = pltpu.make_async_copy(result_rows.at[place], out_hbm.at[place], sems.at[piece])
        copy.start()
        copies.append(copy)
    for copy in copies:
        copy.wait()
    grad_copy.wait()


def finish_kernel(parts, scale, taps, tail, edge, *rest):
    others = rest[: parts - 1]
    unused, grad_hbm, conv_out, rows_low, sem = rest[parts - 1 :]
    channels = tail.shape[1]
    me = lax.axis_index("seq")
    after = jnp.where(me + 1 < parts, others[parts - 2][...], 0.0)
    row = lax.broadcasted_iota(jnp.int32, (16, channels), 0)
    result = edge[...]
    for r in range(3):
        extra = jnp.zeros((1, channels), F32)
        for k in range(r + 1):
            extra = extra + taps[k : k + 1, :] * after[4 + r - k : 5 + r - k, :]
        result = jnp.where(row == 13 + r, result + extra, result)
    rows_low[...] = result.astype(BF16)
    rows = grad_hbm.shape[0]
    copy = pltpu.make_async_copy(rows_low, grad_hbm.at[pl.ds(rows - 16, 16)], sem)
    copy.start()
    total = tail[0:4, :]
    for other in others:
        total = total + other[0:4, :]
    conv_out[...] = total * scale
    copy.wait()


def rotated(block, axis, distance):
    size = lax.axis_size(axis)
    return lax.ppermute(block, axis, [(i, (i + distance) % size) for i in range(size)])


def shards(
    inputs,
    b_proj,
    c_proj,
    step_codes,
    gate_codes,
    decay_rates,
    skip_gain,
    conv_weight,
    out_cotangent,
):
    rows, channels = inputs.shape
    heads = decay_rates.shape[0]
    parts = lax.axis_size("seq")
    chunks = rows // CHUNK
    pieces = rows // STEP_ROWS
    hbm = pl.BlockSpec(memory_space=pltpu.HBM)
    vmem = pl.BlockSpec(memory_space=pltpu.VMEM)
    smem = pl.BlockSpec(memory_space=pltpu.SMEM)
    shape = jax.ShapeDtypeStruct
    dma = pltpu.SemaphoreType.DMA
    big = rows * channels

    def call(kernel, in_specs, out_specs, out_shape, scratch, products, aliases=None):
        return pl.pallas_call(
            kernel,
            in_specs=in_specs,
            out_specs=out_specs,
            out_shape=out_shape,
            scratch_shapes=scratch,
            input_output_aliases=aliases or {},
            compiler_params=pltpu.CompilerParams(vmem_limit_bytes=VMEM_LIMIT),
            cost_estimate=pl.CostEstimate(
                flops=products * 2 * big * 128, bytes_accessed=6 * big, transcendentals=big
            ),
        )

    def stay(array):
        return pltpu.with_memory_space_constraint(array, pltpu.HBM)

    halo = rotated(inputs[rows - 16 :], "seq", 1)
    pay = shape((STATE + 16, channels), BF16)
    narrow = shape((rows, channels), BF16)
    broad = shape((rows, channels), F32)

    near, far, front, logs, adjoint_pay = call(
        functools.partial(adjoint_kernel, heads),
        [hbm] * 5,
        [vmem] * 5,
        [
            shape((32, rows), BF16),
            shape((16, rows), BF16),
            shape((16, rows), BF16),
            shape((3, chunks, channels), F32),
            pay,
        ],
        [
            pltpu.SMEM((heads,), F32),
            pltpu.VMEM((heads, rows), jnp.int32),
            pltpu.VMEM((1, rows), jnp.int32),
            pltpu.VMEM((rows, channels), BF16),
            pltpu.VMEM((rows, 128), BF16),
            pltpu.VMEM((8, rows), F32),
            dma((3,)),
            dma((pieces,)),
            dma((pieces,)),
        ],
        2,
    )(
        stay(decay_rates),
        stay(step_codes),
        stay(gate_codes.reshape(1, rows)),
        stay(out_cotangent),
        stay(c_proj),
    )

    outs = call(
        functools.partial(state_kernel, heads, parts),
        [vmem] * 6,
        [vmem] * (1 + parts),
        [broad, broad] + [pay] * (parts - 1),
        [pltpu.VMEM((rows, channels), BF16)],
        2,
    )(conv_weight, far, inputs, halo, b_proj, adjoint_pay)
    mixed, sigma = outs[:2]
    pays = [rotated(send, "seq", distance + 1) for distance, send in enumerate(outs[2:])]

    tile = pltpu.VMEM((rows, CHUNK), BF16)
    low = pltpu.VMEM((rows, channels), BF16)
    high = pltpu.VMEM((rows, channels), F32)
    base, grad_base, grad_weight = call(
        functools.partial(inner_kernel, heads),
        [smem] + [vmem] * 8,
        [vmem] * 3,
        [broad] * 3,
        [tile, tile, low, low, low, low, high, high],
        10,
    )(skip_gain, near, far, logs, out_cotangent, mixed, sigma, b_proj, c_proj)

    grad_rows, tail, edge = call(
        functools.partial(gradient_kernel, parts),
        [vmem] * (5 + parts),
        [vmem] * 3,
        [narrow, shape((8, channels), F32), shape((16, channels), F32)],
        [pltpu.VMEM((rows + 16, channels), BF16), pltpu.VMEM((rows, channels), F32)],
        2,
    )(conv_weight, grad_base, grad_weight, inputs, halo, b_proj, *pays)
    tails = [rotated(tail, "seq", distance) for distance in range(1, parts)]

    layer_out, grad_rows = call(
        functools.partial(output_kernel, heads, parts),
        [vmem] * (3 + parts),
        [hbm, hbm],
        [narrow, narrow],
        [pltpu.VMEM((rows, channels), BF16), dma((pieces,)), dma],
        2,
    )(front, base, c_proj, grad_rows, *pays)

    scale = float((rows * parts) ** -0.5)
    input_grad, conv_grad = call(
        functools.partial(finish_kernel, parts, scale),
        [vmem] * (2 + parts) + [hbm],
        [hbm, vmem],
        [narrow, shape((4, channels), F32)],
        [pltpu.VMEM((16, channels), BF16), dma],
        0,
        {parts + 2: 0},
    )(conv_weight, tail, edge, *tails, grad_rows)
    return layer_out, input_grad, conv_grad


def solution(mesh):
    in_specs = (
        P(("groups", "seq"), ("head", "sub")),
        P(("groups", "seq"), None),
        P(("groups", "seq"), None),
        P(("head", "sub"), ("groups", "seq")),
        P(("groups", "seq")),
        P(("head", "sub")),
        P(("head", "sub")),
        P(None, ("head", "sub")),
        P(("groups", "seq"), ("head", "sub")),
    )
    out_specs = (
        P(("groups", "seq"), ("head", "sub")),
        P(("groups", "seq"), ("head", "sub")),
        P("groups", ("head", "sub")),
    )
    return jax.shard_map(shards, mesh=mesh, in_specs=in_specs, out_specs=out_specs, check_vma=False)
```

```python
import functools

import jax
import jax.numpy as jnp
from jax import lax
from jax.experimental import pallas as pl
from jax.experimental.pallas import tpu as pltpu
from jax.sharding import PartitionSpec as P

CHUNK = 128
STATE = 128
STEP_ROWS = 512
LOG_ONE = -0.2876820724517809
LOG_TWO = -0.6931471805599453
F32 = jnp.float32
BF16 = jnp.bfloat16
HIGHEST = lax.Precision.HIGHEST
VMEM_LIMIT = 28 * 1024 * 1024


def dot(a, b, dims, precision=None):
    return lax.dot_general(a, b, (dims, ((), ())), preferred_element_type=F32, precision=precision)


def per_lane(scalars, count, channels):
    width = channels // count
    lane = lax.broadcasted_iota(jnp.int32, (1, channels), 1)
    row = jnp.zeros((1, channels), F32)
    for head in range(count):
        inside = (lane >= head * width) & (lane < (head + 1) * width)
        row = jnp.where(inside, scalars[head], row)
    return row


def split_two(value):
    high = value.astype(BF16)
    low = (value - high.astype(F32)).astype(BF16)
    return jnp.concatenate([high.astype(F32), low.astype(F32)], axis=0).astype(BF16)


def spread_matrix(count, channels):
    width = channels // count
    row = lax.broadcasted_iota(jnp.int32, (16, channels), 0)
    lane = lax.broadcasted_iota(jnp.int32, (16, channels), 1)
    return jnp.where((row % 8) == lane // width, 1.0, 0.0).astype(BF16)


def spread(pair, onehot):
    return dot(pair, onehot, ((0,), (0,)))


def adjoint_kernel(
    heads, rates_hbm, codes_hbm, gates_hbm, grad_hbm, c_hbm,
    near_out, far_out, front_out, logs_out, pay_out,
    rates, codes, gates, grad, c_proj, steps, small_sem, grad_sem, c_sem,
):
    rows, channels = grad.shape
    chunks = rows // CHUNK
    pieces = rows // STEP_ROWS
    small = [
        pltpu.make_async_copy(source, target, small_sem.at[i])
        for i, (source, target) in enumerate(
            ((rates_hbm, rates), (codes_hbm, codes), (gates_hbm, gates))
        )
    ]
    large = []
    for copy in small:
        copy.start()
    for piece in range(pieces):
        at = pl.ds(piece * STEP_ROWS, STEP_ROWS)
        large.append(pltpu.make_async_copy(grad_hbm.at[at], grad.at[at], grad_sem.at[piece]))
        large.append(pltpu.make_async_copy(c_hbm.at[at], c_proj.at[at], c_sem.at[piece]))
    for copy in large:
        copy.start()
    for copy in small:
        copy.wait()

    steps[...] = jnp.zeros_like(steps)
    steps[0:heads, :] = jnp.exp2(-codes[...].astype(F32))
    gate = gates[...]
    steps[6:7, :] = jnp.where(gate == 1, 1.0, 0.0).astype(F32)
    steps[7:8, :] = jnp.where(gate == 2, 1.0, 0.0).astype(F32)
    stacked = jnp.concatenate(
        [steps[:, j * CHUNK : (j + 1) * CHUNK] for j in range(chunks)], axis=0
    ).astype(BF16)
    row = lax.broadcasted_iota(jnp.int32, (CHUNK, CHUNK), 0)
    col = lax.broadcasted_iota(jnp.int32, (CHUNK, CHUNK), 1)
    upper = jnp.where(row <= col, 1.0, 0.0).astype(BF16)
    sums = dot(stacked, upper, ((1,), (0,)))
    sub = lax.broadcasted_iota(jnp.int32, (8, CHUNK), 0)
    rate = jnp.zeros((8, CHUNK), F32)
    for head in range(heads):
        rate = jnp.where(sub == head, rates[head], rate)
    cums, mids, befores = [], [], []
    before = jnp.zeros((8, 1), F32)
    for j in range(chunks):
        part = sums[8 * j : 8 * j + 8, :]
        cum = LOG_ONE * part[6:7, :] + LOG_TWO * part[7:8, :] - rate * part
        cums.append(cum)
        mids.append(cum[:, CHUNK // 2 - 1 : CHUNK // 2])
        befores.append(before)
        before = before + cum[:, CHUNK - 1 : CHUNK]
    for j in range(chunks):
        at = slice(j * CHUNK, (j + 1) * CHUNK)
        size = steps[:, at]
        near_out[0:16, at] = split_two(jnp.exp(cums[j] - mids[j]))
        near_out[16:32, at] = split_two(jnp.exp(mids[j] - cums[j]) * size)
        front_out[:, at] = split_two(jnp.exp(befores[j] + cums[j]))
        far_out[:, at] = split_two(jnp.exp(before - befores[j] - cums[j]) * size)
    pick = lax.broadcasted_iota(jnp.int32, (8, CHUNK), 0)
    place = lax.broadcasted_iota(jnp.int32, (8, CHUNK), 1)
    chosen = jnp.where((pick == 0) | ((pick == 1) & (place < CHUNK // 2)), 1.0, 0.0)
    flat = dot(chosen.astype(BF16), stacked, ((1,), (1,)))
    owner = lax.broadcasted_iota(jnp.int32, (chunks, 8 * chunks), 1) // 8
    chunk_at = lax.broadcasted_iota(jnp.int32, (chunks, 8 * chunks), 0)
    lane_rate = per_lane(rates, heads, channels)
    kind = lax.broadcasted_iota(jnp.int32, (8 * chunks, channels), 0) % 8
    lane_head = lax.broadcasted_iota(jnp.int32, (8 * chunks, channels), 1) // (channels // heads)
    mixer = jnp.where(kind == lane_head, -lane_rate, 0.0)
    mixer = jnp.where(kind == 6, LOG_ONE, jnp.where(kind == 7, LOG_TWO, mixer))
    table = []
    for which in range(2):
        own = jnp.where(owner == chunk_at, flat[which : which + 1, :], 0.0)
        table.append(dot(own, mixer, ((1,), (0,)), HIGHEST))
    whole = jnp.exp(table[0])
    middle = jnp.exp(table[1])
    rest_of = jnp.exp(table[0] - table[1])
    logs_out[0] = whole
    logs_out[1] = middle
    logs_out[2] = rest_of
    decay = jnp.exp(jnp.sum(table[0], axis=0, keepdims=True))
    first = decay.astype(BF16).astype(F32)
    second = (decay - first).astype(BF16).astype(F32)
    third = decay - first - second
    row = lax.broadcasted_iota(jnp.int32, (16, channels), 0)
    tail = jnp.where(
        row == 0, first, jnp.where(row == 1, second, jnp.where(row == 2, third, 0.0))
    )
    pay_out[STATE : STATE + 16, :] = tail.astype(BF16)

    onehot = spread_matrix(heads, channels)
    for copy in large:
        copy.wait()
    for piece in range(pieces):
        both = slice(piece * STEP_ROWS, (piece + 1) * STEP_ROWS)
        scale = spread(front_out[:, both], onehot)
        grad[both, :] = (grad[both, :].astype(F32) * scale).astype(BF16)
    pay_out[0:STATE, :] = dot(c_proj[...], grad[...], ((0,), (0,))).astype(BF16)


def back_shift():
    row = lax.broadcasted_iota(jnp.int32, (3 * CHUNK, CHUNK + 16), 0)
    col = lax.broadcasted_iota(jnp.int32, (3 * CHUNK, CHUNK + 16), 1)
    return jnp.where(col == row % CHUNK + 13 + row // CHUNK, 1.0, 0.0).astype(BF16)


def shifted_inputs(shift, before, inputs, at):
    if at == 0:
        block = jnp.concatenate([before, inputs[0:CHUNK, :]], axis=0)
    else:
        block = inputs[at - 16 : at + CHUNK, :]
    return dot(shift, block, ((1,), (0,)))


def lane_tiles(channels):
    return [slice(at, min(at + 128, channels)) for at in range(0, channels, 128)]


def state_kernel(
    heads, parts, taps, far, inputs, halo, b_proj, adjoint_pay, mixed_out, sigma_out, *rest
):
    pays, scaled = rest[: parts - 1], rest[parts - 1]
    rows, channels = inputs.shape
    me = lax.axis_index("seq")
    before = jnp.where(me > 0, halo[...].astype(F32), 0.0).astype(BF16)
    onehot = spread_matrix(heads, channels)
    shift = back_shift()
    for at in range(0, rows, CHUNK):
        both = slice(at, at + CHUNK)
        moved = shifted_inputs(shift, before, inputs, at)
        preact = taps[3:4, :] * inputs[both, :].astype(F32)
        for k in range(3):
            preact = preact + taps[k : k + 1, :] * moved[k * CHUNK : (k + 1) * CHUNK, :]
        sigma = 0.5 * jnp.tanh(0.5 * preact) + 0.5
        mixed = preact * sigma
        sigma_out[both, :] = sigma
        mixed_out[both, :] = mixed
        scaled[both, :] = (mixed * spread(far[:, both], onehot)).astype(BF16)
    state = dot(b_proj[...], scaled[...], ((0,), (0,))).astype(BF16)
    for distance in range(1, parts):
        pay = pays[distance - 1]
        pay[0:STATE, :] = jnp.where(me + distance < parts, state, adjoint_pay[0:STATE, :])
        pay[STATE : STATE + 16, :] = adjoint_pay[STATE : STATE + 16, :]


def merged(parts, pays, forward):
    me = lax.axis_index("seq")
    running = jnp.zeros((STATE, pays[0].shape[1]), F32)
    for distance in range(parts - 1, 0, -1):
        held = pays[distance - 1] if forward else pays[parts - distance - 1]
        there = (me >= distance) if forward else (me + distance < parts)
        decay = (
            held[STATE : STATE + 1, :].astype(F32) + held[STATE + 1 : STATE + 2, :].astype(F32)
        ) + held[STATE + 2 : STATE + 3, :].astype(F32)
        running = jnp.where(there, held[0:STATE, :].astype(F32) + decay * running, 0.0)
    return running.astype(BF16)


def inner_kernel(
    heads, gains, near, far, logs, grad, mixed, sigma, b_proj, c_proj, inputs, halo,
    base_out, grad_base, grad_weight, tap_base, tap_weight,
    ahead_scores, behind_scores, mixed_scaled, mixed_low, grad_scaled, grad_low,
    mixed_fresh, grad_fresh, base_products, weight_products,
):
    rows, channels = grad.shape
    chunks = rows // CHUNK
    blocks = [slice(j * CHUNK, (j + 1) * CHUNK) for j in range(chunks)]
    row = lax.broadcasted_iota(jnp.int32, (CHUNK, CHUNK), 0)
    col = lax.broadcasted_iota(jnp.int32, (CHUNK, CHUNK), 1)
    onehot = spread_matrix(heads, channels)
    gain = per_lane(gains, heads, channels)
    shift = back_shift()
    before = jnp.where(lax.axis_index("seq") > 0, halo[...].astype(F32), 0.0).astype(BF16)
    for both in blocks:
        scale = spread(near[0:16, both], onehot)
        grad_scaled[both, :] = (grad[both, :].astype(F32) * scale).astype(BF16)
    for both in blocks:
        scale = spread(near[16:32, both], onehot)
        mixed_scaled[both, :] = (mixed[both, :] * scale).astype(BF16)
    for both in blocks:
        grad_fresh[both, :] = dot(c_proj[both, :], grad_scaled[both, :], ((0,), (0,)))
    for both in blocks:
        mixed_fresh[both, :] = dot(b_proj[both, :], mixed_scaled[both, :], ((0,), (0,)))
    for both in blocks:
        ahead = dot(c_proj[both, :], b_proj[both, :], ((1,), (1,)))
        ahead_scores[both, :] = jnp.where(row >= col, ahead, 0.0).astype(BF16)
    for both in blocks:
        behind = dot(b_proj[both, :], c_proj[both, :], ((1,), (1,)))
        behind_scores[both, :] = jnp.where(row <= col, behind, 0.0).astype(BF16)
    for lanes in lane_tiles(channels):
        adjoint = jnp.zeros((STATE, lanes.stop - lanes.start), F32)
        for j in range(chunks - 1, -1, -1):
            grad_low[blocks[j], lanes] = (adjoint * logs[2, j : j + 1, lanes]).astype(BF16)
            adjoint = logs[0, j : j + 1, lanes] * adjoint + (
                logs[1, j : j + 1, lanes] * grad_fresh[blocks[j], lanes]
            )
        state = jnp.zeros((STATE, lanes.stop - lanes.start), F32)
        for j in range(chunks):
            mixed_low[blocks[j], lanes] = (state * logs[1, j : j + 1, lanes]).astype(BF16)
            state = logs[0, j : j + 1, lanes] * state + (
                logs[2, j : j + 1, lanes] * mixed_fresh[blocks[j], lanes]
            )
    for both in blocks:
        inner = dot(
            jnp.concatenate([behind_scores[both, :], b_proj[both, :]], axis=1),
            jnp.concatenate([grad_scaled[both, :], grad_low[both, :]], axis=0),
            ((1,), (0,)),
        )
        slope = sigma[both, :] + mixed[both, :] * (1.0 - sigma[both, :])
        inner = gain * grad[both, :].astype(F32) + spread(near[16:32, both], onehot) * inner
        part = slope * inner
        weight = slope * spread(far[:, both], onehot)
        grad_base[both, :] = part
        grad_weight[both, :] = weight
        part = part.astype(BF16)
        weight = weight.astype(BF16)
        moved = shifted_inputs(shift, before, inputs, both.start)
        for k in range(4):
            x = inputs[both, :]
            if k < 3:
                x = moved[k * CHUNK : (k + 1) * CHUNK, :].astype(BF16)
            base_products[k, both, :] = part * x
            weight_products[k, both, :] = weight * x
    for both in blocks:
        inner = dot(
            jnp.concatenate([ahead_scores[both, :], c_proj[both, :]], axis=1),
            jnp.concatenate([mixed_scaled[both, :], mixed_low[both, :]], axis=0),
            ((1,), (0,)),
        )
        base_out[both, :] = gain * mixed[both, :] + spread(near[0:16, both], onehot) * inner
    ones = jnp.ones((8, rows), BF16)
    tap_base[...] = jnp.zeros_like(tap_base)
    for k in range(4):
        sums = dot(ones, base_products[k], ((1,), (0,)))
        tap_base[k : k + 1, :] = sums[0:1, :]
        tap_weight[k] = dot(b_proj[...], weight_products[k], ((0,), (0,)))


def gradient_kernel(parts, taps, base, weight, tap_base, tap_weight, b_proj, *rest):
    pays = rest[: parts - 1]
    grad_out, tail_out, edge_out, window, exact = rest[parts - 1 :]
    rows, channels = base.shape
    chunks = rows // CHUNK
    adjoint = merged(parts, pays, False)
    window[rows : rows + 16, :] = jnp.zeros((16, channels), BF16)
    row = lax.broadcasted_iota(jnp.int32, (3 * CHUNK, CHUNK + 16), 0)
    col = lax.broadcasted_iota(jnp.int32, (3 * CHUNK, CHUNK + 16), 1)
    shift = jnp.where(col == row % CHUNK + 3 - row // CHUNK, 1.0, 0.0).astype(BF16)
    for j in range(chunks):
        both = slice(j * CHUNK, (j + 1) * CHUNK)
        grad_pre = base[both, :] + weight[both, :] * dot(b_proj[both, :], adjoint, ((1,), (0,)))
        window[both, :] = grad_pre.astype(BF16)
        exact[both, :] = grad_pre
    for j in range(chunks):
        at = j * CHUNK
        both = slice(at, at + CHUNK)
        grad_pre = exact[both, :]
        moved = dot(shift, window[at : at + CHUNK + 16, :], ((1,), (0,)))
        result = taps[3:4, :] * grad_pre
        for k in range(3):
            result = result + taps[k : k + 1, :] * moved[k * CHUNK : (k + 1) * CHUNK, :]
        grad_out[both, :] = result.astype(BF16)
        if j == chunks - 1:
            edge_out[...] = result[CHUNK - 16 :, :]
    carried = adjoint.astype(F32)
    for k in range(4):
        tap = jnp.sum(carried * tap_weight[k], axis=0, keepdims=True)
        tail_out[k : k + 1, :] = tap_base[k : k + 1, :] + tap
    tail_out[4:7, :] = exact[0:3, :]
    tail_out[7:8, :] = jnp.zeros((1, channels), F32)


def output_kernel(heads, parts, front, base, c_proj, grad_rows, *rest):
    pays = rest[: parts - 1]
    out_hbm, grad_hbm, result_rows, sems, grad_sem = rest[parts - 1 :]
    rows, channels = base.shape
    grad_copy = pltpu.make_async_copy(grad_rows, grad_hbm, grad_sem)
    grad_copy.start()
    state = merged(parts, pays, True)
    onehot = spread_matrix(heads, channels)
    copies = []
    for piece in range(rows // STEP_ROWS):
        for at in range(piece * STEP_ROWS, (piece + 1) * STEP_ROWS, CHUNK):
            both = slice(at, at + CHUNK)
            carried = dot(c_proj[both, :], state, ((1,), (0,)))
            result = base[both, :] + spread(front[:, both], onehot) * carried
            result_rows[both, :] = result.astype(BF16)
        place = pl.ds(piece * STEP_ROWS, STEP_ROWS)
        copy = pltpu.make_async_copy(result_rows.at[place], out_hbm.at[place], sems.at[piece])
        copy.start()
        copies.append(copy)
    for copy in copies:
        copy.wait()
    grad_copy.wait()


def finish_kernel(parts, scale, taps, tail, edge, *rest):
    others = rest[: parts - 1]
    unused, grad_hbm, conv_out, rows_low, sem = rest[parts - 1 :]
    channels = tail.shape[1]
    me = lax.axis_index("seq")
    after = jnp.where(me + 1 < parts, others[parts - 2][...], 0.0)
    row = lax.broadcasted_iota(jnp.int32, (16, channels), 0)
    result = edge[...]
    for r in range(3):
        extra = jnp.zeros((1, channels), F32)
        for k in range(r + 1):
            extra = extra + taps[k : k + 1, :] * after[4 + r - k : 5 + r - k, :]
        result = jnp.where(row == 13 + r, result + extra, result)
    rows_low[...] = result.astype(BF16)
    rows = grad_hbm.shape[0]
    copy = pltpu.make_async_copy(rows_low, grad_hbm.at[pl.ds(rows - 16, 16)], sem)
    copy.start()
    total = tail[0:4, :]
    for other in others:
        total = total + other[0:4, :]
    conv_out[...] = total * scale
    copy.wait()


def rotated(block, axis, distance):
    size = lax.axis_size(axis)
    return lax.ppermute(block, axis, [(i, (i + distance) % size) for i in range(size)])


def shards(
    inputs,
    b_proj,
    c_proj,
    step_codes,
    gate_codes,
    decay_rates,
    skip_gain,
    conv_weight,
    out_cotangent,
):
    rows, channels = inputs.shape
    heads = decay_rates.shape[0]
    parts = lax.axis_size("seq")
    chunks = rows // CHUNK
    pieces = rows // STEP_ROWS
    hbm = pl.BlockSpec(memory_space=pltpu.HBM)
    vmem = pl.BlockSpec(memory_space=pltpu.VMEM)
    smem = pl.BlockSpec(memory_space=pltpu.SMEM)
    shape = jax.ShapeDtypeStruct
    dma = pltpu.SemaphoreType.DMA
    big = rows * channels

    def call(kernel, in_specs, out_specs, out_shape, scratch, products, aliases=None):
        return pl.pallas_call(
            kernel,
            in_specs=in_specs,
            out_specs=out_specs,
            out_shape=out_shape,
            scratch_shapes=scratch,
            input_output_aliases=aliases or {},
            compiler_params=pltpu.CompilerParams(vmem_limit_bytes=VMEM_LIMIT),
            cost_estimate=pl.CostEstimate(
                flops=products * 2 * big * 128, bytes_accessed=6 * big, transcendentals=big
            ),
        )

    def stay(array):
        return pltpu.with_memory_space_constraint(array, pltpu.HBM)

    halo = rotated(inputs[rows - 16 :], "seq", 1)
    pay = shape((STATE + 16, channels), BF16)
    narrow = shape((rows, channels), BF16)
    broad = shape((rows, channels), F32)

    near, far, front, logs, adjoint_pay = call(
        functools.partial(adjoint_kernel, heads),
        [hbm] * 5,
        [vmem] * 5,
        [
            shape((32, rows), BF16),
            shape((16, rows), BF16),
            shape((16, rows), BF16),
            shape((3, chunks, channels), F32),
            pay,
        ],
        [
            pltpu.SMEM((heads,), F32),
            pltpu.VMEM((heads, rows), jnp.int32),
            pltpu.VMEM((1, rows), jnp.int32),
            pltpu.VMEM((rows, channels), BF16),
            pltpu.VMEM((rows, 128), BF16),
            pltpu.VMEM((8, rows), F32),
            dma((3,)),
            dma((pieces,)),
            dma((pieces,)),
        ],
        2,
    )(
        stay(decay_rates),
        stay(step_codes),
        stay(gate_codes.reshape(1, rows)),
        stay(out_cotangent),
        stay(c_proj),
    )

    outs = call(
        functools.partial(state_kernel, heads, parts),
        [vmem] * 6,
        [vmem] * (1 + parts),
        [broad, broad] + [pay] * (parts - 1),
        [pltpu.VMEM((rows, channels), BF16)],
        2,
    )(conv_weight, far, inputs, halo, b_proj, adjoint_pay)
    mixed, sigma = outs[:2]
    pays = [rotated(send, "seq", distance + 1) for distance, send in enumerate(outs[2:])]

    tile = pltpu.VMEM((rows, CHUNK), BF16)
    low = pltpu.VMEM((rows, channels), BF16)
    high = pltpu.VMEM((rows, channels), F32)
    products = pltpu.VMEM((4, rows, channels), BF16)
    base, grad_base, grad_weight, tap_base, tap_weight = call(
        functools.partial(inner_kernel, heads),
        [smem] + [vmem] * 10,
        [vmem] * 5,
        [broad] * 3 + [shape((8, channels), F32), shape((4, STATE, channels), F32)],
        [tile, tile, low, low, low, low, high, high, products, products],
        18,
    )(skip_gain, near, far, logs, out_cotangent, mixed, sigma, b_proj, c_proj, inputs, halo)

    grad_rows, tail, edge = call(
        functools.partial(gradient_kernel, parts),
        [vmem] * (5 + parts),
        [vmem] * 3,
        [narrow, shape((8, channels), F32), shape((16, channels), F32)],
        [pltpu.VMEM((rows + 16, channels), BF16), pltpu.VMEM((rows, channels), F32)],
        2,
    )(conv_weight, grad_base, grad_weight, tap_base, tap_weight, b_proj, *pays)
    tails = [rotated(tail, "seq", distance) for distance in range(1, parts)]

    layer_out, grad_rows = call(
        functools.partial(output_kernel, heads, parts),
        [vmem] * (3 + parts),
        [hbm, hbm],
        [narrow, narrow],
        [pltpu.VMEM((rows, channels), BF16), dma((pieces,)), dma],
        2,
    )(front, base, c_proj, grad_rows, *pays)

    scale = float((rows * parts) ** -0.5)
    input_grad, conv_grad = call(
        functools.partial(finish_kernel, parts, scale),
        [vmem] * (2 + parts) + [hbm],
        [hbm, vmem],
        [narrow, shape((4, channels), F32)],
        [pltpu.VMEM((16, channels), BF16), dma],
        0,
        {parts + 2: 0},
    )(conv_weight, tail, edge, *tails, grad_rows)
    return layer_out, input_grad, conv_grad


def solution(mesh):
    in_specs = (
        P(("groups", "seq"), ("head", "sub")),
        P(("groups", "seq"), None),
        P(("groups", "seq"), None),
        P(("head", "sub"), ("groups", "seq")),
        P(("groups", "seq")),
        P(("head", "sub")),
        P(("head", "sub")),
        P(None, ("head", "sub")),
        P(("groups", "seq"), ("head", "sub")),
    )
    out_specs = (
        P(("groups", "seq"), ("head", "sub")),
        P(("groups", "seq"), ("head", "sub")),
        P("groups", ("head", "sub")),
    )
    return jax.shard_map(shards, mesh=mesh, in_specs=in_specs, out_specs=out_specs, check_vma=False)
```

```python
import functools

import jax
import jax.numpy as jnp
from jax import lax
from jax.experimental import pallas as pl
from jax.experimental.pallas import tpu as pltpu
from jax.sharding import PartitionSpec as P

CHUNK = 128
STATE = 128
STEP_ROWS = 512
LOG_ONE = -0.2876820724517809
LOG_TWO = -0.6931471805599453
F32 = jnp.float32
BF16 = jnp.bfloat16
HIGHEST = lax.Precision.HIGHEST
VMEM_LIMIT = 20 * 1024 * 1024


def dot(a, b, dims, precision=None):
    return lax.dot_general(a, b, (dims, ((), ())), preferred_element_type=F32, precision=precision)


def per_lane(scalars, count, channels):
    width = channels // count
    lane = lax.broadcasted_iota(jnp.int32, (1, channels), 1)
    row = jnp.zeros((1, channels), F32)
    for head in range(count):
        inside = (lane >= head * width) & (lane < (head + 1) * width)
        row = jnp.where(inside, scalars[head], row)
    return row


def split_two(value):
    high = value.astype(BF16)
    low = (value - high.astype(F32)).astype(BF16)
    return jnp.concatenate([high.astype(F32), low.astype(F32)], axis=0).astype(BF16)


def spread_matrix(count, channels):
    width = channels // count
    row = lax.broadcasted_iota(jnp.int32, (16, channels), 0)
    lane = lax.broadcasted_iota(jnp.int32, (16, channels), 1)
    return jnp.where((row % 8) == lane // width, 1.0, 0.0).astype(BF16)


def spread(pair, onehot):
    return dot(pair, onehot, ((0,), (0,)))


def reduce_kernel(
    heads, parts, rates_hbm, codes_hbm, gates_hbm, taps_hbm, inputs_hbm, b_hbm, grad_hbm, c_hbm,
    near_out, far_out, front_out, logs_out, lead_out, mixed_out, sigma_out,
    inputs, b_proj, grad, c_proj, *rest
):
    pays = rest[: parts - 1]
    rates, codes, gates, taps, steps, scaled, lead_pair, extra, sems = rest[parts - 1 :]
    rows, channels = grad.shape
    chunks = rows // CHUNK
    sources = (rates_hbm, codes_hbm, gates_hbm, taps_hbm, inputs_hbm, b_hbm, grad_hbm, c_hbm)
    targets = (rates, codes, gates, taps, inputs, b_proj, grad, c_proj)
    copies = [
        pltpu.make_async_copy(source, target, sems.at[i])
        for i, (source, target) in enumerate(zip(sources, targets))
    ]
    for copy in copies:
        copy.start()
    for copy in copies[:3]:
        copy.wait()

    steps[...] = jnp.zeros_like(steps)
    steps[0:heads, :] = jnp.exp2(-codes[...].astype(F32))
    gate = gates[...]
    steps[6:7, :] = jnp.where(gate == 1, 1.0, 0.0).astype(F32)
    steps[7:8, :] = jnp.where(gate == 2, 1.0, 0.0).astype(F32)
    stacked = jnp.concatenate(
        [steps[:, j * CHUNK : (j + 1) * CHUNK] for j in range(chunks)], axis=0
    ).astype(BF16)
    row = lax.broadcasted_iota(jnp.int32, (CHUNK, CHUNK), 0)
    col = lax.broadcasted_iota(jnp.int32, (CHUNK, CHUNK), 1)
    upper = jnp.where(row <= col, 1.0, 0.0).astype(BF16)
    sums = dot(stacked, upper, ((1,), (0,)))
    sub = lax.broadcasted_iota(jnp.int32, (8, CHUNK), 0)
    rate = jnp.zeros((8, CHUNK), F32)
    for head in range(heads):
        rate = jnp.where(sub == head, rates[head], rate)
    cums, mids, befores = [], [], []
    before = jnp.zeros((8, 1), F32)
    for j in range(chunks):
        part = sums[8 * j : 8 * j + 8, :]
        cum = LOG_ONE * part[6:7, :] + LOG_TWO * part[7:8, :] - rate * part
        cums.append(cum)
        mids.append(cum[:, CHUNK // 2 - 1 : CHUNK // 2])
        befores.append(before)
        before = before + cum[:, CHUNK - 1 : CHUNK]
    for j in range(chunks):
        at = slice(j * CHUNK, (j + 1) * CHUNK)
        size = steps[:, at]
        near_out[0:16, at] = split_two(jnp.exp(cums[j] - mids[j]))
        near_out[16:32, at] = split_two(jnp.exp(mids[j] - cums[j]) * size)
        front_out[:, at] = split_two(jnp.exp(befores[j] + cums[j]))
        far_out[:, at] = split_two(jnp.exp(before - befores[j] - cums[j]) * size)
    lead_pair[...] = split_two(jnp.exp(-jnp.maximum(cums[0], -8.0)) * steps[:, 0:CHUNK])
    pick = lax.broadcasted_iota(jnp.int32, (8, CHUNK), 0)
    place = lax.broadcasted_iota(jnp.int32, (8, CHUNK), 1)
    chosen = jnp.where((pick == 0) | ((pick == 1) & (place < CHUNK // 2)), 1.0, 0.0)
    flat = dot(chosen.astype(BF16), stacked, ((1,), (1,)))
    owner = lax.broadcasted_iota(jnp.int32, (chunks, 8 * chunks), 1) // 8
    chunk_at = lax.broadcasted_iota(jnp.int32, (chunks, 8 * chunks), 0)
    lane_rate = per_lane(rates, heads, channels)
    kind = lax.broadcasted_iota(jnp.int32, (8 * chunks, channels), 0) % 8
    lane_head = lax.broadcasted_iota(jnp.int32, (8 * chunks, channels), 1) // (channels // heads)
    mixer = jnp.where(kind == lane_head, -lane_rate, 0.0)
    mixer = jnp.where(kind == 6, LOG_ONE, jnp.where(kind == 7, LOG_TWO, mixer))
    table = []
    for which in range(2):
        own = jnp.where(owner == chunk_at, flat[which : which + 1, :], 0.0)
        table.append(dot(own, mixer, ((1,), (0,)), HIGHEST))
    whole = jnp.exp(table[0])
    middle = jnp.exp(table[1])
    rest_of = jnp.exp(table[0] - table[1])
    logs_out[0] = whole
    logs_out[1] = middle
    logs_out[2] = rest_of
    decay = jnp.exp(jnp.sum(table[0], axis=0, keepdims=True))
    first = decay.astype(BF16).astype(F32)
    extra[...] = jnp.zeros_like(extra)
    extra[0:1, :] = first
    extra[1:2, :] = decay - first

    onehot = spread_matrix(heads, channels)
    lead_out[...] = spread(lead_pair[:, 0:16], onehot)
    for copy in copies[3:6]:
        copy.wait()
    shift = back_shift()
    nothing = jnp.zeros((16, channels), BF16)
    for at in range(0, rows, CHUNK):
        both = slice(at, at + CHUNK)
        if at == 0:
            block = jnp.concatenate([nothing, inputs[both, :]], axis=0)
        else:
            block = inputs[at - 16 : at + CHUNK, :]
        moved = dot(shift, block, ((1,), (0,)))
        preact = taps[3:4, :] * inputs[both, :].astype(F32)
        for k in range(3):
            preact = preact + taps[k : k + 1, :] * moved[k * CHUNK : (k + 1) * CHUNK, :]
        sigma = 0.5 * jnp.tanh(0.5 * preact) + 0.5
        mixed = preact * sigma
        scale = spread(far_out[:, both], onehot)
        sigma_out[both, :] = sigma
        mixed_out[both, :] = mixed
        scaled[both, :] = (mixed * scale).astype(BF16)
        if at == 0:
            extra[11:14, :] = scale[0:3, :]
    state = dot(b_proj[...], scaled[...], ((0,), (0,))).astype(BF16)
    extra[2:5, :] = inputs[0:16, :].astype(F32)[0:3, :]
    extra[5:8, :] = inputs[rows - 16 : rows, :].astype(F32)[13:16, :]
    extra[8:11, 0:STATE] = b_proj[0:16, :].astype(F32)[0:3, :]
    for copy in copies[6:]:
        copy.wait()
    for at in range(0, rows, STEP_ROWS):
        both = slice(at, at + STEP_ROWS)
        scale = spread(front_out[:, both], onehot)
        scaled[both, :] = (grad[both, :].astype(F32) * scale).astype(BF16)
    adjoint = dot(c_proj[...], scaled[...], ((0,), (0,))).astype(BF16)
    me = lax.axis_index("seq")
    for distance in range(1, parts):
        pay = pays[distance - 1]
        pay[0:STATE, :] = jnp.where(me + distance < parts, state, adjoint)
        pay[STATE : STATE + 16, :] = extra[...].astype(BF16)


def back_shift():
    row = lax.broadcasted_iota(jnp.int32, (3 * CHUNK, CHUNK + 16), 0)
    col = lax.broadcasted_iota(jnp.int32, (3 * CHUNK, CHUNK + 16), 1)
    return jnp.where(col == row % CHUNK + 13 + row // CHUNK, 1.0, 0.0).astype(BF16)


def tail_rows(pay):
    return pay[STATE : STATE + 16, :].astype(F32)


def first_preact(taps, halo, first):
    joined = jnp.concatenate([halo[0:3, :], first[0:8, :]], axis=0)
    preact = taps[0:1, :] * joined[0:8, :]
    for k in range(1, 4):
        preact = preact + taps[k : k + 1, :] * joined[k : k + 8, :]
    return preact


def first_change(taps, halo, first):
    true = first_preact(taps, halo, first)
    bare = first_preact(taps, jnp.zeros_like(halo), first)
    change = true * (0.5 * jnp.tanh(0.5 * true) + 0.5) - bare * (0.5 * jnp.tanh(0.5 * bare) + 0.5)
    row = lax.broadcasted_iota(jnp.int32, change.shape, 0)
    change = jnp.where(row < 3, change, 0.0)
    return jnp.concatenate([change, jnp.zeros_like(change)], axis=0)


def lane_tiles(channels):
    return [slice(at, min(at + 128, channels)) for at in range(0, channels, 128)]


def merged_adjoint(parts, pays):
    me = lax.axis_index("seq")
    running = jnp.zeros((STATE, pays[0].shape[1]), F32)
    for distance in range(parts - 1, 0, -1):
        held = pays[parts - distance - 1]
        tail = tail_rows(held)
        decay = tail[0:1, :] + tail[1:2, :]
        there = me + distance < parts
        running = jnp.where(there, held[0:STATE, :].astype(F32) + decay * running, 0.0)
    return running.astype(BF16)


def own_halo(pays):
    return jnp.where(lax.axis_index("seq") > 0, tail_rows(pays[0])[5:8, :], 0.0)


def merged_state(parts, taps, pays):
    me = lax.axis_index("seq")
    channels = pays[0].shape[1]
    running = jnp.zeros((STATE, channels), F32)
    tails = [tail_rows(pay) for pay in pays]
    blank = jnp.zeros((5, channels), F32)
    for distance in range(parts - 1, 0, -1):
        held = pays[distance - 1]
        tail = tails[distance - 1]
        state = held[0:STATE, :].astype(F32)
        if distance < parts - 1:
            halo = jnp.where(me > distance, tails[distance][5:8, :], 0.0)
            first = jnp.concatenate([tail[2:5, :], blank], axis=0)
            scale = jnp.concatenate([tail[11:14, :], blank, blank, blank[0:3, :]], axis=0)
            change = (first_change(taps, halo, first) * scale).astype(BF16)
            row = lax.broadcasted_iota(jnp.int32, (16, STATE), 0)
            lines = jnp.concatenate([tail[8:11, 0:STATE], blank[:, 0:STATE]], axis=0)
            lines = jnp.concatenate([lines, jnp.zeros_like(lines)], axis=0)
            lines = jnp.where(row < 3, lines, 0.0).astype(BF16)
            state = state + dot(lines, change, ((0,), (0,)))
        decay = tail[0:1, :] + tail[1:2, :]
        running = jnp.where(me >= distance, state + decay * running, 0.0)
    return running


def inner_kernel(
    heads, gains, near, far, logs, grad, mixed, sigma, b_proj, c_proj,
    base_out, grad_base, grad_weight, first_out,
    ahead_scores, behind_scores, mixed_scaled, mixed_low, grad_scaled, grad_low,
    mixed_fresh, grad_fresh,
):
    rows, channels = grad.shape
    chunks = rows // CHUNK
    blocks = [slice(j * CHUNK, (j + 1) * CHUNK) for j in range(chunks)]
    row = lax.broadcasted_iota(jnp.int32, (CHUNK, CHUNK), 0)
    col = lax.broadcasted_iota(jnp.int32, (CHUNK, CHUNK), 1)
    onehot = spread_matrix(heads, channels)
    gain = per_lane(gains, heads, channels)
    for both in blocks:
        scale = spread(near[0:16, both], onehot)
        grad_scaled[both, :] = (grad[both, :].astype(F32) * scale).astype(BF16)
    for both in blocks:
        scale = spread(near[16:32, both], onehot)
        mixed_scaled[both, :] = (mixed[both, :] * scale).astype(BF16)
    for both in blocks:
        grad_fresh[both, :] = dot(c_proj[both, :], grad_scaled[both, :], ((0,), (0,)))
    for both in blocks:
        mixed_fresh[both, :] = dot(b_proj[both, :], mixed_scaled[both, :], ((0,), (0,)))
    for both in blocks:
        ahead = dot(c_proj[both, :], b_proj[both, :], ((1,), (1,)))
        ahead_scores[both, :] = jnp.where(row >= col, ahead, 0.0).astype(BF16)
    for both in blocks:
        behind = dot(b_proj[both, :], c_proj[both, :], ((1,), (1,)))
        behind_scores[both, :] = jnp.where(row <= col, behind, 0.0).astype(BF16)
    for lanes in lane_tiles(channels):
        adjoint = jnp.zeros((STATE, lanes.stop - lanes.start), F32)
        for j in range(chunks - 1, -1, -1):
            grad_low[blocks[j], lanes] = (adjoint * logs[2, j : j + 1, lanes]).astype(BF16)
            adjoint = logs[0, j : j + 1, lanes] * adjoint + (
                logs[1, j : j + 1, lanes] * grad_fresh[blocks[j], lanes]
            )
        state = jnp.zeros((STATE, lanes.stop - lanes.start), F32)
        for j in range(chunks):
            mixed_low[blocks[j], lanes] = (state * logs[1, j : j + 1, lanes]).astype(BF16)
            state = logs[0, j : j + 1, lanes] * state + (
                logs[2, j : j + 1, lanes] * mixed_fresh[blocks[j], lanes]
            )
    for both in blocks:
        inner = dot(
            jnp.concatenate([behind_scores[both, :], b_proj[both, :]], axis=1),
            jnp.concatenate([grad_scaled[both, :], grad_low[both, :]], axis=0),
            ((1,), (0,)),
        )
        slope = sigma[both, :] + mixed[both, :] * (1.0 - sigma[both, :])
        inner = gain * grad[both, :].astype(F32) + spread(near[16:32, both], onehot) * inner
        weight = spread(far[:, both], onehot)
        grad_base[both, :] = slope * inner
        grad_weight[both, :] = slope * weight
        if both.start == 0:
            first_out[0:8, :] = inner[0:8, :]
            first_out[8:16, :] = weight[0:8, :]
    for both in blocks:
        inner = dot(
            jnp.concatenate([ahead_scores[both, :], c_proj[both, :]], axis=1),
            jnp.concatenate([mixed_scaled[both, :], mixed_low[both, :]], axis=0),
            ((1,), (0,)),
        )
        base_out[both, :] = gain * mixed[both, :] + spread(near[0:16, both], onehot) * inner


def gradient_kernel(parts, taps, base, weight, unscaled, inputs, b_proj, *rest):
    pays = rest[: parts - 1]
    grad_out, tail_out, edge_out, window, exact = rest[parts - 1 :]
    rows, channels = base.shape
    chunks = rows // CHUNK
    adjoint = merged_adjoint(parts, pays)
    halo = own_halo(pays)
    preact = first_preact(taps, halo, inputs[0:16, :].astype(F32))
    sigma = 0.5 * jnp.tanh(0.5 * preact) + 0.5
    slope = sigma + preact * sigma * (1.0 - sigma)
    window[rows : rows + 16, :] = jnp.zeros((16, channels), BF16)
    row = lax.broadcasted_iota(jnp.int32, (3 * CHUNK, CHUNK + 16), 0)
    col = lax.broadcasted_iota(jnp.int32, (3 * CHUNK, CHUNK + 16), 1)
    shift = jnp.where(col == row % CHUNK + 3 - row // CHUNK, 1.0, 0.0).astype(BF16)
    partial = [jnp.zeros((8, channels), F32) for _ in range(4)]
    for j in range(chunks):
        both = slice(j * CHUNK, (j + 1) * CHUNK)
        carried = dot(b_proj[both, :], adjoint, ((1,), (0,)))
        grad_pre = base[both, :] + weight[both, :] * carried
        if j == 0:
            first = slope * (unscaled[0:8, :] + unscaled[8:16, :] * carried[0:8, :])
            grad_pre = jnp.concatenate([first, grad_pre[8:, :]], axis=0)
        window[both, :] = grad_pre.astype(BF16)
        exact[both, :] = grad_pre
    for j in range(chunks):
        at = j * CHUNK
        both = slice(at, at + CHUNK)
        grad_pre = exact[both, :]
        moved = dot(shift, window[at : at + CHUNK + 16, :], ((1,), (0,)))
        x = inputs[both, :].astype(F32)
        result = taps[3:4, :] * grad_pre
        partial[3] = partial[3] + (grad_pre * x).reshape(CHUNK // 8, 8, channels).sum(axis=0)
        for k in range(3):
            part = moved[k * CHUNK : (k + 1) * CHUNK, :]
            result = result + taps[k : k + 1, :] * part
            partial[k] = partial[k] + (part * x).reshape(CHUNK // 8, 8, channels).sum(axis=0)
        grad_out[both, :] = result.astype(BF16)
        if j == chunks - 1:
            edge_out[...] = result[CHUNK - 16 :, :]
    for k in range(4):
        tap = jnp.sum(partial[k], axis=0, keepdims=True)
        for j in range(k, 3):
            tap = tap + first[j - k : j - k + 1, :] * halo[j : j + 1, :]
        tail_out[k : k + 1, :] = tap
    tail_out[4:7, :] = first[0:3, :]
    tail_out[7:8, :] = jnp.zeros((1, channels), F32)


def output_kernel(
    heads, parts, gains, taps, front, lead, base, inputs, b_proj, c_proj, grad_rows, *rest
):
    pays = rest[: parts - 1]
    out_hbm, grad_hbm, result_rows, sems, grad_sem = rest[parts - 1 :]
    rows, channels = base.shape
    grad_copy = pltpu.make_async_copy(grad_rows, grad_hbm, grad_sem)
    grad_copy.start()
    incoming = merged_state(parts, taps, pays)
    onehot = spread_matrix(heads, channels)
    change = first_change(taps, own_halo(pays), inputs[0:16, :].astype(F32))
    change_scaled = (change * lead[...]).astype(BF16)
    state = incoming + dot(b_proj[0:16, :], change_scaled, ((0,), (0,)))
    state = state.astype(BF16)
    row = lax.broadcasted_iota(jnp.int32, (16, 16), 0)
    col = lax.broadcasted_iota(jnp.int32, (16, 16), 1)
    scores = dot(c_proj[0:16, :], b_proj[0:16, :], ((1,), (1,)))
    scores = jnp.where(row >= col, scores, 0.0).astype(BF16)
    top = dot(c_proj[0:16, :], incoming.astype(BF16), ((1,), (0,)))
    top = top + dot(scores, change_scaled, ((1,), (0,)))
    top = top * spread(front[:, 0:16], onehot) + base[0:16, :]
    top = top + per_lane(gains, heads, channels) * change
    copies = []
    for piece in range(rows // STEP_ROWS):
        for at in range(piece * STEP_ROWS, (piece + 1) * STEP_ROWS, CHUNK):
            both = slice(at, at + CHUNK)
            carried = dot(c_proj[both, :], state, ((1,), (0,)))
            result = base[both, :] + spread(front[:, both], onehot) * carried
            result_rows[both, :] = result.astype(BF16)
            if at == 0:
                result_rows[0:16, :] = top.astype(BF16)
        place = pl.ds(piece * STEP_ROWS, STEP_ROWS)
        copy = pltpu.make_async_copy(result_rows.at[place], out_hbm.at[place], sems.at[piece])
        copy.start()
        copies.append(copy)
    for copy in copies:
        copy.wait()
    grad_copy.wait()


def finish_kernel(parts, scale, taps, tail, edge, *rest):
    others = rest[: parts - 1]
    unused, grad_hbm, conv_out, rows_low, sem = rest[parts - 1 :]
    channels = tail.shape[1]
    me = lax.axis_index("seq")
    after = jnp.where(me + 1 < parts, others[parts - 2][...], 0.0)
    row = lax.broadcasted_iota(jnp.int32, (16, channels), 0)
    result = edge[...]
    for r in range(3):
        extra = jnp.zeros((1, channels), F32)
        for k in range(r + 1):
            extra = extra + taps[k : k + 1, :] * after[4 + r - k : 5 + r - k, :]
        result = jnp.where(row == 13 + r, result + extra, result)
    rows_low[...] = result.astype(BF16)
    rows = grad_hbm.shape[0]
    copy = pltpu.make_async_copy(rows_low, grad_hbm.at[pl.ds(rows - 16, 16)], sem)
    copy.start()
    total = tail[0:4, :]
    for other in others:
        total = total + other[0:4, :]
    conv_out[...] = total * scale
    copy.wait()


def rotated(block, axis, distance):
    size = lax.axis_size(axis)
    return lax.ppermute(block, axis, [(i, (i + distance) % size) for i in range(size)])


def shards(
    inputs,
    b_proj,
    c_proj,
    step_codes,
    gate_codes,
    decay_rates,
    skip_gain,
    conv_weight,
    out_cotangent,
):
    rows, channels = inputs.shape
    heads = decay_rates.shape[0]
    parts = lax.axis_size("seq")
    chunks = rows // CHUNK
    pieces = rows // STEP_ROWS
    hbm = pl.BlockSpec(memory_space=pltpu.HBM)
    vmem = pl.BlockSpec(memory_space=pltpu.VMEM)
    smem = pl.BlockSpec(memory_space=pltpu.SMEM)
    shape = jax.ShapeDtypeStruct
    dma = pltpu.SemaphoreType.DMA
    big = rows * channels

    def call(kernel, in_specs, out_specs, out_shape, scratch, products, aliases=None):
        return pl.pallas_call(
            kernel,
            in_specs=in_specs,
            out_specs=out_specs,
            out_shape=out_shape,
            scratch_shapes=scratch,
            input_output_aliases=aliases or {},
            compiler_params=pltpu.CompilerParams(vmem_limit_bytes=VMEM_LIMIT),
            cost_estimate=pl.CostEstimate(
                flops=products * 2 * big * 128, bytes_accessed=6 * big, transcendentals=big
            ),
        )

    def stay(array):
        return pltpu.with_memory_space_constraint(array, pltpu.HBM)

    pay = shape((STATE + 16, channels), BF16)
    narrow = shape((rows, channels), BF16)
    broad = shape((rows, channels), F32)
    slim = shape((rows, STATE), BF16)

    outs = call(
        functools.partial(reduce_kernel, heads, parts),
        [hbm] * 8,
        [vmem] * (10 + parts),
        [
            shape((32, rows), BF16),
            shape((16, rows), BF16),
            shape((16, rows), BF16),
            shape((3, chunks, channels), F32),
            shape((16, channels), F32),
            broad,
            broad,
            narrow,
            slim,
            narrow,
            slim,
        ]
        + [pay] * (parts - 1),
        [
            pltpu.SMEM((heads,), F32),
            pltpu.VMEM((heads, rows), jnp.int32),
            pltpu.VMEM((1, rows), jnp.int32),
            pltpu.VMEM((4, channels), F32),
            pltpu.VMEM((8, rows), F32),
            pltpu.VMEM((rows, channels), BF16),
            pltpu.VMEM((16, CHUNK), BF16),
            pltpu.VMEM((16, channels), F32),
            dma((8,)),
        ],
        4,
    )(
        stay(decay_rates),
        stay(step_codes),
        stay(gate_codes.reshape(1, rows)),
        stay(conv_weight),
        stay(inputs),
        stay(b_proj),
        stay(out_cotangent),
        stay(c_proj),
    )
    near, far, front, logs, lead, mixed, sigma = outs[:7]
    inputs, b_proj, out_cotangent, c_proj = outs[7:11]
    pays = [rotated(send, "seq", distance + 1) for distance, send in enumerate(outs[11:])]

    tile = pltpu.VMEM((rows, CHUNK), BF16)
    low = pltpu.VMEM((rows, channels), BF16)
    high = pltpu.VMEM((rows, channels), F32)
    base, grad_base, grad_weight, unscaled = call(
        functools.partial(inner_kernel, heads),
        [smem] + [vmem] * 8,
        [vmem] * 4,
        [broad] * 3 + [shape((16, channels), F32)],
        [tile, tile, low, low, low, low, high, high],
        10,
    )(skip_gain, near, far, logs, out_cotangent, mixed, sigma, b_proj, c_proj)

    grad_rows, tail, edge = call(
        functools.partial(gradient_kernel, parts),
        [vmem] * (5 + parts),
        [vmem] * 3,
        [narrow, shape((8, channels), F32), shape((16, channels), F32)],
        [pltpu.VMEM((rows + 16, channels), BF16), pltpu.VMEM((rows, channels), F32)],
        2,
    )(conv_weight, grad_base, grad_weight, unscaled, inputs, b_proj, *pays)
    tails = [rotated(tail, "seq", distance) for distance in range(1, parts)]

    layer_out, grad_rows = call(
        functools.partial(output_kernel, heads, parts),
        [smem] + [vmem] * (7 + parts),
        [hbm, hbm],
        [narrow, narrow],
        [pltpu.VMEM((rows, channels), BF16), dma((pieces,)), dma],
        2,
    )(skip_gain, conv_weight, front, lead, base, inputs, b_proj, c_proj, grad_rows, *pays)

    scale = float((rows * parts) ** -0.5)
    input_grad, conv_grad = call(
        functools.partial(finish_kernel, parts, scale),
        [vmem] * (2 + parts) + [hbm],
        [hbm, vmem],
        [narrow, shape((4, channels), F32)],
        [pltpu.VMEM((16, channels), BF16), dma],
        0,
        {parts + 2: 0},
    )(conv_weight, tail, edge, *tails, grad_rows)
    return layer_out, input_grad, conv_grad


def solution(mesh):
    in_specs = (
        P(("groups", "seq"), ("head", "sub")),
        P(("groups", "seq"), None),
        P(("groups", "seq"), None),
        P(("head", "sub"), ("groups", "seq")),
        P(("groups", "seq")),
        P(("head", "sub")),
        P(("head", "sub")),
        P(None, ("head", "sub")),
        P(("groups", "seq"), ("head", "sub")),
    )
    out_specs = (
        P(("groups", "seq"), ("head", "sub")),
        P(("groups", "seq"), ("head", "sub")),
        P("groups", ("head", "sub")),
    )
    return jax.shard_map(shards, mesh=mesh, in_specs=in_specs, out_specs=out_specs, check_vma=False)
```

```python
import functools

import jax
import jax.numpy as jnp
from jax import lax
from jax.experimental import pallas as pl
from jax.experimental.pallas import tpu as pltpu
from jax.sharding import PartitionSpec as P

CHUNK = 128
STATE = 128
STEP_ROWS = 512
LOG_ONE = -0.2876820724517809
LOG_TWO = -0.6931471805599453
F32 = jnp.float32
BF16 = jnp.bfloat16
HIGHEST = lax.Precision.HIGHEST
VMEM_LIMIT = 20 * 1024 * 1024


def dot(a, b, dims, precision=None):
    return lax.dot_general(a, b, (dims, ((), ())), preferred_element_type=F32, precision=precision)


def per_lane(scalars, count, channels):
    width = channels // count
    lane = lax.broadcasted_iota(jnp.int32, (1, channels), 1)
    row = jnp.zeros((1, channels), F32)
    for head in range(count):
        inside = (lane >= head * width) & (lane < (head + 1) * width)
        row = jnp.where(inside, scalars[head], row)
    return row


def split_two(value):
    high = value.astype(BF16)
    low = (value - high.astype(F32)).astype(BF16)
    return jnp.concatenate([high.astype(F32), low.astype(F32)], axis=0).astype(BF16)


def spread_matrix(count, channels):
    width = channels // count
    row = lax.broadcasted_iota(jnp.int32, (16, channels), 0)
    lane = lax.broadcasted_iota(jnp.int32, (16, channels), 1)
    return jnp.where((row % 8) == lane // width, 1.0, 0.0).astype(BF16)


def spread(pair, onehot):
    return dot(pair, onehot, ((0,), (0,)))


def reduce_kernel(
    heads, parts,
    rates_hbm, gains_hbm, codes_hbm, gates_hbm, taps_hbm, inputs_hbm, b_hbm, grad_hbm, c_hbm,
    near_out, far_out, front_out, logs_out, lead_out, gain_out, mixed_out, sigma_out,
    inputs, b_proj, grad, c_proj, *rest
):
    pays = rest[: parts - 1]
    rates, gains, codes, gates, taps, steps, scaled, lead_pair, extra, sems = rest[parts - 1 :]
    rows, channels = grad.shape
    chunks = rows // CHUNK
    sources = (
        rates_hbm, gains_hbm, codes_hbm, gates_hbm, taps_hbm, inputs_hbm, b_hbm, grad_hbm, c_hbm
    )
    targets = (rates, gains, codes, gates, taps, inputs, b_proj, grad, c_proj)
    copies = [
        pltpu.make_async_copy(source, target, sems.at[i])
        for i, (source, target) in enumerate(zip(sources, targets))
    ]
    for copy in copies:
        copy.start()
    for copy in copies[:4]:
        copy.wait()

    steps[...] = jnp.zeros_like(steps)
    steps[0:heads, :] = jnp.exp2(-codes[...].astype(F32))
    gate = gates[...]
    steps[6:7, :] = jnp.where(gate == 1, 1.0, 0.0).astype(F32)
    steps[7:8, :] = jnp.where(gate == 2, 1.0, 0.0).astype(F32)
    stacked = jnp.concatenate(
        [steps[:, j * CHUNK : (j + 1) * CHUNK] for j in range(chunks)], axis=0
    ).astype(BF16)
    row = lax.broadcasted_iota(jnp.int32, (CHUNK, CHUNK), 0)
    col = lax.broadcasted_iota(jnp.int32, (CHUNK, CHUNK), 1)
    upper = jnp.where(row <= col, 1.0, 0.0).astype(BF16)
    sums = dot(stacked, upper, ((1,), (0,)))
    sub = lax.broadcasted_iota(jnp.int32, (8, CHUNK), 0)
    rate = jnp.zeros((8, CHUNK), F32)
    for head in range(heads):
        rate = jnp.where(sub == head, rates[head], rate)
    cums, mids, befores = [], [], []
    before = jnp.zeros((8, 1), F32)
    for j in range(chunks):
        part = sums[8 * j : 8 * j + 8, :]
        cum = LOG_ONE * part[6:7, :] + LOG_TWO * part[7:8, :] - rate * part
        cums.append(cum)
        mids.append(cum[:, CHUNK // 2 - 1 : CHUNK // 2])
        befores.append(before)
        before = before + cum[:, CHUNK - 1 : CHUNK]
    for j in range(chunks):
        at = slice(j * CHUNK, (j + 1) * CHUNK)
        size = steps[:, at]
        near_out[0:16, at] = split_two(jnp.exp(cums[j] - mids[j]))
        near_out[16:32, at] = split_two(jnp.exp(mids[j] - cums[j]) * size)
        front_out[:, at] = split_two(jnp.exp(befores[j] + cums[j]))
        far_out[:, at] = split_two(jnp.exp(before - befores[j] - cums[j]) * size)
    lead_pair[...] = split_two(jnp.exp(-jnp.maximum(cums[0], -8.0)) * steps[:, 0:CHUNK])
    pick = lax.broadcasted_iota(jnp.int32, (8, CHUNK), 0)
    place = lax.broadcasted_iota(jnp.int32, (8, CHUNK), 1)
    chosen = jnp.where((pick == 0) | ((pick == 1) & (place < CHUNK // 2)), 1.0, 0.0)
    flat = dot(chosen.astype(BF16), stacked, ((1,), (1,)))
    owner = lax.broadcasted_iota(jnp.int32, (chunks, 8 * chunks), 1) // 8
    chunk_at = lax.broadcasted_iota(jnp.int32, (chunks, 8 * chunks), 0)
    lane_rate = per_lane(rates, heads, channels)
    kind = lax.broadcasted_iota(jnp.int32, (8 * chunks, channels), 0) % 8
    lane_head = lax.broadcasted_iota(jnp.int32, (8 * chunks, channels), 1) // (channels // heads)
    mixer = jnp.where(kind == lane_head, -lane_rate, 0.0)
    mixer = jnp.where(kind == 6, LOG_ONE, jnp.where(kind == 7, LOG_TWO, mixer))
    table = []
    for which in range(2):
        own = jnp.where(owner == chunk_at, flat[which : which + 1, :], 0.0)
        table.append(dot(own, mixer, ((1,), (0,)), HIGHEST))
    whole = jnp.exp(table[0])
    middle = jnp.exp(table[1])
    rest_of = jnp.exp(table[0] - table[1])
    logs_out[0] = whole
    logs_out[1] = middle
    logs_out[2] = rest_of
    decay = jnp.exp(jnp.sum(table[0], axis=0, keepdims=True))
    first = decay.astype(BF16).astype(F32)
    extra[...] = jnp.zeros_like(extra)
    extra[0:1, :] = first
    extra[1:2, :] = decay - first

    onehot = spread_matrix(heads, channels)
    lead_out[...] = spread(lead_pair[:, 0:16], onehot)
    gain_out[...] = jnp.broadcast_to(per_lane(gains, heads, channels), (8, channels))
    for copy in copies[4:7]:
        copy.wait()
    shift = back_shift()
    nothing = jnp.zeros((16, channels), BF16)
    for at in range(0, rows, CHUNK):
        both = slice(at, at + CHUNK)
        if at == 0:
            block = jnp.concatenate([nothing, inputs[both, :]], axis=0)
        else:
            block = inputs[at - 16 : at + CHUNK, :]
        moved = dot(shift, block, ((1,), (0,)))
        preact = taps[3:4, :] * inputs[both, :].astype(F32)
        for k in range(3):
            preact = preact + taps[k : k + 1, :] * moved[k * CHUNK : (k + 1) * CHUNK, :]
        sigma = 0.5 * jnp.tanh(0.5 * preact) + 0.5
        mixed = preact * sigma
        scale = spread(far_out[:, both], onehot)
        sigma_out[both, :] = sigma
        mixed_out[both, :] = mixed
        scaled[both, :] = (mixed * scale).astype(BF16)
        if at == 0:
            extra[11:14, :] = scale[0:3, :]
    state = dot(b_proj[...], scaled[...], ((0,), (0,))).astype(BF16)
    extra[2:5, :] = inputs[0:16, :].astype(F32)[0:3, :]
    extra[5:8, :] = inputs[rows - 16 : rows, :].astype(F32)[13:16, :]
    extra[8:11, 0:STATE] = b_proj[0:16, :].astype(F32)[0:3, :]
    for copy in copies[7:]:
        copy.wait()
    for at in range(0, rows, STEP_ROWS):
        both = slice(at, at + STEP_ROWS)
        scale = spread(front_out[:, both], onehot)
        scaled[both, :] = (grad[both, :].astype(F32) * scale).astype(BF16)
    adjoint = dot(c_proj[...], scaled[...], ((0,), (0,))).astype(BF16)
    me = lax.axis_index("seq")
    for distance in range(1, parts):
        pay = pays[distance - 1]
        pay[0:STATE, :] = jnp.where(me + distance < parts, state, adjoint)
        pay[STATE : STATE + 16, :] = extra[...].astype(BF16)


def back_shift():
    row = lax.broadcasted_iota(jnp.int32, (3 * CHUNK, CHUNK + 16), 0)
    col = lax.broadcasted_iota(jnp.int32, (3 * CHUNK, CHUNK + 16), 1)
    return jnp.where(col == row % CHUNK + 13 + row // CHUNK, 1.0, 0.0).astype(BF16)


def tail_rows(pay):
    return pay[STATE : STATE + 16, :].astype(F32)


def first_preact(taps, halo, first):
    joined = jnp.concatenate([halo[0:3, :], first[0:8, :]], axis=0)
    preact = taps[0:1, :] * joined[0:8, :]
    for k in range(1, 4):
        preact = preact + taps[k : k + 1, :] * joined[k : k + 8, :]
    return preact


def first_change(taps, halo, first):
    true = first_preact(taps, halo, first)
    bare = first_preact(taps, jnp.zeros_like(halo), first)
    change = true * (0.5 * jnp.tanh(0.5 * true) + 0.5) - bare * (0.5 * jnp.tanh(0.5 * bare) + 0.5)
    row = lax.broadcasted_iota(jnp.int32, change.shape, 0)
    change = jnp.where(row < 3, change, 0.0)
    return jnp.concatenate([change, jnp.zeros_like(change)], axis=0)


def lane_tiles(channels):
    return [slice(at, min(at + 128, channels)) for at in range(0, channels, 128)]


def merged_adjoint(parts, pays):
    me = lax.axis_index("seq")
    running = jnp.zeros((STATE, pays[0].shape[1]), F32)
    for distance in range(parts - 1, 0, -1):
        held = pays[parts - distance - 1]
        tail = tail_rows(held)
        decay = tail[0:1, :] + tail[1:2, :]
        there = me + distance < parts
        running = jnp.where(there, held[0:STATE, :].astype(F32) + decay * running, 0.0)
    return running.astype(BF16)


def own_halo(pays):
    return jnp.where(lax.axis_index("seq") > 0, tail_rows(pays[0])[5:8, :], 0.0)


def merged_state(parts, taps, pays):
    me = lax.axis_index("seq")
    channels = pays[0].shape[1]
    running = jnp.zeros((STATE, channels), F32)
    tails = [tail_rows(pay) for pay in pays]
    blank = jnp.zeros((5, channels), F32)
    for distance in range(parts - 1, 0, -1):
        held = pays[distance - 1]
        tail = tails[distance - 1]
        state = held[0:STATE, :].astype(F32)
        if distance < parts - 1:
            halo = jnp.where(me > distance, tails[distance][5:8, :], 0.0)
            first = jnp.concatenate([tail[2:5, :], blank], axis=0)
            scale = jnp.concatenate([tail[11:14, :], blank, blank, blank[0:3, :]], axis=0)
            change = (first_change(taps, halo, first) * scale).astype(BF16)
            row = lax.broadcasted_iota(jnp.int32, (16, STATE), 0)
            lines = jnp.concatenate([tail[8:11, 0:STATE], blank[:, 0:STATE]], axis=0)
            lines = jnp.concatenate([lines, jnp.zeros_like(lines)], axis=0)
            lines = jnp.where(row < 3, lines, 0.0).astype(BF16)
            state = state + dot(lines, change, ((0,), (0,)))
        decay = tail[0:1, :] + tail[1:2, :]
        running = jnp.where(me >= distance, state + decay * running, 0.0)
    return running


def inner_kernel(
    heads, gains, near, far, logs, grad, mixed, sigma, b_proj, c_proj,
    base_out, grad_base, grad_weight, first_out,
    ahead_scores, behind_scores, mixed_scaled, mixed_low, grad_scaled, grad_low,
    mixed_fresh, grad_fresh,
):
    rows, channels = grad.shape
    chunks = rows // CHUNK
    blocks = [slice(j * CHUNK, (j + 1) * CHUNK) for j in range(chunks)]
    row = lax.broadcasted_iota(jnp.int32, (CHUNK, CHUNK), 0)
    col = lax.broadcasted_iota(jnp.int32, (CHUNK, CHUNK), 1)
    onehot = spread_matrix(heads, channels)
    gain = gains[0:1, :]
    for both in blocks:
        scale = spread(near[0:16, both], onehot)
        grad_scaled[both, :] = (grad[both, :].astype(F32) * scale).astype(BF16)
    for both in blocks:
        scale = spread(near[16:32, both], onehot)
        mixed_scaled[both, :] = (mixed[both, :] * scale).astype(BF16)
    for both in blocks:
        grad_fresh[both, :] = dot(c_proj[both, :], grad_scaled[both, :], ((0,), (0,)))
    for both in blocks:
        mixed_fresh[both, :] = dot(b_proj[both, :], mixed_scaled[both, :], ((0,), (0,)))
    for both in blocks:
        ahead = dot(c_proj[both, :], b_proj[both, :], ((1,), (1,)))
        ahead_scores[both, :] = jnp.where(row >= col, ahead, 0.0).astype(BF16)
    for both in blocks:
        behind = dot(b_proj[both, :], c_proj[both, :], ((1,), (1,)))
        behind_scores[both, :] = jnp.where(row <= col, behind, 0.0).astype(BF16)
    for lanes in lane_tiles(channels):
        adjoint = jnp.zeros((STATE, lanes.stop - lanes.start), F32)
        for j in range(chunks - 1, -1, -1):
            grad_low[blocks[j], lanes] = (adjoint * logs[2, j : j + 1, lanes]).astype(BF16)
            adjoint = logs[0, j : j + 1, lanes] * adjoint + (
                logs[1, j : j + 1, lanes] * grad_fresh[blocks[j], lanes]
            )
        state = jnp.zeros((STATE, lanes.stop - lanes.start), F32)
        for j in range(chunks):
            mixed_low[blocks[j], lanes] = (state * logs[1, j : j + 1, lanes]).astype(BF16)
            state = logs[0, j : j + 1, lanes] * state + (
                logs[2, j : j + 1, lanes] * mixed_fresh[blocks[j], lanes]
            )
    for both in blocks:
        inner = dot(
            jnp.concatenate([behind_scores[both, :], b_proj[both, :]], axis=1),
            jnp.concatenate([grad_scaled[both, :], grad_low[both, :]], axis=0),
            ((1,), (0,)),
        )
        slope = sigma[both, :] + mixed[both, :] * (1.0 - sigma[both, :])
        inner = gain * grad[both, :].astype(F32) + spread(near[16:32, both], onehot) * inner
        weight = spread(far[:, both], onehot)
        grad_base[both, :] = slope * inner
        grad_weight[both, :] = slope * weight
        if both.start == 0:
            first_out[0:8, :] = inner[0:8, :]
            first_out[8:16, :] = weight[0:8, :]
    for both in blocks:
        inner = dot(
            jnp.concatenate([ahead_scores[both, :], c_proj[both, :]], axis=1),
            jnp.concatenate([mixed_scaled[both, :], mixed_low[both, :]], axis=0),
            ((1,), (0,)),
        )
        base_out[both, :] = gain * mixed[both, :] + spread(near[0:16, both], onehot) * inner


def gradient_kernel(parts, taps, base, weight, unscaled, inputs, b_proj, *rest):
    pays = rest[: parts - 1]
    grad_out, tail_out, edge_out, window, exact = rest[parts - 1 :]
    rows, channels = base.shape
    chunks = rows // CHUNK
    adjoint = merged_adjoint(parts, pays)
    halo = own_halo(pays)
    preact = first_preact(taps, halo, inputs[0:16, :].astype(F32))
    sigma = 0.5 * jnp.tanh(0.5 * preact) + 0.5
    slope = sigma + preact * sigma * (1.0 - sigma)
    window[rows : rows + 16, :] = jnp.zeros((16, channels), BF16)
    row = lax.broadcasted_iota(jnp.int32, (3 * CHUNK, CHUNK + 16), 0)
    col = lax.broadcasted_iota(jnp.int32, (3 * CHUNK, CHUNK + 16), 1)
    shift = jnp.where(col == row % CHUNK + 3 - row // CHUNK, 1.0, 0.0).astype(BF16)
    partial = [jnp.zeros((8, channels), F32) for _ in range(4)]
    for j in range(chunks):
        both = slice(j * CHUNK, (j + 1) * CHUNK)
        carried = dot(b_proj[both, :], adjoint, ((1,), (0,)))
        grad_pre = base[both, :] + weight[both, :] * carried
        if j == 0:
            first = slope * (unscaled[0:8, :] + unscaled[8:16, :] * carried[0:8, :])
            grad_pre = jnp.concatenate([first, grad_pre[8:, :]], axis=0)
        window[both, :] = grad_pre.astype(BF16)
        exact[both, :] = grad_pre
    for j in range(chunks):
        at = j * CHUNK
        both = slice(at, at + CHUNK)
        grad_pre = exact[both, :]
        moved = dot(shift, window[at : at + CHUNK + 16, :], ((1,), (0,)))
        x = inputs[both, :].astype(F32)
        result = taps[3:4, :] * grad_pre
        partial[3] = partial[3] + (grad_pre * x).reshape(CHUNK // 8, 8, channels).sum(axis=0)
        for k in range(3):
            part = moved[k * CHUNK : (k + 1) * CHUNK, :]
            result = result + taps[k : k + 1, :] * part
            partial[k] = partial[k] + (part * x).reshape(CHUNK // 8, 8, channels).sum(axis=0)
        grad_out[both, :] = result.astype(BF16)
        if j == chunks - 1:
            edge_out[...] = result[CHUNK - 16 :, :]
    for k in range(4):
        tap = jnp.sum(partial[k], axis=0, keepdims=True)
        for j in range(k, 3):
            tap = tap + first[j - k : j - k + 1, :] * halo[j : j + 1, :]
        tail_out[k : k + 1, :] = tap
    tail_out[4:7, :] = first[0:3, :]
    tail_out[7:8, :] = jnp.zeros((1, channels), F32)


def output_kernel(
    heads, parts, gains, taps, front, lead, base, inputs, b_proj, c_proj, grad_rows, *rest
):
    pays = rest[: parts - 1]
    out_hbm, grad_hbm, result_rows, sems, grad_sem = rest[parts - 1 :]
    rows, channels = base.shape
    grad_copy = pltpu.make_async_copy(grad_rows, grad_hbm, grad_sem)
    grad_copy.start()
    incoming = merged_state(parts, taps, pays)
    onehot = spread_matrix(heads, channels)
    change = first_change(taps, own_halo(pays), inputs[0:16, :].astype(F32))
    change_scaled = (change * lead[...]).astype(BF16)
    state = incoming + dot(b_proj[0:16, :], change_scaled, ((0,), (0,)))
    state = state.astype(BF16)
    row = lax.broadcasted_iota(jnp.int32, (16, 16), 0)
    col = lax.broadcasted_iota(jnp.int32, (16, 16), 1)
    scores = dot(c_proj[0:16, :], b_proj[0:16, :], ((1,), (1,)))
    scores = jnp.where(row >= col, scores, 0.0).astype(BF16)
    top = dot(c_proj[0:16, :], incoming.astype(BF16), ((1,), (0,)))
    top = top + dot(scores, change_scaled, ((1,), (0,)))
    top = top * spread(front[:, 0:16], onehot) + base[0:16, :]
    top = top + gains[0:1, :] * change
    copies = []
    for piece in range(rows // STEP_ROWS):
        for at in range(piece * STEP_ROWS, (piece + 1) * STEP_ROWS, CHUNK):
            both = slice(at, at + CHUNK)
            carried = dot(c_proj[both, :], state, ((1,), (0,)))
            result = base[both, :] + spread(front[:, both], onehot) * carried
            result_rows[both, :] = result.astype(BF16)
            if at == 0:
                result_rows[0:16, :] = top.astype(BF16)
        place = pl.ds(piece * STEP_ROWS, STEP_ROWS)
        copy = pltpu.make_async_copy(result_rows.at[place], out_hbm.at[place], sems.at[piece])
        copy.start()
        copies.append(copy)
    for copy in copies:
        copy.wait()
    grad_copy.wait()


def finish_kernel(parts, scale, taps, tail, edge, *rest):
    others = rest[: parts - 1]
    unused, grad_hbm, conv_out, rows_low, sem = rest[parts - 1 :]
    channels = tail.shape[1]
    me = lax.axis_index("seq")
    after = jnp.where(me + 1 < parts, others[parts - 2][...], 0.0)
    row = lax.broadcasted_iota(jnp.int32, (16, channels), 0)
    result = edge[...]
    for r in range(3):
        extra = jnp.zeros((1, channels), F32)
        for k in range(r + 1):
            extra = extra + taps[k : k + 1, :] * after[4 + r - k : 5 + r - k, :]
        result = jnp.where(row == 13 + r, result + extra, result)
    rows_low[...] = result.astype(BF16)
    rows = grad_hbm.shape[0]
    copy = pltpu.make_async_copy(rows_low, grad_hbm.at[pl.ds(rows - 16, 16)], sem)
    copy.start()
    total = tail[0:4, :]
    for other in others:
        total = total + other[0:4, :]
    conv_out[...] = total * scale
    copy.wait()


def rotated(block, axis, distance):
    size = lax.axis_size(axis)
    return lax.ppermute(block, axis, [(i, (i + distance) % size) for i in range(size)])


def shards(
    inputs,
    b_proj,
    c_proj,
    step_codes,
    gate_codes,
    decay_rates,
    skip_gain,
    conv_weight,
    out_cotangent,
):
    rows, channels = inputs.shape
    heads = decay_rates.shape[0]
    parts = lax.axis_size("seq")
    chunks = rows // CHUNK
    pieces = rows // STEP_ROWS
    hbm = pl.BlockSpec(memory_space=pltpu.HBM)
    vmem = pl.BlockSpec(memory_space=pltpu.VMEM)
    shape = jax.ShapeDtypeStruct
    dma = pltpu.SemaphoreType.DMA
    big = rows * channels

    def call(kernel, in_specs, out_specs, out_shape, scratch, products, aliases=None):
        return pl.pallas_call(
            kernel,
            in_specs=in_specs,
            out_specs=out_specs,
            out_shape=out_shape,
            scratch_shapes=scratch,
            input_output_aliases=aliases or {},
            compiler_params=pltpu.CompilerParams(vmem_limit_bytes=VMEM_LIMIT),
            cost_estimate=pl.CostEstimate(
                flops=products * 2 * big * 128, bytes_accessed=6 * big, transcendentals=big
            ),
        )

    def stay(array):
        return pltpu.with_memory_space_constraint(array, pltpu.HBM)

    pay = shape((STATE + 16, channels), BF16)
    narrow = shape((rows, channels), BF16)
    broad = shape((rows, channels), F32)
    slim = shape((rows, STATE), BF16)

    outs = call(
        functools.partial(reduce_kernel, heads, parts),
        [hbm] * 9,
        [vmem] * (11 + parts),
        [
            shape((32, rows), BF16),
            shape((16, rows), BF16),
            shape((16, rows), BF16),
            shape((3, chunks, channels), F32),
            shape((16, channels), F32),
            shape((8, channels), F32),
            broad,
            broad,
            narrow,
            slim,
            narrow,
            slim,
        ]
        + [pay] * (parts - 1),
        [
            pltpu.SMEM((heads,), F32),
            pltpu.SMEM((heads,), F32),
            pltpu.VMEM((heads, rows), jnp.int32),
            pltpu.VMEM((1, rows), jnp.int32),
            pltpu.VMEM((4, channels), F32),
            pltpu.VMEM((8, rows), F32),
            pltpu.VMEM((rows, channels), BF16),
            pltpu.VMEM((16, CHUNK), BF16),
            pltpu.VMEM((16, channels), F32),
            dma((9,)),
        ],
        4,
    )(
        stay(decay_rates),
        stay(skip_gain),
        stay(step_codes),
        stay(gate_codes.reshape(1, rows)),
        stay(conv_weight),
        stay(inputs),
        stay(b_proj),
        stay(out_cotangent),
        stay(c_proj),
    )
    near, far, front, logs, lead, gain, mixed, sigma = outs[:8]
    inputs, b_proj, out_cotangent, c_proj = outs[8:12]
    pays = [rotated(send, "seq", distance + 1) for distance, send in enumerate(outs[12:])]

    tile = pltpu.VMEM((rows, CHUNK), BF16)
    low = pltpu.VMEM((rows, channels), BF16)
    high = pltpu.VMEM((rows, channels), F32)
    base, grad_base, grad_weight, unscaled = call(
        functools.partial(inner_kernel, heads),
        [vmem] * 9,
        [vmem] * 4,
        [broad] * 3 + [shape((16, channels), F32)],
        [tile, tile, low, low, low, low, high, high],
        10,
    )(gain, near, far, logs, out_cotangent, mixed, sigma, b_proj, c_proj)

    grad_rows, tail, edge = call(
        functools.partial(gradient_kernel, parts),
        [vmem] * (5 + parts),
        [vmem] * 3,
        [narrow, shape((8, channels), F32), shape((16, channels), F32)],
        [pltpu.VMEM((rows + 16, channels), BF16), pltpu.VMEM((rows, channels), F32)],
        2,
    )(conv_weight, grad_base, grad_weight, unscaled, inputs, b_proj, *pays)
    tails = [rotated(tail, "seq", distance) for distance in range(1, parts)]

    layer_out, grad_rows = call(
        functools.partial(output_kernel, heads, parts),
        [vmem] * (8 + parts),
        [hbm, hbm],
        [narrow, narrow],
        [pltpu.VMEM((rows, channels), BF16), dma((pieces,)), dma],
        2,
    )(gain, conv_weight, front, lead, base, inputs, b_proj, c_proj, grad_rows, *pays)

    scale = float((rows * parts) ** -0.5)
    input_grad, conv_grad = call(
        functools.partial(finish_kernel, parts, scale),
        [vmem] * (2 + parts) + [hbm],
        [hbm, vmem],
        [narrow, shape((4, channels), F32)],
        [pltpu.VMEM((16, channels), BF16), dma],
        0,
        {parts + 2: 0},
    )(conv_weight, tail, edge, *tails, grad_rows)
    return layer_out, input_grad, conv_grad


def solution(mesh):
    in_specs = (
        P(("groups", "seq"), ("head", "sub")),
        P(("groups", "seq"), None),
        P(("groups", "seq"), None),
        P(("head", "sub"), ("groups", "seq")),
        P(("groups", "seq")),
        P(("head", "sub")),
        P(("head", "sub")),
        P(None, ("head", "sub")),
        P(("groups", "seq"), ("head", "sub")),
    )
    out_specs = (
        P(("groups", "seq"), ("head", "sub")),
        P(("groups", "seq"), ("head", "sub")),
        P("groups", ("head", "sub")),
    )
    return jax.shard_map(shards, mesh=mesh, in_specs=in_specs, out_specs=out_specs, check_vma=False)
```

```python
import functools

import jax
import jax.numpy as jnp
from jax import lax
from jax.experimental import pallas as pl
from jax.experimental.pallas import tpu as pltpu
from jax.sharding import PartitionSpec as P

CHUNK = 128
STATE = 128
PIECES = 4
STEP_ROWS = 512
LOG_ONE = -0.2876820724517809
LOG_TWO = -0.6931471805599453
F32 = jnp.float32
BF16 = jnp.bfloat16
HIGHEST = lax.Precision.HIGHEST
VMEM_LIMIT = 20 * 1024 * 1024


def dot(a, b, dims, precision=None):
    return lax.dot_general(a, b, (dims, ((), ())), preferred_element_type=F32, precision=precision)


def per_lane(scalars, count, channels):
    width = channels // count
    lane = lax.broadcasted_iota(jnp.int32, (1, channels), 1)
    row = jnp.zeros((1, channels), F32)
    for head in range(count):
        inside = (lane >= head * width) & (lane < (head + 1) * width)
        row = jnp.where(inside, scalars[head], row)
    return row


def split_two(value):
    high = value.astype(BF16)
    low = (value - high.astype(F32)).astype(BF16)
    return jnp.concatenate([high.astype(F32), low.astype(F32)], axis=0).astype(BF16)


def spread_matrix(count, channels):
    width = channels // count
    row = lax.broadcasted_iota(jnp.int32, (16, channels), 0)
    lane = lax.broadcasted_iota(jnp.int32, (16, channels), 1)
    return jnp.where((row % 8) == lane // width, 1.0, 0.0).astype(BF16)


def spread(pair, onehot):
    return dot(pair, onehot, ((0,), (0,)))


def reduce_kernel(
    heads, parts,
    rates_hbm, gains_hbm, codes_hbm, gates_hbm, taps_hbm, inputs_hbm, b_hbm, grad_hbm, c_hbm,
    near_out, far_out, front_out, logs_out, lead_out, gain_out, mixed_out, sigma_out,
    inputs, b_proj, grad, c_proj, *rest
):
    pays = rest[: parts - 1]
    rates, gains, codes, gates, taps, steps, scaled, lead_pair, extra, sems = rest[parts - 1 :]
    rows, channels = grad.shape
    chunks = rows // CHUNK
    sources = (
        rates_hbm, gains_hbm, codes_hbm, gates_hbm, taps_hbm, inputs_hbm, b_hbm, grad_hbm, c_hbm
    )
    targets = (rates, gains, codes, gates, taps, inputs, b_proj, grad, c_proj)
    copies = []
    for i, (source, target) in enumerate(zip(sources, targets)):
        cuts = PIECES if i in (5, 7) else 1
        high = source.shape[0] // cuts if cuts > 1 else None
        parts_of = []
        for cut in range(cuts):
            place = pl.ds(cut * high, high) if cuts > 1 else slice(None)
            copy = pltpu.make_async_copy(source.at[place], target.at[place], sems.at[i, cut])
            copy.start()
            parts_of.append(copy)
        copies.append(parts_of)
    for copy in sum(copies[:4], []):
        copy.wait()

    steps[...] = jnp.zeros_like(steps)
    steps[0:heads, :] = jnp.exp2(-codes[...].astype(F32))
    gate = gates[...]
    steps[6:7, :] = jnp.where(gate == 1, 1.0, 0.0).astype(F32)
    steps[7:8, :] = jnp.where(gate == 2, 1.0, 0.0).astype(F32)
    stacked = jnp.concatenate(
        [steps[:, j * CHUNK : (j + 1) * CHUNK] for j in range(chunks)], axis=0
    ).astype(BF16)
    row = lax.broadcasted_iota(jnp.int32, (CHUNK, CHUNK), 0)
    col = lax.broadcasted_iota(jnp.int32, (CHUNK, CHUNK), 1)
    upper = jnp.where(row <= col, 1.0, 0.0).astype(BF16)
    sums = dot(stacked, upper, ((1,), (0,)))
    sub = lax.broadcasted_iota(jnp.int32, (8, CHUNK), 0)
    rate = jnp.zeros((8, CHUNK), F32)
    for head in range(heads):
        rate = jnp.where(sub == head, rates[head], rate)
    cums, mids, befores = [], [], []
    before = jnp.zeros((8, 1), F32)
    for j in range(chunks):
        part = sums[8 * j : 8 * j + 8, :]
        cum = LOG_ONE * part[6:7, :] + LOG_TWO * part[7:8, :] - rate * part
        cums.append(cum)
        mids.append(cum[:, CHUNK // 2 - 1 : CHUNK // 2])
        befores.append(before)
        before = before + cum[:, CHUNK - 1 : CHUNK]
    for j in range(chunks):
        at = slice(j * CHUNK, (j + 1) * CHUNK)
        size = steps[:, at]
        near_out[0:16, at] = split_two(jnp.exp(cums[j] - mids[j]))
        near_out[16:32, at] = split_two(jnp.exp(mids[j] - cums[j]) * size)
        front_out[:, at] = split_two(jnp.exp(befores[j] + cums[j]))
        far_out[:, at] = split_two(jnp.exp(before - befores[j] - cums[j]) * size)
    lead_pair[...] = split_two(jnp.exp(-jnp.maximum(cums[0], -8.0)) * steps[:, 0:CHUNK])
    pick = lax.broadcasted_iota(jnp.int32, (8, CHUNK), 0)
    place = lax.broadcasted_iota(jnp.int32, (8, CHUNK), 1)
    chosen = jnp.where((pick == 0) | ((pick == 1) & (place < CHUNK // 2)), 1.0, 0.0)
    flat = dot(chosen.astype(BF16), stacked, ((1,), (1,)))
    owner = lax.broadcasted_iota(jnp.int32, (chunks, 8 * chunks), 1) // 8
    chunk_at = lax.broadcasted_iota(jnp.int32, (chunks, 8 * chunks), 0)
    lane_rate = per_lane(rates, heads, channels)
    kind = lax.broadcasted_iota(jnp.int32, (8 * chunks, channels), 0) % 8
    lane_head = lax.broadcasted_iota(jnp.int32, (8 * chunks, channels), 1) // (channels // heads)
    mixer = jnp.where(kind == lane_head, -lane_rate, 0.0)
    mixer = jnp.where(kind == 6, LOG_ONE, jnp.where(kind == 7, LOG_TWO, mixer))
    table = []
    for which in range(2):
        own = jnp.where(owner == chunk_at, flat[which : which + 1, :], 0.0)
        table.append(dot(own, mixer, ((1,), (0,)), HIGHEST))
    whole = jnp.exp(table[0])
    middle = jnp.exp(table[1])
    rest_of = jnp.exp(table[0] - table[1])
    logs_out[0] = whole
    logs_out[1] = middle
    logs_out[2] = rest_of
    decay = jnp.exp(jnp.sum(table[0], axis=0, keepdims=True))
    first = decay.astype(BF16).astype(F32)
    extra[...] = jnp.zeros_like(extra)
    extra[0:1, :] = first
    extra[1:2, :] = decay - first

    onehot = spread_matrix(heads, channels)
    lead_out[...] = spread(lead_pair[:, 0:16], onehot)
    gain_out[...] = jnp.broadcast_to(per_lane(gains, heads, channels), (8, channels))
    for copy in sum(copies[4:7], []):
        copy.wait()
    shift = back_shift()
    nothing = jnp.zeros((16, channels), BF16)
    for at in range(0, rows, CHUNK):
        both = slice(at, at + CHUNK)
        if at == 0:
            block = jnp.concatenate([nothing, inputs[both, :]], axis=0)
        else:
            block = inputs[at - 16 : at + CHUNK, :]
        moved = dot(shift, block, ((1,), (0,)))
        preact = taps[3:4, :] * inputs[both, :].astype(F32)
        for k in range(3):
            preact = preact + taps[k : k + 1, :] * moved[k * CHUNK : (k + 1) * CHUNK, :]
        sigma = 0.5 * jnp.tanh(0.5 * preact) + 0.5
        mixed = preact * sigma
        scale = spread(far_out[:, both], onehot)
        sigma_out[both, :] = sigma
        mixed_out[both, :] = mixed
        scaled[both, :] = (mixed * scale).astype(BF16)
        if at == 0:
            extra[11:14, :] = scale[0:3, :]
    state = dot(b_proj[...], scaled[...], ((0,), (0,))).astype(BF16)
    extra[2:5, :] = inputs[0:16, :].astype(F32)[0:3, :]
    extra[5:8, :] = inputs[rows - 16 : rows, :].astype(F32)[13:16, :]
    extra[8:11, 0:STATE] = b_proj[0:16, :].astype(F32)[0:3, :]
    for copy in sum(copies[7:], []):
        copy.wait()
    for at in range(0, rows, STEP_ROWS):
        both = slice(at, at + STEP_ROWS)
        scale = spread(front_out[:, both], onehot)
        scaled[both, :] = (grad[both, :].astype(F32) * scale).astype(BF16)
    adjoint = dot(c_proj[...], scaled[...], ((0,), (0,))).astype(BF16)
    me = lax.axis_index("seq")
    for distance in range(1, parts):
        pay = pays[distance - 1]
        pay[0:STATE, :] = jnp.where(partner(me, distance, parts) > me, state, adjoint)
        pay[STATE : STATE + 16, :] = extra[...].astype(BF16)


def back_shift():
    row = lax.broadcasted_iota(jnp.int32, (3 * CHUNK, CHUNK + 16), 0)
    col = lax.broadcasted_iota(jnp.int32, (3 * CHUNK, CHUNK + 16), 1)
    return jnp.where(col == row % CHUNK + 13 + row // CHUNK, 1.0, 0.0).astype(BF16)


def tail_rows(held, source):
    return held[source, STATE : STATE + 16, :].astype(F32)


def first_preact(taps, halo, first):
    joined = jnp.concatenate([halo[0:3, :], first[0:8, :]], axis=0)
    preact = taps[0:1, :] * joined[0:8, :]
    for k in range(1, 4):
        preact = preact + taps[k : k + 1, :] * joined[k : k + 8, :]
    return preact


def first_change(taps, halo, first):
    true = first_preact(taps, halo, first)
    bare = first_preact(taps, jnp.zeros_like(halo), first)
    change = true * (0.5 * jnp.tanh(0.5 * true) + 0.5) - bare * (0.5 * jnp.tanh(0.5 * bare) + 0.5)
    row = lax.broadcasted_iota(jnp.int32, change.shape, 0)
    change = jnp.where(row < 3, change, 0.0)
    return jnp.concatenate([change, jnp.zeros_like(change)], axis=0)


def lane_tiles(channels):
    return [slice(at, min(at + 128, channels)) for at in range(0, channels, 128)]


def partner(me, distance, parts):
    return (me ^ distance) if parts & (parts - 1) == 0 else (me + distance) % parts


def sender(me, distance, parts):
    return (me ^ distance) if parts & (parts - 1) == 0 else (me + parts - distance) % parts


def sort_blocks(parts, pays, held):
    me = lax.axis_index("seq")
    held[me] = jnp.zeros(held.shape[1:], BF16)
    for distance in range(1, parts):
        held[sender(me, distance, parts)] = pays[distance - 1][...]


def merged_adjoint(parts, held):
    me = lax.axis_index("seq")
    running = jnp.zeros((STATE, held.shape[2]), F32)
    for source in range(parts - 1, 0, -1):
        tail = tail_rows(held, source)
        decay = tail[0:1, :] + tail[1:2, :]
        block = held[source, 0:STATE, :].astype(F32)
        running = jnp.where(source > me, block + decay * running, running)
    return running.astype(BF16)


def own_halo(held):
    me = lax.axis_index("seq")
    return jnp.where(me > 0, tail_rows(held, jnp.maximum(me - 1, 0))[5:8, :], 0.0)


def merged_state(parts, taps, held):
    me = lax.axis_index("seq")
    channels = held.shape[2]
    running = jnp.zeros((STATE, channels), F32)
    blank = jnp.zeros((5, channels), F32)
    tails = [tail_rows(held, source) for source in range(parts - 1)]
    for source in range(parts - 1):
        tail = tails[source]
        state = held[source, 0:STATE, :].astype(F32)
        if source > 0:
            first = jnp.concatenate([tail[2:5, :], blank], axis=0)
            scale = jnp.concatenate([tail[11:14, :], blank, blank, blank[0:3, :]], axis=0)
            change = first_change(taps, tails[source - 1][5:8, :], first)
            change = (change * scale).astype(BF16)
            row = lax.broadcasted_iota(jnp.int32, (16, STATE), 0)
            lines = jnp.concatenate([tail[8:11, 0:STATE], blank[:, 0:STATE]], axis=0)
            lines = jnp.concatenate([lines, jnp.zeros_like(lines)], axis=0)
            lines = jnp.where(row < 3, lines, 0.0).astype(BF16)
            state = state + dot(lines, change, ((0,), (0,)))
        decay = tail[0:1, :] + tail[1:2, :]
        running = jnp.where(source < me, state + decay * running, running)
    return running


def inner_kernel(
    heads, gains, near, far, logs, grad, mixed, sigma, b_proj, c_proj,
    inputs, base_out, grad_base, grad_weight, first_out, moved_out,
    ahead_scores, behind_scores, mixed_scaled, mixed_low, grad_scaled, grad_low,
    mixed_fresh, grad_fresh,
):
    rows, channels = grad.shape
    chunks = rows // CHUNK
    blocks = [slice(j * CHUNK, (j + 1) * CHUNK) for j in range(chunks)]
    row = lax.broadcasted_iota(jnp.int32, (CHUNK, CHUNK), 0)
    col = lax.broadcasted_iota(jnp.int32, (CHUNK, CHUNK), 1)
    onehot = spread_matrix(heads, channels)
    gain = gains[0:1, :]
    for both in blocks:
        scale = spread(near[0:16, both], onehot)
        grad_scaled[both, :] = (grad[both, :].astype(F32) * scale).astype(BF16)
    for both in blocks:
        scale = spread(near[16:32, both], onehot)
        mixed_scaled[both, :] = (mixed[both, :] * scale).astype(BF16)
    for both in blocks:
        grad_fresh[both, :] = dot(c_proj[both, :], grad_scaled[both, :], ((0,), (0,)))
    for both in blocks:
        mixed_fresh[both, :] = dot(b_proj[both, :], mixed_scaled[both, :], ((0,), (0,)))
    for both in blocks:
        ahead = dot(c_proj[both, :], b_proj[both, :], ((1,), (1,)))
        ahead_scores[both, :] = jnp.where(row >= col, ahead, 0.0).astype(BF16)
    for both in blocks:
        behind = dot(b_proj[both, :], c_proj[both, :], ((1,), (1,)))
        behind_scores[both, :] = jnp.where(row <= col, behind, 0.0).astype(BF16)
    for lanes in lane_tiles(channels):
        adjoint = jnp.zeros((STATE, lanes.stop - lanes.start), F32)
        for j in range(chunks - 1, -1, -1):
            grad_low[blocks[j], lanes] = (adjoint * logs[2, j : j + 1, lanes]).astype(BF16)
            adjoint = logs[0, j : j + 1, lanes] * adjoint + (
                logs[1, j : j + 1, lanes] * grad_fresh[blocks[j], lanes]
            )
        state = jnp.zeros((STATE, lanes.stop - lanes.start), F32)
        for j in range(chunks):
            mixed_low[blocks[j], lanes] = (state * logs[1, j : j + 1, lanes]).astype(BF16)
            state = logs[0, j : j + 1, lanes] * state + (
                logs[2, j : j + 1, lanes] * mixed_fresh[blocks[j], lanes]
            )
    for both in blocks:
        inner = dot(
            jnp.concatenate([behind_scores[both, :], b_proj[both, :]], axis=1),
            jnp.concatenate([grad_scaled[both, :], grad_low[both, :]], axis=0),
            ((1,), (0,)),
        )
        slope = sigma[both, :] + mixed[both, :] * (1.0 - sigma[both, :])
        inner = gain * grad[both, :].astype(F32) + spread(near[16:32, both], onehot) * inner
        weight = spread(far[:, both], onehot)
        grad_base[both, :] = slope * inner
        grad_weight[both, :] = slope * weight
        if both.start == 0:
            first_out[0:8, :] = inner[0:8, :]
            first_out[8:16, :] = weight[0:8, :]
    for both in blocks:
        inner = dot(
            jnp.concatenate([ahead_scores[both, :], c_proj[both, :]], axis=1),
            jnp.concatenate([mixed_scaled[both, :], mixed_low[both, :]], axis=0),
            ((1,), (0,)),
        )
        base_out[both, :] = gain * mixed[both, :] + spread(near[0:16, both], onehot) * inner
    shift = back_shift()
    for both in blocks:
        if both.start == 0:
            nothing = jnp.zeros((16, channels), BF16)
            block = jnp.concatenate([nothing, inputs[both, :]], axis=0)
        else:
            block = inputs[both.start - 16 : both.stop, :]
        moved = dot(shift, block, ((1,), (0,)))
        for k in range(3):
            moved_out[k, both, :] = moved[k * CHUNK : (k + 1) * CHUNK, :].astype(BF16)


def gradient_kernel(parts, taps, base, weight, unscaled, inputs, moved, b_proj, *rest):
    pays = rest[: parts - 1]
    exact, window, tail_out, held, products = rest[parts - 1 :]
    rows, channels = base.shape
    chunks = rows // CHUNK
    sort_blocks(parts, pays, held)
    adjoint = merged_adjoint(parts, held)
    halo = own_halo(held)
    preact = first_preact(taps, halo, inputs[0:16, :].astype(F32))
    sigma = 0.5 * jnp.tanh(0.5 * preact) + 0.5
    slope = sigma + preact * sigma * (1.0 - sigma)
    window[rows : rows + 16, :] = jnp.zeros((16, channels), BF16)
    for j in range(chunks):
        both = slice(j * CHUNK, (j + 1) * CHUNK)
        carried = dot(b_proj[both, :], adjoint, ((1,), (0,)))
        grad_pre = base[both, :] + weight[both, :] * carried
        if j == 0:
            first = slope * (unscaled[0:8, :] + unscaled[8:16, :] * carried[0:8, :])
            grad_pre = jnp.concatenate([first, grad_pre[8:, :]], axis=0)
        exact[both, :] = grad_pre
        low = grad_pre.astype(BF16)
        window[both, :] = low
        for k in range(3):
            products[k, both, :] = low * moved[k, both, :]
        products[3, both, :] = low * inputs[both, :]
    ones = jnp.ones((8, rows), BF16)
    for k in range(4):
        tap = dot(ones, products[k], ((1,), (0,)))[0:1, :]
        for j in range(k, 3):
            tap = tap + first[j - k : j - k + 1, :] * halo[j : j + 1, :]
        tail_out[k : k + 1, :] = tap
    tail_out[4:7, :] = first[0:3, :]
    tail_out[7:8, :] = jnp.zeros((1, channels), F32)


def output_kernel(
    heads, parts, gains, taps, front, lead, base, inputs, b_proj, c_proj, exact, window, *rest
):
    pays = rest[: parts - 1]
    out_hbm, grad_hbm, edge_out, held, result_rows, grad_rows, sems, grad_sems = rest[parts - 1 :]
    rows, channels = base.shape
    sort_blocks(parts, pays, held)
    incoming = merged_state(parts, taps, held)
    onehot = spread_matrix(heads, channels)
    change = first_change(taps, own_halo(held), inputs[0:16, :].astype(F32))
    change_scaled = (change * lead[...]).astype(BF16)
    state = incoming + dot(b_proj[0:16, :], change_scaled, ((0,), (0,)))
    state = state.astype(BF16)
    row = lax.broadcasted_iota(jnp.int32, (16, 16), 0)
    col = lax.broadcasted_iota(jnp.int32, (16, 16), 1)
    scores = dot(c_proj[0:16, :], b_proj[0:16, :], ((1,), (1,)))
    scores = jnp.where(row >= col, scores, 0.0).astype(BF16)
    top = dot(c_proj[0:16, :], incoming.astype(BF16), ((1,), (0,)))
    top = top + dot(scores, change_scaled, ((1,), (0,)))
    top = top * spread(front[:, 0:16], onehot) + base[0:16, :]
    top = top + gains[0:1, :] * change
    row = lax.broadcasted_iota(jnp.int32, (3 * CHUNK, CHUNK + 16), 0)
    col = lax.broadcasted_iota(jnp.int32, (3 * CHUNK, CHUNK + 16), 1)
    shift = jnp.where(col == row % CHUNK + 3 - row // CHUNK, 1.0, 0.0).astype(BF16)
    copies = []
    for piece in range(rows // STEP_ROWS):
        for at in range(piece * STEP_ROWS, (piece + 1) * STEP_ROWS, CHUNK):
            both = slice(at, at + CHUNK)
            moved = dot(shift, window[at : at + CHUNK + 16, :], ((1,), (0,)))
            result = taps[3:4, :] * exact[both, :]
            for k in range(3):
                result = result + taps[k : k + 1, :] * moved[k * CHUNK : (k + 1) * CHUNK, :]
            grad_rows[both, :] = result.astype(BF16)
            if at + CHUNK == rows:
                edge_out[...] = result[CHUNK - 16 :, :]
            carried = dot(c_proj[both, :], state, ((1,), (0,)))
            result = base[both, :] + spread(front[:, both], onehot) * carried
            result_rows[both, :] = result.astype(BF16)
            if at == 0:
                result_rows[0:16, :] = top.astype(BF16)
        place = pl.ds(piece * STEP_ROWS, STEP_ROWS)
        copy = pltpu.make_async_copy(result_rows.at[place], out_hbm.at[place], sems.at[piece])
        copy.start()
        copies.append(copy)
        copy = pltpu.make_async_copy(
            grad_rows.at[place], grad_hbm.at[place], grad_sems.at[piece]
        )
        copy.start()
        copies.append(copy)
    for copy in copies:
        copy.wait()


def finish_kernel(parts, scale, taps, tail, edge, *rest):
    others = rest[: parts - 1]
    unused, grad_hbm, conv_out, rows_low, sem = rest[parts - 1 :]
    channels = tail.shape[1]
    me = lax.axis_index("seq")
    after = jnp.zeros(tail.shape, F32)
    for distance in range(1, parts):
        here = sender(me, distance, parts) == me + 1
        after = jnp.where(here, others[distance - 1][...], after)
    row = lax.broadcasted_iota(jnp.int32, (16, channels), 0)
    result = edge[...]
    for r in range(3):
        extra = jnp.zeros((1, channels), F32)
        for k in range(r + 1):
            extra = extra + taps[k : k + 1, :] * after[4 + r - k : 5 + r - k, :]
        result = jnp.where(row == 13 + r, result + extra, result)
    rows_low[...] = result.astype(BF16)
    rows = grad_hbm.shape[0]
    copy = pltpu.make_async_copy(rows_low, grad_hbm.at[pl.ds(rows - 16, 16)], sem)
    copy.start()
    total = tail[0:4, :]
    for other in others:
        total = total + other[0:4, :]
    conv_out[...] = total * scale
    copy.wait()


def rotated(block, axis, distance):
    size = lax.axis_size(axis)
    return lax.ppermute(block, axis, [(i, partner(i, distance, size)) for i in range(size)])


def shards(
    inputs,
    b_proj,
    c_proj,
    step_codes,
    gate_codes,
    decay_rates,
    skip_gain,
    conv_weight,
    out_cotangent,
):
    rows, channels = inputs.shape
    heads = decay_rates.shape[0]
    parts = lax.axis_size("seq")
    chunks = rows // CHUNK
    pieces = rows // STEP_ROWS
    hbm = pl.BlockSpec(memory_space=pltpu.HBM)
    vmem = pl.BlockSpec(memory_space=pltpu.VMEM)
    shape = jax.ShapeDtypeStruct
    dma = pltpu.SemaphoreType.DMA
    big = rows * channels

    def call(kernel, in_specs, out_specs, out_shape, scratch, products, aliases=None):
        return pl.pallas_call(
            kernel,
            in_specs=in_specs,
            out_specs=out_specs,
            out_shape=out_shape,
            scratch_shapes=scratch,
            input_output_aliases=aliases or {},
            compiler_params=pltpu.CompilerParams(vmem_limit_bytes=VMEM_LIMIT),
            cost_estimate=pl.CostEstimate(
                flops=products * 2 * big * 128, bytes_accessed=6 * big, transcendentals=big
            ),
        )

    def stay(array):
        return pltpu.with_memory_space_constraint(array, pltpu.HBM)

    pay = shape((STATE + 16, channels), BF16)
    narrow = shape((rows, channels), BF16)
    broad = shape((rows, channels), F32)
    slim = shape((rows, STATE), BF16)

    outs = call(
        functools.partial(reduce_kernel, heads, parts),
        [hbm] * 9,
        [vmem] * (11 + parts),
        [
            shape((32, rows), BF16),
            shape((16, rows), BF16),
            shape((16, rows), BF16),
            shape((3, chunks, channels), F32),
            shape((16, channels), F32),
            shape((8, channels), F32),
            broad,
            broad,
            narrow,
            slim,
            narrow,
            slim,
        ]
        + [pay] * (parts - 1),
        [
            pltpu.SMEM((heads,), F32),
            pltpu.SMEM((heads,), F32),
            pltpu.VMEM((heads, rows), jnp.int32),
            pltpu.VMEM((1, rows), jnp.int32),
            pltpu.VMEM((4, channels), F32),
            pltpu.VMEM((8, rows), F32),
            pltpu.VMEM((rows, channels), BF16),
            pltpu.VMEM((16, CHUNK), BF16),
            pltpu.VMEM((16, channels), F32),
            dma((9, PIECES)),
        ],
        4,
    )(
        stay(decay_rates),
        stay(skip_gain),
        stay(step_codes),
        stay(gate_codes.reshape(1, rows)),
        stay(conv_weight),
        stay(inputs),
        stay(b_proj),
        stay(out_cotangent),
        stay(c_proj),
    )
    near, far, front, logs, lead, gain, mixed, sigma = outs[:8]
    inputs, b_proj, out_cotangent, c_proj = outs[8:12]
    pays = [rotated(send, "seq", distance + 1) for distance, send in enumerate(outs[12:])]

    tile = pltpu.VMEM((rows, CHUNK), BF16)
    low = pltpu.VMEM((rows, channels), BF16)
    high = pltpu.VMEM((rows, channels), F32)
    base, grad_base, grad_weight, unscaled, moved = call(
        functools.partial(inner_kernel, heads),
        [vmem] * 10,
        [vmem] * 5,
        [broad] * 3 + [shape((16, channels), F32), shape((3, rows, channels), BF16)],
        [tile, tile, low, low, low, low, high, high],
        10,
    )(gain, near, far, logs, out_cotangent, mixed, sigma, b_proj, c_proj, inputs)

    held = pltpu.VMEM((parts, STATE + 16, channels), BF16)
    exact, window, tail = call(
        functools.partial(gradient_kernel, parts),
        [vmem] * (6 + parts),
        [vmem] * 3,
        [broad, shape((rows + 16, channels), BF16), shape((8, channels), F32)],
        [held, pltpu.VMEM((4, rows, channels), BF16)],
        2,
    )(conv_weight, grad_base, grad_weight, unscaled, inputs, moved, b_proj, *pays)
    tails = [rotated(tail, "seq", distance) for distance in range(1, parts)]

    layer_out, grad_rows, edge = call(
        functools.partial(output_kernel, heads, parts),
        [vmem] * (9 + parts),
        [hbm, hbm, vmem],
        [narrow, narrow, shape((16, channels), F32)],
        [held, low, low, dma((pieces,)), dma((pieces,))],
        4,
    )(gain, conv_weight, front, lead, base, inputs, b_proj, c_proj, exact, window, *pays)

    scale = float((rows * parts) ** -0.5)
    input_grad, conv_grad = call(
        functools.partial(finish_kernel, parts, scale),
        [vmem] * (2 + parts) + [hbm],
        [hbm, vmem],
        [narrow, shape((4, channels), F32)],
        [pltpu.VMEM((16, channels), BF16), dma],
        0,
        {parts + 2: 0},
    )(conv_weight, tail, edge, *tails, grad_rows)
    return layer_out, input_grad, conv_grad


def solution(mesh):
    in_specs = (
        P(("groups", "seq"), ("head", "sub")),
        P(("groups", "seq"), None),
        P(("groups", "seq"), None),
        P(("head", "sub"), ("groups", "seq")),
        P(("groups", "seq")),
        P(("head", "sub")),
        P(("head", "sub")),
        P(None, ("head", "sub")),
        P(("groups", "seq"), ("head", "sub")),
    )
    out_specs = (
        P(("groups", "seq"), ("head", "sub")),
        P(("groups", "seq"), ("head", "sub")),
        P("groups", ("head", "sub")),
    )
    return jax.shard_map(shards, mesh=mesh, in_specs=in_specs, out_specs=out_specs, check_vma=False)
```

```python
import functools

import jax
import jax.numpy as jnp
from jax import lax
from jax.experimental import pallas as pl
from jax.experimental.pallas import tpu as pltpu
from jax.sharding import PartitionSpec as P

CHUNK = 128
STATE = 128
STEP_ROWS = 512
LOG_ONE = -0.2876820724517809
LOG_TWO = -0.6931471805599453
F32 = jnp.float32
BF16 = jnp.bfloat16
HIGHEST = lax.Precision.HIGHEST
VMEM_LIMIT = 20 * 1024 * 1024


def dot(a, b, dims, precision=None):
    return lax.dot_general(a, b, (dims, ((), ())), preferred_element_type=F32, precision=precision)


def per_lane(scalars, count, channels):
    width = channels // count
    lane = lax.broadcasted_iota(jnp.int32, (1, channels), 1)
    row = jnp.zeros((1, channels), F32)
    for head in range(count):
        inside = (lane >= head * width) & (lane < (head + 1) * width)
        row = jnp.where(inside, scalars[head], row)
    return row


def split_two(value):
    high = value.astype(BF16)
    low = (value - high.astype(F32)).astype(BF16)
    return jnp.concatenate([high.astype(F32), low.astype(F32)], axis=0).astype(BF16)


def head_of(lane, width):
    if width & (width - 1) == 0:
        return lane >> (width.bit_length() - 1)
    return lane // width


def spread_matrix(count, channels):
    width = channels // count
    row = lax.broadcasted_iota(jnp.int32, (16, channels), 0)
    lane = lax.broadcasted_iota(jnp.int32, (16, channels), 1)
    return jnp.where((row & 7) == head_of(lane, width), 1.0, 0.0).astype(BF16)


def spread(pair, onehot):
    return dot(pair, onehot, ((0,), (0,)))


def reduce_kernel(
    heads, parts,
    rates_hbm, gains_hbm, codes_hbm, gates_hbm, taps_hbm, inputs_hbm, b_hbm, grad_hbm, c_hbm,
    near_out, far_out, front_out, logs_out, lead_out, gain_out, mixed_out, sigma_out,
    inputs, b_proj, grad, c_proj, *rest
):
    pays = rest[: parts - 1]
    rates, gains, codes, gates, taps, steps, scaled, lead_pair, extra, sems = rest[parts - 1 :]
    rows, channels = grad.shape
    chunks = rows // CHUNK
    sources = (
        rates_hbm, gains_hbm, codes_hbm, gates_hbm, taps_hbm, inputs_hbm, b_hbm, grad_hbm, c_hbm
    )
    targets = (rates, gains, codes, gates, taps, inputs, b_proj, grad, c_proj)
    copies = [
        pltpu.make_async_copy(source, target, sems.at[i])
        for i, (source, target) in enumerate(zip(sources, targets))
    ]
    for copy in copies:
        copy.start()
    for copy in copies[:4]:
        copy.wait()

    steps[...] = jnp.zeros_like(steps)
    steps[0:heads, :] = jnp.exp2(-codes[...].astype(F32))
    gate = gates[...]
    steps[6:7, :] = jnp.where(gate == 1, 1.0, 0.0).astype(F32)
    steps[7:8, :] = jnp.where(gate == 2, 1.0, 0.0).astype(F32)
    stacked = jnp.concatenate(
        [steps[:, j * CHUNK : (j + 1) * CHUNK] for j in range(chunks)], axis=0
    ).astype(BF16)
    row = lax.broadcasted_iota(jnp.int32, (CHUNK, CHUNK), 0)
    col = lax.broadcasted_iota(jnp.int32, (CHUNK, CHUNK), 1)
    upper = jnp.where(row <= col, 1.0, 0.0).astype(BF16)
    sums = dot(stacked, upper, ((1,), (0,)))
    sub = lax.broadcasted_iota(jnp.int32, (8, CHUNK), 0)
    rate = jnp.zeros((8, CHUNK), F32)
    for head in range(heads):
        rate = jnp.where(sub == head, rates[head], rate)
    cums, mids, befores = [], [], []
    before = jnp.zeros((8, 1), F32)
    for j in range(chunks):
        part = sums[8 * j : 8 * j + 8, :]
        cum = LOG_ONE * part[6:7, :] + LOG_TWO * part[7:8, :] - rate * part
        cums.append(cum)
        mids.append(cum[:, CHUNK // 2 - 1 : CHUNK // 2])
        befores.append(before)
        before = before + cum[:, CHUNK - 1 : CHUNK]
    for j in range(chunks):
        at = slice(j * CHUNK, (j + 1) * CHUNK)
        size = steps[:, at]
        near_out[0:16, at] = split_two(jnp.exp(cums[j] - mids[j]))
        near_out[16:32, at] = split_two(jnp.exp(mids[j] - cums[j]) * size)
        front_out[:, at] = split_two(jnp.exp(befores[j] + cums[j]))
        far_out[:, at] = split_two(jnp.exp(before - befores[j] - cums[j]) * size)
    lead_pair[...] = split_two(jnp.exp(-jnp.maximum(cums[0], -8.0)) * steps[:, 0:CHUNK])
    pick = lax.broadcasted_iota(jnp.int32, (8, CHUNK), 0)
    place = lax.broadcasted_iota(jnp.int32, (8, CHUNK), 1)
    chosen = jnp.where((pick == 0) | ((pick == 1) & (place < CHUNK // 2)), 1.0, 0.0)
    flat = dot(chosen.astype(BF16), stacked, ((1,), (1,)))
    owner = lax.broadcasted_iota(jnp.int32, (chunks, 8 * chunks), 1) >> 3
    chunk_at = lax.broadcasted_iota(jnp.int32, (chunks, 8 * chunks), 0)
    lane_rate = per_lane(rates, heads, channels)
    kind = lax.broadcasted_iota(jnp.int32, (8 * chunks, channels), 0) & 7
    lane = lax.broadcasted_iota(jnp.int32, (8 * chunks, channels), 1)
    lane_head = head_of(lane, channels // heads)
    mixer = jnp.where(kind == lane_head, -lane_rate, 0.0)
    mixer = jnp.where(kind == 6, LOG_ONE, jnp.where(kind == 7, LOG_TWO, mixer))
    table = []
    for which in range(2):
        own = jnp.where(owner == chunk_at, flat[which : which + 1, :], 0.0)
        table.append(dot(own, mixer, ((1,), (0,)), HIGHEST))
    whole = jnp.exp(table[0])
    middle = jnp.exp(table[1])
    rest_of = jnp.exp(table[0] - table[1])
    logs_out[0] = whole
    logs_out[1] = middle
    logs_out[2] = rest_of
    decay = jnp.exp(jnp.sum(table[0], axis=0, keepdims=True))
    first = decay.astype(BF16).astype(F32)
    extra[...] = jnp.zeros_like(extra)
    extra[0:1, :] = first
    extra[1:2, :] = decay - first

    onehot = spread_matrix(heads, channels)
    lead_out[...] = spread(lead_pair[:, 0:16], onehot)
    gain_out[...] = jnp.broadcast_to(per_lane(gains, heads, channels), (8, channels))
    for copy in copies[4:7]:
        copy.wait()
    shift = back_shift()
    nothing = jnp.zeros((16, channels), BF16)
    for at in range(0, rows, CHUNK):
        both = slice(at, at + CHUNK)
        if at == 0:
            block = jnp.concatenate([nothing, inputs[both, :]], axis=0)
        else:
            block = inputs[at - 16 : at + CHUNK, :]
        moved = dot(shift, block, ((1,), (0,)))
        preact = taps[3:4, :] * inputs[both, :].astype(F32)
        for k in range(3):
            preact = preact + taps[k : k + 1, :] * moved[k * CHUNK : (k + 1) * CHUNK, :]
        sigma = 0.5 * jnp.tanh(0.5 * preact) + 0.5
        mixed = preact * sigma
        scale = spread(far_out[:, both], onehot)
        sigma_out[both, :] = sigma
        mixed_out[both, :] = mixed
        scaled[both, :] = (mixed * scale).astype(BF16)
        if at == 0:
            extra[11:14, :] = scale[0:3, :]
    state = dot(b_proj[...], scaled[...], ((0,), (0,))).astype(BF16)
    extra[2:5, :] = inputs[0:16, :].astype(F32)[0:3, :]
    extra[5:8, :] = inputs[rows - 16 : rows, :].astype(F32)[13:16, :]
    extra[8:11, 0:STATE] = b_proj[0:16, :].astype(F32)[0:3, :]
    for copy in copies[7:]:
        copy.wait()
    for at in range(0, rows, STEP_ROWS):
        both = slice(at, at + STEP_ROWS)
        scale = spread(front_out[:, both], onehot)
        scaled[both, :] = (grad[both, :].astype(F32) * scale).astype(BF16)
    adjoint = dot(c_proj[...], scaled[...], ((0,), (0,))).astype(BF16)
    me = lax.axis_index("seq")
    for distance in range(1, parts):
        pay = pays[distance - 1]
        pay[0:STATE, :] = jnp.where(partner(me, distance, parts) > me, state, adjoint)
        pay[STATE : STATE + 16, :] = extra[...].astype(BF16)


def back_shift():
    row = lax.broadcasted_iota(jnp.int32, (3 * CHUNK, CHUNK + 16), 0)
    col = lax.broadcasted_iota(jnp.int32, (3 * CHUNK, CHUNK + 16), 1)
    at = (row & (CHUNK - 1)) + 13 + (row >> 7)
    return jnp.where(col == at, 1.0, 0.0).astype(BF16)


def tail_rows(held, source):
    return held[source, STATE : STATE + 16, :].astype(F32)


def first_preact(taps, halo, first):
    joined = jnp.concatenate([halo[0:3, :], first[0:8, :]], axis=0)
    preact = taps[0:1, :] * joined[0:8, :]
    for k in range(1, 4):
        preact = preact + taps[k : k + 1, :] * joined[k : k + 8, :]
    return preact


def first_change(taps, halo, first):
    true = first_preact(taps, halo, first)
    bare = first_preact(taps, jnp.zeros_like(halo), first)
    change = true * (0.5 * jnp.tanh(0.5 * true) + 0.5) - bare * (0.5 * jnp.tanh(0.5 * bare) + 0.5)
    row = lax.broadcasted_iota(jnp.int32, change.shape, 0)
    change = jnp.where(row < 3, change, 0.0)
    return jnp.concatenate([change, jnp.zeros_like(change)], axis=0)


def lane_tiles(channels):
    return [slice(at, min(at + 128, channels)) for at in range(0, channels, 128)]


def partner(me, distance, parts):
    return (me ^ distance) if parts & (parts - 1) == 0 else (me + distance) % parts


def sender(me, distance, parts):
    return (me ^ distance) if parts & (parts - 1) == 0 else (me + parts - distance) % parts


def sort_blocks(parts, pays, held):
    me = lax.axis_index("seq")
    held[me] = jnp.zeros(held.shape[1:], BF16)
    for distance in range(1, parts):
        held[sender(me, distance, parts)] = pays[distance - 1][...]


def merged_adjoint(parts, held):
    me = lax.axis_index("seq")
    running = jnp.zeros((STATE, held.shape[2]), F32)
    for source in range(parts - 1, 0, -1):
        tail = tail_rows(held, source)
        decay = tail[0:1, :] + tail[1:2, :]
        block = held[source, 0:STATE, :].astype(F32)
        running = jnp.where(source > me, block + decay * running, running)
    return running.astype(BF16)


def own_halo(held):
    me = lax.axis_index("seq")
    return jnp.where(me > 0, tail_rows(held, jnp.maximum(me - 1, 0))[5:8, :], 0.0)


def merged_state(parts, taps, held):
    me = lax.axis_index("seq")
    channels = held.shape[2]
    running = jnp.zeros((STATE, channels), F32)
    blank = jnp.zeros((5, channels), F32)
    tails = [tail_rows(held, source) for source in range(parts - 1)]
    for source in range(parts - 1):
        tail = tails[source]
        state = held[source, 0:STATE, :].astype(F32)
        if source > 0:
            first = jnp.concatenate([tail[2:5, :], blank], axis=0)
            scale = jnp.concatenate([tail[11:14, :], blank, blank, blank[0:3, :]], axis=0)
            change = first_change(taps, tails[source - 1][5:8, :], first)
            change = (change * scale).astype(BF16)
            row = lax.broadcasted_iota(jnp.int32, (16, STATE), 0)
            lines = jnp.concatenate([tail[8:11, 0:STATE], blank[:, 0:STATE]], axis=0)
            lines = jnp.concatenate([lines, jnp.zeros_like(lines)], axis=0)
            lines = jnp.where(row < 3, lines, 0.0).astype(BF16)
            state = state + dot(lines, change, ((0,), (0,)))
        decay = tail[0:1, :] + tail[1:2, :]
        running = jnp.where(source < me, state + decay * running, running)
    return running


def inner_kernel(
    heads, gains, near, far, logs, grad, mixed, sigma, b_proj, c_proj,
    inputs, base_out, grad_base, grad_weight, first_out, moved_out,
    ahead_scores, behind_scores, mixed_scaled, mixed_low, grad_scaled, grad_low,
    mixed_fresh, grad_fresh,
):
    rows, channels = grad.shape
    chunks = rows // CHUNK
    blocks = [slice(j * CHUNK, (j + 1) * CHUNK) for j in range(chunks)]
    row = lax.broadcasted_iota(jnp.int32, (CHUNK, CHUNK), 0)
    col = lax.broadcasted_iota(jnp.int32, (CHUNK, CHUNK), 1)
    onehot = spread_matrix(heads, channels)
    gain = gains[0:1, :]
    for both in blocks:
        scale = spread(near[0:16, both], onehot)
        grad_scaled[both, :] = (grad[both, :].astype(F32) * scale).astype(BF16)
    for both in blocks:
        scale = spread(near[16:32, both], onehot)
        mixed_scaled[both, :] = (mixed[both, :] * scale).astype(BF16)
    for both in blocks:
        grad_fresh[both, :] = dot(c_proj[both, :], grad_scaled[both, :], ((0,), (0,)))
    for both in blocks:
        mixed_fresh[both, :] = dot(b_proj[both, :], mixed_scaled[both, :], ((0,), (0,)))
    for both in blocks:
        ahead = dot(c_proj[both, :], b_proj[both, :], ((1,), (1,)))
        ahead_scores[both, :] = jnp.where(row >= col, ahead, 0.0).astype(BF16)
    for both in blocks:
        behind = dot(b_proj[both, :], c_proj[both, :], ((1,), (1,)))
        behind_scores[both, :] = jnp.where(row <= col, behind, 0.0).astype(BF16)
    for lanes in lane_tiles(channels):
        adjoint = jnp.zeros((STATE, lanes.stop - lanes.start), F32)
        for j in range(chunks - 1, -1, -1):
            grad_low[blocks[j], lanes] = (adjoint * logs[2, j : j + 1, lanes]).astype(BF16)
            adjoint = logs[0, j : j + 1, lanes] * adjoint + (
                logs[1, j : j + 1, lanes] * grad_fresh[blocks[j], lanes]
            )
        state = jnp.zeros((STATE, lanes.stop - lanes.start), F32)
        for j in range(chunks):
            mixed_low[blocks[j], lanes] = (state * logs[1, j : j + 1, lanes]).astype(BF16)
            state = logs[0, j : j + 1, lanes] * state + (
                logs[2, j : j + 1, lanes] * mixed_fresh[blocks[j], lanes]
            )
    for both in blocks:
        inner = dot(
            jnp.concatenate([behind_scores[both, :], b_proj[both, :]], axis=1),
            jnp.concatenate([grad_scaled[both, :], grad_low[both, :]], axis=0),
            ((1,), (0,)),
        )
        slope = sigma[both, :] + mixed[both, :] * (1.0 - sigma[both, :])
        inner = gain * grad[both, :].astype(F32) + spread(near[16:32, both], onehot) * inner
        weight = spread(far[:, both], onehot)
        grad_base[both, :] = slope * inner
        grad_weight[both, :] = slope * weight
        if both.start == 0:
            first_out[0:8, :] = inner[0:8, :]
            first_out[8:16, :] = weight[0:8, :]
    for both in blocks:
        inner = dot(
            jnp.concatenate([ahead_scores[both, :], c_proj[both, :]], axis=1),
            jnp.concatenate([mixed_scaled[both, :], mixed_low[both, :]], axis=0),
            ((1,), (0,)),
        )
        base_out[both, :] = gain * mixed[both, :] + spread(near[0:16, both], onehot) * inner
    shift = back_shift()
    for both in blocks:
        if both.start == 0:
            nothing = jnp.zeros((16, channels), BF16)
            block = jnp.concatenate([nothing, inputs[both, :]], axis=0)
        else:
            block = inputs[both.start - 16 : both.stop, :]
        moved = dot(shift, block, ((1,), (0,)))
        for k in range(3):
            moved_out[k, both, :] = moved[k * CHUNK : (k + 1) * CHUNK, :].astype(BF16)


def gradient_kernel(parts, taps, base, weight, unscaled, inputs, moved, b_proj, *rest):
    pays = rest[: parts - 1]
    exact, window, tail_out, held, products = rest[parts - 1 :]
    rows, channels = base.shape
    chunks = rows // CHUNK
    sort_blocks(parts, pays, held)
    adjoint = merged_adjoint(parts, held)
    halo = own_halo(held)
    preact = first_preact(taps, halo, inputs[0:16, :].astype(F32))
    sigma = 0.5 * jnp.tanh(0.5 * preact) + 0.5
    slope = sigma + preact * sigma * (1.0 - sigma)
    window[rows : rows + 16, :] = jnp.zeros((16, channels), BF16)
    for j in range(chunks):
        both = slice(j * CHUNK, (j + 1) * CHUNK)
        carried = dot(b_proj[both, :], adjoint, ((1,), (0,)))
        grad_pre = base[both, :] + weight[both, :] * carried
        if j == 0:
            first = slope * (unscaled[0:8, :] + unscaled[8:16, :] * carried[0:8, :])
            grad_pre = jnp.concatenate([first, grad_pre[8:, :]], axis=0)
        exact[both, :] = grad_pre
        low = grad_pre.astype(BF16)
        window[both, :] = low
        for k in range(3):
            products[k, both, :] = low * moved[k, both, :]
        products[3, both, :] = low * inputs[both, :]
    ones = jnp.ones((8, rows), BF16)
    for k in range(4):
        tap = dot(ones, products[k], ((1,), (0,)))[0:1, :]
        for j in range(k, 3):
            tap = tap + first[j - k : j - k + 1, :] * halo[j : j + 1, :]
        tail_out[k : k + 1, :] = tap
    tail_out[4:7, :] = first[0:3, :]
    tail_out[7:8, :] = jnp.zeros((1, channels), F32)


def output_kernel(
    heads, parts, gains, taps, front, lead, base, inputs, b_proj, c_proj, exact, window, *rest
):
    pays = rest[: parts - 1]
    out_hbm, grad_hbm, edge_out, held, result_rows, grad_rows, sems, grad_sems = rest[parts - 1 :]
    rows, channels = base.shape
    sort_blocks(parts, pays, held)
    incoming = merged_state(parts, taps, held)
    onehot = spread_matrix(heads, channels)
    change = first_change(taps, own_halo(held), inputs[0:16, :].astype(F32))
    change_scaled = (change * lead[...]).astype(BF16)
    state = incoming + dot(b_proj[0:16, :], change_scaled, ((0,), (0,)))
    state = state.astype(BF16)
    row = lax.broadcasted_iota(jnp.int32, (16, 16), 0)
    col = lax.broadcasted_iota(jnp.int32, (16, 16), 1)
    scores = dot(c_proj[0:16, :], b_proj[0:16, :], ((1,), (1,)))
    scores = jnp.where(row >= col, scores, 0.0).astype(BF16)
    top = dot(c_proj[0:16, :], incoming.astype(BF16), ((1,), (0,)))
    top = top + dot(scores, change_scaled, ((1,), (0,)))
    top = top * spread(front[:, 0:16], onehot) + base[0:16, :]
    top = top + gains[0:1, :] * change
    row = lax.broadcasted_iota(jnp.int32, (3 * CHUNK, CHUNK + 16), 0)
    col = lax.broadcasted_iota(jnp.int32, (3 * CHUNK, CHUNK + 16), 1)
    shift = jnp.where(col == (row & (CHUNK - 1)) + 3 - (row >> 7), 1.0, 0.0).astype(BF16)
    copies = []
    for piece in range(rows // STEP_ROWS):
        for at in range(piece * STEP_ROWS, (piece + 1) * STEP_ROWS, CHUNK):
            both = slice(at, at + CHUNK)
            moved = dot(shift, window[at : at + CHUNK + 16, :], ((1,), (0,)))
            result = taps[3:4, :] * exact[both, :]
            for k in range(3):
                result = result + taps[k : k + 1, :] * moved[k * CHUNK : (k + 1) * CHUNK, :]
            grad_rows[both, :] = result.astype(BF16)
            if at + CHUNK == rows:
                edge_out[...] = result[CHUNK - 16 :, :]
            carried = dot(c_proj[both, :], state, ((1,), (0,)))
            result = base[both, :] + spread(front[:, both], onehot) * carried
            result_rows[both, :] = result.astype(BF16)
            if at == 0:
                result_rows[0:16, :] = top.astype(BF16)
        place = pl.ds(piece * STEP_ROWS, STEP_ROWS)
        copy = pltpu.make_async_copy(result_rows.at[place], out_hbm.at[place], sems.at[piece])
        copy.start()
        copies.append(copy)
        copy = pltpu.make_async_copy(
            grad_rows.at[place], grad_hbm.at[place], grad_sems.at[piece]
        )
        copy.start()
        copies.append(copy)
    for copy in copies:
        copy.wait()


def finish_kernel(parts, scale, taps, tail, edge, *rest):
    others = rest[: parts - 1]
    unused, grad_hbm, conv_out, rows_low, sem = rest[parts - 1 :]
    channels = tail.shape[1]
    me = lax.axis_index("seq")
    after = jnp.zeros(tail.shape, F32)
    for distance in range(1, parts):
        here = sender(me, distance, parts) == me + 1
        after = jnp.where(here, others[distance - 1][...], after)
    row = lax.broadcasted_iota(jnp.int32, (16, channels), 0)
    result = edge[...]
    for r in range(3):
        extra = jnp.zeros((1, channels), F32)
        for k in range(r + 1):
            extra = extra + taps[k : k + 1, :] * after[4 + r - k : 5 + r - k, :]
        result = jnp.where(row == 13 + r, result + extra, result)
    rows_low[...] = result.astype(BF16)
    rows = grad_hbm.shape[0]
    copy = pltpu.make_async_copy(rows_low, grad_hbm.at[pl.ds(rows - 16, 16)], sem)
    copy.start()
    total = tail[0:4, :]
    for other in others:
        total = total + other[0:4, :]
    conv_out[...] = total * scale
    copy.wait()


def rotated(block, axis, distance):
    size = lax.axis_size(axis)
    return lax.ppermute(block, axis, [(i, partner(i, distance, size)) for i in range(size)])


def shards(
    inputs,
    b_proj,
    c_proj,
    step_codes,
    gate_codes,
    decay_rates,
    skip_gain,
    conv_weight,
    out_cotangent,
):
    rows, channels = inputs.shape
    heads = decay_rates.shape[0]
    parts = lax.axis_size("seq")
    chunks = rows // CHUNK
    pieces = rows // STEP_ROWS
    hbm = pl.BlockSpec(memory_space=pltpu.HBM)
    vmem = pl.BlockSpec(memory_space=pltpu.VMEM)
    shape = jax.ShapeDtypeStruct
    dma = pltpu.SemaphoreType.DMA
    big = rows * channels

    def call(kernel, in_specs, out_specs, out_shape, scratch, products, aliases=None):
        return pl.pallas_call(
            kernel,
            in_specs=in_specs,
            out_specs=out_specs,
            out_shape=out_shape,
            scratch_shapes=scratch,
            input_output_aliases=aliases or {},
            compiler_params=pltpu.CompilerParams(vmem_limit_bytes=VMEM_LIMIT),
            cost_estimate=pl.CostEstimate(
                flops=products * 2 * big * 128, bytes_accessed=6 * big, transcendentals=big
            ),
        )

    def stay(array):
        return pltpu.with_memory_space_constraint(array, pltpu.HBM)

    pay = shape((STATE + 16, channels), BF16)
    narrow = shape((rows, channels), BF16)
    broad = shape((rows, channels), F32)
    slim = shape((rows, STATE), BF16)

    outs = call(
        functools.partial(reduce_kernel, heads, parts),
        [hbm] * 9,
        [vmem] * (11 + parts),
        [
            shape((32, rows), BF16),
            shape((16, rows), BF16),
            shape((16, rows), BF16),
            shape((3, chunks, channels), F32),
            shape((16, channels), F32),
            shape((8, channels), F32),
            broad,
            broad,
            narrow,
            slim,
            narrow,
            slim,
        ]
        + [pay] * (parts - 1),
        [
            pltpu.SMEM((heads,), F32),
            pltpu.SMEM((heads,), F32),
            pltpu.VMEM((heads, rows), jnp.int32),
            pltpu.VMEM((1, rows), jnp.int32),
            pltpu.VMEM((4, channels), F32),
            pltpu.VMEM((8, rows), F32),
            pltpu.VMEM((rows, channels), BF16),
            pltpu.VMEM((16, CHUNK), BF16),
            pltpu.VMEM((16, channels), F32),
            dma((9,)),
        ],
        4,
    )(
        stay(decay_rates),
        stay(skip_gain),
        stay(step_codes),
        stay(gate_codes.reshape(1, rows)),
        stay(conv_weight),
        stay(inputs),
        stay(b_proj),
        stay(out_cotangent),
        stay(c_proj),
    )
    near, far, front, logs, lead, gain, mixed, sigma = outs[:8]
    inputs, b_proj, out_cotangent, c_proj = outs[8:12]
    pays = [rotated(send, "seq", distance + 1) for distance, send in enumerate(outs[12:])]

    tile = pltpu.VMEM((rows, CHUNK), BF16)
    low = pltpu.VMEM((rows, channels), BF16)
    high = pltpu.VMEM((rows, channels), F32)
    base, grad_base, grad_weight, unscaled, moved = call(
        functools.partial(inner_kernel, heads),
        [vmem] * 10,
        [vmem] * 5,
        [broad] * 3 + [shape((16, channels), F32), shape((3, rows, channels), BF16)],
        [tile, tile, low, low, low, low, high, high],
        10,
    )(gain, near, far, logs, out_cotangent, mixed, sigma, b_proj, c_proj, inputs)

    held = pltpu.VMEM((parts, STATE + 16, channels), BF16)
    exact, window, tail = call(
        functools.partial(gradient_kernel, parts),
        [vmem] * (6 + parts),
        [vmem] * 3,
        [broad, shape((rows + 16, channels), BF16), shape((8, channels), F32)],
        [held, pltpu.VMEM((4, rows, channels), BF16)],
        2,
    )(conv_weight, grad_base, grad_weight, unscaled, inputs, moved, b_proj, *pays)
    tails = [rotated(tail, "seq", distance) for distance in range(1, parts)]

    layer_out, grad_rows, edge = call(
        functools.partial(output_kernel, heads, parts),
        [vmem] * (9 + parts),
        [hbm, hbm, vmem],
        [narrow, narrow, shape((16, channels), F32)],
        [held, low, low, dma((pieces,)), dma((pieces,))],
        4,
    )(gain, conv_weight, front, lead, base, inputs, b_proj, c_proj, exact, window, *pays)

    scale = float((rows * parts) ** -0.5)
    input_grad, conv_grad = call(
        functools.partial(finish_kernel, parts, scale),
        [vmem] * (2 + parts) + [hbm],
        [hbm, vmem],
        [narrow, shape((4, channels), F32)],
        [pltpu.VMEM((16, channels), BF16), dma],
        0,
        {parts + 2: 0},
    )(conv_weight, tail, edge, *tails, grad_rows)
    return layer_out, input_grad, conv_grad


def solution(mesh):
    in_specs = (
        P(("groups", "seq"), ("head", "sub")),
        P(("groups", "seq"), None),
        P(("groups", "seq"), None),
        P(("head", "sub"), ("groups", "seq")),
        P(("groups", "seq")),
        P(("head", "sub")),
        P(("head", "sub")),
        P(None, ("head", "sub")),
        P(("groups", "seq"), ("head", "sub")),
    )
    out_specs = (
        P(("groups", "seq"), ("head", "sub")),
        P(("groups", "seq"), ("head", "sub")),
        P("groups", ("head", "sub")),
    )
    return jax.shard_map(shards, mesh=mesh, in_specs=in_specs, out_specs=out_specs, check_vma=False)
```

```python
import functools

import jax
import jax.numpy as jnp
from jax import lax
from jax.experimental import pallas as pl
from jax.experimental.pallas import tpu as pltpu
from jax.sharding import PartitionSpec as P

CHUNK = 128
STATE = 128
STEP_ROWS = 512
LOG_ONE = -0.2876820724517809
LOG_TWO = -0.6931471805599453
F32 = jnp.float32
BF16 = jnp.bfloat16
HIGHEST = lax.Precision.HIGHEST
VMEM_LIMIT = 20 * 1024 * 1024


def dot(a, b, dims, precision=None):
    return lax.dot_general(a, b, (dims, ((), ())), preferred_element_type=F32, precision=precision)


def per_lane(scalars, count, channels):
    width = channels // count
    lane = lax.broadcasted_iota(jnp.int32, (1, channels), 1)
    row = jnp.zeros((1, channels), F32)
    for head in range(count):
        inside = (lane >= head * width) & (lane < (head + 1) * width)
        row = jnp.where(inside, scalars[head], row)
    return row


def split_two(value):
    high = value.astype(BF16)
    low = (value - high.astype(F32)).astype(BF16)
    return jnp.concatenate([high.astype(F32), low.astype(F32)], axis=0).astype(BF16)


def head_of(lane, width):
    if width & (width - 1) == 0:
        return lane >> (width.bit_length() - 1)
    return lane // width


def spread_matrix(count, channels):
    width = channels // count
    row = lax.broadcasted_iota(jnp.int32, (16, channels), 0)
    lane = lax.broadcasted_iota(jnp.int32, (16, channels), 1)
    return jnp.where((row & 7) == head_of(lane, width), 1.0, 0.0).astype(BF16)


def spread(pair, onehot):
    return dot(pair, onehot, ((0,), (0,)))


def reduce_kernel(
    heads, parts,
    rates_hbm, gains_hbm, codes_hbm, gates_hbm, taps_hbm, inputs_hbm, b_hbm, grad_hbm, c_hbm,
    near_out, far_out, front_out, logs_out, lead_out, gain_out, mixed_out, sigma_out,
    inputs, b_proj, grad, c_proj, *rest
):
    pays = rest[: parts - 1]
    rates, gains, codes, gates, taps, steps, scaled, lead_pair, extra, sems = rest[parts - 1 :]
    rows, channels = grad.shape
    chunks = rows // CHUNK
    sources = (
        rates_hbm, gains_hbm, codes_hbm, gates_hbm, taps_hbm, inputs_hbm, b_hbm, grad_hbm, c_hbm
    )
    targets = (rates, gains, codes, gates, taps, inputs, b_proj, grad, c_proj)
    copies = [
        pltpu.make_async_copy(source, target, sems.at[i])
        for i, (source, target) in enumerate(zip(sources, targets))
    ]
    for copy in copies:
        copy.start()
    for copy in copies[:4]:
        copy.wait()

    steps[...] = jnp.zeros_like(steps)
    steps[0:heads, :] = jnp.exp2(-codes[...].astype(F32))
    gate = gates[...]
    steps[6:7, :] = jnp.where(gate == 1, 1.0, 0.0).astype(F32)
    steps[7:8, :] = jnp.where(gate == 2, 1.0, 0.0).astype(F32)
    stacked = jnp.concatenate(
        [steps[:, j * CHUNK : (j + 1) * CHUNK] for j in range(chunks)], axis=0
    ).astype(BF16)
    row = lax.broadcasted_iota(jnp.int32, (CHUNK, CHUNK), 0)
    col = lax.broadcasted_iota(jnp.int32, (CHUNK, CHUNK), 1)
    upper = jnp.where(row <= col, 1.0, 0.0).astype(BF16)
    sums = dot(stacked, upper, ((1,), (0,)))
    sub = lax.broadcasted_iota(jnp.int32, (8, CHUNK), 0)
    rate = jnp.zeros((8, CHUNK), F32)
    for head in range(heads):
        rate = jnp.where(sub == head, rates[head], rate)
    cums, mids, befores = [], [], []
    before = jnp.zeros((8, 1), F32)
    for j in range(chunks):
        part = sums[8 * j : 8 * j + 8, :]
        cum = LOG_ONE * part[6:7, :] + LOG_TWO * part[7:8, :] - rate * part
        cums.append(cum)
        mids.append(cum[:, CHUNK // 2 - 1 : CHUNK // 2])
        befores.append(before)
        before = before + cum[:, CHUNK - 1 : CHUNK]
    for j in range(chunks):
        at = slice(j * CHUNK, (j + 1) * CHUNK)
        size = steps[:, at]
        near_out[0:16, at] = split_two(jnp.exp(cums[j] - mids[j]))
        near_out[16:32, at] = split_two(jnp.exp(mids[j] - cums[j]) * size)
        front_out[:, at] = split_two(jnp.exp(befores[j] + cums[j]))
        far_out[:, at] = split_two(jnp.exp(before - befores[j] - cums[j]) * size)
    lead_pair[...] = split_two(jnp.exp(-jnp.maximum(cums[0], -8.0)) * steps[:, 0:CHUNK])
    pick = lax.broadcasted_iota(jnp.int32, (8, CHUNK), 0)
    place = lax.broadcasted_iota(jnp.int32, (8, CHUNK), 1)
    chosen = jnp.where((pick == 0) | ((pick == 1) & (place < CHUNK // 2)), 1.0, 0.0)
    flat = dot(chosen.astype(BF16), stacked, ((1,), (1,)))
    owner = lax.broadcasted_iota(jnp.int32, (chunks, 8 * chunks), 1) >> 3
    chunk_at = lax.broadcasted_iota(jnp.int32, (chunks, 8 * chunks), 0)
    lane_rate = per_lane(rates, heads, channels)
    kind = lax.broadcasted_iota(jnp.int32, (8 * chunks, channels), 0) & 7
    lane = lax.broadcasted_iota(jnp.int32, (8 * chunks, channels), 1)
    lane_head = head_of(lane, channels // heads)
    mixer = jnp.where(kind == lane_head, -lane_rate, 0.0)
    mixer = jnp.where(kind == 6, LOG_ONE, jnp.where(kind == 7, LOG_TWO, mixer))
    table = []
    for which in range(2):
        own = jnp.where(owner == chunk_at, flat[which : which + 1, :], 0.0)
        table.append(dot(own, mixer, ((1,), (0,)), HIGHEST))
    whole = jnp.exp(table[0])
    middle = jnp.exp(table[1])
    rest_of = jnp.exp(table[0] - table[1])
    logs_out[0] = whole
    logs_out[1] = middle
    logs_out[2] = rest_of
    decay = jnp.exp(jnp.sum(table[0], axis=0, keepdims=True))
    first = decay.astype(BF16).astype(F32)
    extra[...] = jnp.zeros_like(extra)
    extra[0:1, :] = first
    extra[1:2, :] = decay - first

    onehot = spread_matrix(heads, channels)
    lead_out[...] = spread(lead_pair[:, 0:16], onehot)
    gain_out[...] = jnp.broadcast_to(per_lane(gains, heads, channels), (8, channels))
    for copy in copies[4:7]:
        copy.wait()
    shift = back_shift()
    nothing = jnp.zeros((16, channels), BF16)
    for at in range(0, rows, CHUNK):
        both = slice(at, at + CHUNK)
        if at == 0:
            block = jnp.concatenate([nothing, inputs[both, :]], axis=0)
        else:
            block = inputs[at - 16 : at + CHUNK, :]
        moved = dot(shift, block, ((1,), (0,)))
        preact = taps[3:4, :] * inputs[both, :].astype(F32)
        for k in range(3):
            preact = preact + taps[k : k + 1, :] * moved[k * CHUNK : (k + 1) * CHUNK, :]
        sigma = 0.5 * jnp.tanh(0.5 * preact) + 0.5
        mixed = preact * sigma
        scale = spread(far_out[:, both], onehot)
        sigma_out[both, :] = sigma
        mixed_out[both, :] = mixed
        scaled[both, :] = (mixed * scale).astype(BF16)
        if at == 0:
            extra[11:14, :] = scale[0:3, :]
    state = dot(b_proj[...], scaled[...], ((0,), (0,))).astype(BF16)
    extra[2:5, :] = inputs[0:16, :].astype(F32)[0:3, :]
    extra[5:8, :] = inputs[rows - 16 : rows, :].astype(F32)[13:16, :]
    extra[8:11, 0:STATE] = b_proj[0:16, :].astype(F32)[0:3, :]
    for copy in copies[7:]:
        copy.wait()
    for at in range(0, rows, STEP_ROWS):
        both = slice(at, at + STEP_ROWS)
        scale = spread(front_out[:, both], onehot)
        scaled[both, :] = (grad[both, :].astype(F32) * scale).astype(BF16)
    adjoint = dot(c_proj[...], scaled[...], ((0,), (0,))).astype(BF16)
    me = lax.axis_index("seq")
    for distance in range(1, parts):
        pay = pays[distance - 1]
        pay[0:STATE, :] = jnp.where(partner(me, distance, parts) > me, state, adjoint)
        pay[STATE : STATE + 16, :] = extra[...].astype(BF16)


def back_shift():
    row = lax.broadcasted_iota(jnp.int32, (3 * CHUNK, CHUNK + 16), 0)
    col = lax.broadcasted_iota(jnp.int32, (3 * CHUNK, CHUNK + 16), 1)
    at = (row & (CHUNK - 1)) + 13 + (row >> 7)
    return jnp.where(col == at, 1.0, 0.0).astype(BF16)


def tail_rows(held, source):
    return held[source, STATE : STATE + 16, :].astype(F32)


def first_preact(taps, halo, first):
    joined = jnp.concatenate([halo[0:3, :], first[0:8, :]], axis=0)
    preact = taps[0:1, :] * joined[0:8, :]
    for k in range(1, 4):
        preact = preact + taps[k : k + 1, :] * joined[k : k + 8, :]
    return preact


def first_change(taps, halo, first):
    true = first_preact(taps, halo, first)
    bare = first_preact(taps, jnp.zeros_like(halo), first)
    change = true * (0.5 * jnp.tanh(0.5 * true) + 0.5) - bare * (0.5 * jnp.tanh(0.5 * bare) + 0.5)
    row = lax.broadcasted_iota(jnp.int32, change.shape, 0)
    change = jnp.where(row < 3, change, 0.0)
    return jnp.concatenate([change, jnp.zeros_like(change)], axis=0)


def lane_tiles(channels):
    return [slice(at, min(at + 128, channels)) for at in range(0, channels, 128)]


def partner(me, distance, parts):
    return (me ^ distance) if parts & (parts - 1) == 0 else (me + distance) % parts


def sender(me, distance, parts):
    return (me ^ distance) if parts & (parts - 1) == 0 else (me + parts - distance) % parts


def sort_blocks(parts, pays, held):
    me = lax.axis_index("seq")
    held[me] = jnp.zeros(held.shape[1:], BF16)
    for distance in range(1, parts):
        held[sender(me, distance, parts)] = pays[distance - 1][...]


def merged_adjoint(parts, held):
    me = lax.axis_index("seq")
    running = jnp.zeros((STATE, held.shape[2]), F32)
    for source in range(parts - 1, 0, -1):
        tail = tail_rows(held, source)
        decay = tail[0:1, :] + tail[1:2, :]
        block = held[source, 0:STATE, :].astype(F32)
        running = jnp.where(source > me, block + decay * running, running)
    return running.astype(BF16)


def own_halo(held):
    me = lax.axis_index("seq")
    return jnp.where(me > 0, tail_rows(held, jnp.maximum(me - 1, 0))[5:8, :], 0.0)


def merged_state(parts, taps, held):
    me = lax.axis_index("seq")
    channels = held.shape[2]
    running = jnp.zeros((STATE, channels), F32)
    blank = jnp.zeros((5, channels), F32)
    tails = [tail_rows(held, source) for source in range(parts - 1)]
    for source in range(parts - 1):
        tail = tails[source]
        state = held[source, 0:STATE, :].astype(F32)
        if source > 0:
            first = jnp.concatenate([tail[2:5, :], blank], axis=0)
            scale = jnp.concatenate([tail[11:14, :], blank, blank, blank[0:3, :]], axis=0)
            change = first_change(taps, tails[source - 1][5:8, :], first)
            change = (change * scale).astype(BF16)
            row = lax.broadcasted_iota(jnp.int32, (16, STATE), 0)
            lines = jnp.concatenate([tail[8:11, 0:STATE], blank[:, 0:STATE]], axis=0)
            lines = jnp.concatenate([lines, jnp.zeros_like(lines)], axis=0)
            lines = jnp.where(row < 3, lines, 0.0).astype(BF16)
            state = state + dot(lines, change, ((0,), (0,)))
        decay = tail[0:1, :] + tail[1:2, :]
        running = jnp.where(source < me, state + decay * running, running)
    return running


def inner_kernel(
    heads, gains, near, far, logs, grad, mixed, sigma, b_proj, c_proj,
    base_out, grad_base, grad_weight, first_out,
    ahead_scores, behind_scores, mixed_scaled, mixed_low, grad_scaled, grad_low,
    mixed_fresh, grad_fresh,
):
    rows, channels = grad.shape
    chunks = rows // CHUNK
    blocks = [slice(j * CHUNK, (j + 1) * CHUNK) for j in range(chunks)]
    row = lax.broadcasted_iota(jnp.int32, (CHUNK, CHUNK), 0)
    col = lax.broadcasted_iota(jnp.int32, (CHUNK, CHUNK), 1)
    onehot = spread_matrix(heads, channels)
    gain = gains[0:1, :]
    for both in blocks:
        scale = spread(near[0:16, both], onehot)
        grad_scaled[both, :] = (grad[both, :].astype(F32) * scale).astype(BF16)
    for both in blocks:
        scale = spread(near[16:32, both], onehot)
        mixed_scaled[both, :] = (mixed[both, :] * scale).astype(BF16)
    for both in blocks:
        grad_fresh[both, :] = dot(c_proj[both, :], grad_scaled[both, :], ((0,), (0,)))
    for both in blocks:
        mixed_fresh[both, :] = dot(b_proj[both, :], mixed_scaled[both, :], ((0,), (0,)))
    for both in blocks:
        ahead = dot(c_proj[both, :], b_proj[both, :], ((1,), (1,)))
        ahead_scores[both, :] = jnp.where(row >= col, ahead, 0.0).astype(BF16)
    for both in blocks:
        behind = dot(b_proj[both, :], c_proj[both, :], ((1,), (1,)))
        behind_scores[both, :] = jnp.where(row <= col, behind, 0.0).astype(BF16)
    for lanes in lane_tiles(channels):
        adjoint = jnp.zeros((STATE, lanes.stop - lanes.start), F32)
        for j in range(chunks - 1, -1, -1):
            grad_low[blocks[j], lanes] = (adjoint * logs[2, j : j + 1, lanes]).astype(BF16)
            adjoint = logs[0, j : j + 1, lanes] * adjoint + (
                logs[1, j : j + 1, lanes] * grad_fresh[blocks[j], lanes]
            )
        state = jnp.zeros((STATE, lanes.stop - lanes.start), F32)
        for j in range(chunks):
            mixed_low[blocks[j], lanes] = (state * logs[1, j : j + 1, lanes]).astype(BF16)
            state = logs[0, j : j + 1, lanes] * state + (
                logs[2, j : j + 1, lanes] * mixed_fresh[blocks[j], lanes]
            )
    for both in blocks:
        inner = dot(
            jnp.concatenate([behind_scores[both, :], b_proj[both, :]], axis=1),
            jnp.concatenate([grad_scaled[both, :], grad_low[both, :]], axis=0),
            ((1,), (0,)),
        )
        slope = sigma[both, :] + mixed[both, :] * (1.0 - sigma[both, :])
        inner = gain * grad[both, :].astype(F32) + spread(near[16:32, both], onehot) * inner
        weight = spread(far[:, both], onehot)
        grad_base[both, :] = slope * inner
        grad_weight[both, :] = slope * weight
        if both.start == 0:
            first_out[0:8, :] = inner[0:8, :]
            first_out[8:16, :] = weight[0:8, :]
    for both in blocks:
        inner = dot(
            jnp.concatenate([ahead_scores[both, :], c_proj[both, :]], axis=1),
            jnp.concatenate([mixed_scaled[both, :], mixed_low[both, :]], axis=0),
            ((1,), (0,)),
        )
        base_out[both, :] = gain * mixed[both, :] + spread(near[0:16, both], onehot) * inner


def gradient_kernel(parts, taps, base, weight, unscaled, inputs, b_proj, *rest):
    pays = rest[: parts - 1]
    grad_out, tail_out, edge_out, window, exact, held = rest[parts - 1 :]
    rows, channels = base.shape
    chunks = rows // CHUNK
    sort_blocks(parts, pays, held)
    adjoint = merged_adjoint(parts, held)
    halo = own_halo(held)
    preact = first_preact(taps, halo, inputs[0:16, :].astype(F32))
    sigma = 0.5 * jnp.tanh(0.5 * preact) + 0.5
    slope = sigma + preact * sigma * (1.0 - sigma)
    window[rows : rows + 16, :] = jnp.zeros((16, channels), BF16)
    row = lax.broadcasted_iota(jnp.int32, (3 * CHUNK, CHUNK + 16), 0)
    col = lax.broadcasted_iota(jnp.int32, (3 * CHUNK, CHUNK + 16), 1)
    shift = jnp.where(col == (row & (CHUNK - 1)) + 3 - (row >> 7), 1.0, 0.0).astype(BF16)
    partial = [jnp.zeros((8, channels), F32) for _ in range(4)]
    for j in range(chunks):
        both = slice(j * CHUNK, (j + 1) * CHUNK)
        carried = dot(b_proj[both, :], adjoint, ((1,), (0,)))
        grad_pre = base[both, :] + weight[both, :] * carried
        if j == 0:
            first = slope * (unscaled[0:8, :] + unscaled[8:16, :] * carried[0:8, :])
            grad_pre = jnp.concatenate([first, grad_pre[8:, :]], axis=0)
        window[both, :] = grad_pre.astype(BF16)
        exact[both, :] = grad_pre
    for j in range(chunks):
        at = j * CHUNK
        both = slice(at, at + CHUNK)
        grad_pre = exact[both, :]
        moved = dot(shift, window[at : at + CHUNK + 16, :], ((1,), (0,)))
        x = inputs[both, :].astype(F32)
        result = taps[3:4, :] * grad_pre
        partial[3] = partial[3] + (grad_pre * x).reshape(CHUNK // 8, 8, channels).sum(axis=0)
        for k in range(3):
            part = moved[k * CHUNK : (k + 1) * CHUNK, :]
            result = result + taps[k : k + 1, :] * part
            partial[k] = partial[k] + (part * x).reshape(CHUNK // 8, 8, channels).sum(axis=0)
        grad_out[both, :] = result.astype(BF16)
        if j == chunks - 1:
            edge_out[...] = result[CHUNK - 16 :, :]
    for k in range(4):
        tap = jnp.sum(partial[k], axis=0, keepdims=True)
        for j in range(k, 3):
            tap = tap + first[j - k : j - k + 1, :] * halo[j : j + 1, :]
        tail_out[k : k + 1, :] = tap
    tail_out[4:7, :] = first[0:3, :]
    tail_out[7:8, :] = jnp.zeros((1, channels), F32)


def output_kernel(
    heads, parts, gains, taps, front, lead, base, inputs, b_proj, c_proj, grad_rows, *rest
):
    pays = rest[: parts - 1]
    out_hbm, grad_hbm, held, result_rows, sems, grad_sem = rest[parts - 1 :]
    rows, channels = base.shape
    grad_copy = pltpu.make_async_copy(grad_rows, grad_hbm, grad_sem)
    grad_copy.start()
    sort_blocks(parts, pays, held)
    incoming = merged_state(parts, taps, held)
    onehot = spread_matrix(heads, channels)
    change = first_change(taps, own_halo(held), inputs[0:16, :].astype(F32))
    change_scaled = (change * lead[...]).astype(BF16)
    state = incoming + dot(b_proj[0:16, :], change_scaled, ((0,), (0,)))
    state = state.astype(BF16)
    row = lax.broadcasted_iota(jnp.int32, (16, 16), 0)
    col = lax.broadcasted_iota(jnp.int32, (16, 16), 1)
    scores = dot(c_proj[0:16, :], b_proj[0:16, :], ((1,), (1,)))
    scores = jnp.where(row >= col, scores, 0.0).astype(BF16)
    top = dot(c_proj[0:16, :], incoming.astype(BF16), ((1,), (0,)))
    top = top + dot(scores, change_scaled, ((1,), (0,)))
    top = top * spread(front[:, 0:16], onehot) + base[0:16, :]
    top = top + gains[0:1, :] * change
    copies = []
    for piece in range(rows // STEP_ROWS):
        for at in range(piece * STEP_ROWS, (piece + 1) * STEP_ROWS, CHUNK):
            both = slice(at, at + CHUNK)
            carried = dot(c_proj[both, :], state, ((1,), (0,)))
            result = base[both, :] + spread(front[:, both], onehot) * carried
            result_rows[both, :] = result.astype(BF16)
            if at == 0:
                result_rows[0:16, :] = top.astype(BF16)
        place = pl.ds(piece * STEP_ROWS, STEP_ROWS)
        copy = pltpu.make_async_copy(result_rows.at[place], out_hbm.at[place], sems.at[piece])
        copy.start()
        copies.append(copy)
    for copy in copies:
        copy.wait()
    grad_copy.wait()


def finish_kernel(parts, scale, taps, tail, edge, *rest):
    others = rest[: parts - 1]
    unused, grad_hbm, conv_out, rows_low, sem = rest[parts - 1 :]
    channels = tail.shape[1]
    me = lax.axis_index("seq")
    after = jnp.zeros(tail.shape, F32)
    for distance in range(1, parts):
        here = sender(me, distance, parts) == me + 1
        after = jnp.where(here, others[distance - 1][...], after)
    row = lax.broadcasted_iota(jnp.int32, (16, channels), 0)
    result = edge[...]
    for r in range(3):
        extra = jnp.zeros((1, channels), F32)
        for k in range(r + 1):
            extra = extra + taps[k : k + 1, :] * after[4 + r - k : 5 + r - k, :]
        result = jnp.where(row == 13 + r, result + extra, result)
    rows_low[...] = result.astype(BF16)
    rows = grad_hbm.shape[0]
    copy = pltpu.make_async_copy(rows_low, grad_hbm.at[pl.ds(rows - 16, 16)], sem)
    copy.start()
    total = tail[0:4, :]
    for other in others:
        total = total + other[0:4, :]
    conv_out[...] = total * scale
    copy.wait()


def rotated(block, axis, distance):
    size = lax.axis_size(axis)
    return lax.ppermute(block, axis, [(i, partner(i, distance, size)) for i in range(size)])


def shards(
    inputs,
    b_proj,
    c_proj,
    step_codes,
    gate_codes,
    decay_rates,
    skip_gain,
    conv_weight,
    out_cotangent,
):
    rows, channels = inputs.shape
    heads = decay_rates.shape[0]
    parts = lax.axis_size("seq")
    chunks = rows // CHUNK
    pieces = rows // STEP_ROWS
    hbm = pl.BlockSpec(memory_space=pltpu.HBM)
    vmem = pl.BlockSpec(memory_space=pltpu.VMEM)
    shape = jax.ShapeDtypeStruct
    dma = pltpu.SemaphoreType.DMA
    big = rows * channels

    def call(kernel, in_specs, out_specs, out_shape, scratch, products, aliases=None):
        return pl.pallas_call(
            kernel,
            in_specs=in_specs,
            out_specs=out_specs,
            out_shape=out_shape,
            scratch_shapes=scratch,
            input_output_aliases=aliases or {},
            compiler_params=pltpu.CompilerParams(vmem_limit_bytes=VMEM_LIMIT),
            cost_estimate=pl.CostEstimate(
                flops=products * 2 * big * 128, bytes_accessed=6 * big, transcendentals=big
            ),
        )

    def stay(array):
        return pltpu.with_memory_space_constraint(array, pltpu.HBM)

    pay = shape((STATE + 16, channels), BF16)
    narrow = shape((rows, channels), BF16)
    broad = shape((rows, channels), F32)
    slim = shape((rows, STATE), BF16)

    outs = call(
        functools.partial(reduce_kernel, heads, parts),
        [hbm] * 9,
        [vmem] * (11 + parts),
        [
            shape((32, rows), BF16),
            shape((16, rows), BF16),
            shape((16, rows), BF16),
            shape((3, chunks, channels), F32),
            shape((16, channels), F32),
            shape((8, channels), F32),
            broad,
            broad,
            narrow,
            slim,
            narrow,
            slim,
        ]
        + [pay] * (parts - 1),
        [
            pltpu.SMEM((heads,), F32),
            pltpu.SMEM((heads,), F32),
            pltpu.VMEM((heads, rows), jnp.int32),
            pltpu.VMEM((1, rows), jnp.int32),
            pltpu.VMEM((4, channels), F32),
            pltpu.VMEM((8, rows), F32),
            pltpu.VMEM((rows, channels), BF16),
            pltpu.VMEM((16, CHUNK), BF16),
            pltpu.VMEM((16, channels), F32),
            dma((9,)),
        ],
        4,
    )(
        stay(decay_rates),
        stay(skip_gain),
        stay(step_codes),
        stay(gate_codes.reshape(1, rows)),
        stay(conv_weight),
        stay(inputs),
        stay(b_proj),
        stay(out_cotangent),
        stay(c_proj),
    )
    near, far, front, logs, lead, gain, mixed, sigma = outs[:8]
    inputs, b_proj, out_cotangent, c_proj = outs[8:12]
    pays = [rotated(send, "seq", distance + 1) for distance, send in enumerate(outs[12:])]

    tile = pltpu.VMEM((rows, CHUNK), BF16)
    low = pltpu.VMEM((rows, channels), BF16)
    high = pltpu.VMEM((rows, channels), F32)
    base, grad_base, grad_weight, unscaled = call(
        functools.partial(inner_kernel, heads),
        [vmem] * 9,
        [vmem] * 4,
        [broad] * 3 + [shape((16, channels), F32)],
        [tile, tile, low, low, low, low, high, high],
        10,
    )(gain, near, far, logs, out_cotangent, mixed, sigma, b_proj, c_proj)

    held = pltpu.VMEM((parts, STATE + 16, channels), BF16)
    grad_rows, tail, edge = call(
        functools.partial(gradient_kernel, parts),
        [vmem] * (5 + parts),
        [vmem] * 3,
        [narrow, shape((8, channels), F32), shape((16, channels), F32)],
        [pltpu.VMEM((rows + 16, channels), BF16), high, held],
        2,
    )(conv_weight, grad_base, grad_weight, unscaled, inputs, b_proj, *pays)
    tails = [rotated(tail, "seq", distance) for distance in range(1, parts)]

    layer_out, grad_rows = call(
        functools.partial(output_kernel, heads, parts),
        [vmem] * (8 + parts),
        [hbm, hbm],
        [narrow, narrow],
        [held, low, dma((pieces,)), dma],
        2,
    )(gain, conv_weight, front, lead, base, inputs, b_proj, c_proj, grad_rows, *pays)

    scale = float((rows * parts) ** -0.5)
    input_grad, conv_grad = call(
        functools.partial(finish_kernel, parts, scale),
        [vmem] * (2 + parts) + [hbm],
        [hbm, vmem],
        [narrow, shape((4, channels), F32)],
        [pltpu.VMEM((16, channels), BF16), dma],
        0,
        {parts + 2: 0},
    )(conv_weight, tail, edge, *tails, grad_rows)
    return layer_out, input_grad, conv_grad


def solution(mesh):
    in_specs = (
        P(("groups", "seq"), ("head", "sub")),
        P(("groups", "seq"), None),
        P(("groups", "seq"), None),
        P(("head", "sub"), ("groups", "seq")),
        P(("groups", "seq")),
        P(("head", "sub")),
        P(("head", "sub")),
        P(None, ("head", "sub")),
        P(("groups", "seq"), ("head", "sub")),
    )
    out_specs = (
        P(("groups", "seq"), ("head", "sub")),
        P(("groups", "seq"), ("head", "sub")),
        P("groups", ("head", "sub")),
    )
    return jax.shard_map(shards, mesh=mesh, in_specs=in_specs, out_specs=out_specs, check_vma=False)
```

```python
import functools

import jax
import jax.numpy as jnp
from jax import lax
from jax.experimental import pallas as pl
from jax.experimental.pallas import tpu as pltpu
from jax.sharding import PartitionSpec as P

CHUNK = 128
STATE = 128
STEP_ROWS = 512
LOG_ONE = -0.2876820724517809
LOG_TWO = -0.6931471805599453
F32 = jnp.float32
BF16 = jnp.bfloat16
HIGHEST = lax.Precision.HIGHEST
VMEM_LIMIT = 20 * 1024 * 1024


def dot(a, b, dims, precision=None):
    return lax.dot_general(a, b, (dims, ((), ())), preferred_element_type=F32, precision=precision)


def per_lane(scalars, count, channels):
    width = channels // count
    lane = lax.broadcasted_iota(jnp.int32, (1, channels), 1)
    row = jnp.zeros((1, channels), F32)
    for head in range(count):
        inside = (lane >= head * width) & (lane < (head + 1) * width)
        row = jnp.where(inside, scalars[head], row)
    return row


def split_two(value):
    high = value.astype(BF16)
    low = (value - high.astype(F32)).astype(BF16)
    return jnp.concatenate([high.astype(F32), low.astype(F32)], axis=0).astype(BF16)


def head_of(lane, width):
    if width & (width - 1) == 0:
        return lane >> (width.bit_length() - 1)
    return lane // width


def spread_matrix(count, channels):
    width = channels // count
    row = lax.broadcasted_iota(jnp.int32, (16, channels), 0)
    lane = lax.broadcasted_iota(jnp.int32, (16, channels), 1)
    return jnp.where((row & 7) == head_of(lane, width), 1.0, 0.0).astype(BF16)


def spread(pair, onehot):
    return dot(pair, onehot, ((0,), (0,)))


def reduce_kernel(
    heads, parts,
    rates_hbm, gains_hbm, codes_hbm, gates_hbm, taps_hbm, inputs_hbm, b_hbm, grad_hbm, c_hbm,
    near_out, far_out, front_out, logs_out, lead_out, gain_out, mixed_out, sigma_out,
    inputs, b_proj, grad, c_proj, *rest
):
    pays = rest[: parts - 1]
    rates, gains, codes, gates, taps, steps, scaled, lead_pair, extra, sems = rest[parts - 1 :]
    rows, channels = grad.shape
    chunks = rows // CHUNK
    sources = (
        rates_hbm, gains_hbm, codes_hbm, gates_hbm, taps_hbm, inputs_hbm, b_hbm, grad_hbm, c_hbm
    )
    targets = (rates, gains, codes, gates, taps, inputs, b_proj, grad, c_proj)
    copies = [
        pltpu.make_async_copy(source, target, sems.at[i])
        for i, (source, target) in enumerate(zip(sources, targets))
    ]
    for copy in copies:
        copy.start()
    for copy in copies[:4]:
        copy.wait()

    steps[...] = jnp.zeros_like(steps)
    steps[0:heads, :] = jnp.exp2(-codes[...].astype(F32))
    gate = gates[...]
    steps[6:7, :] = jnp.where(gate == 1, 1.0, 0.0).astype(F32)
    steps[7:8, :] = jnp.where(gate == 2, 1.0, 0.0).astype(F32)
    stacked = jnp.concatenate(
        [steps[:, j * CHUNK : (j + 1) * CHUNK] for j in range(chunks)], axis=0
    ).astype(BF16)
    row = lax.broadcasted_iota(jnp.int32, (CHUNK, CHUNK), 0)
    col = lax.broadcasted_iota(jnp.int32, (CHUNK, CHUNK), 1)
    upper = jnp.where(row <= col, 1.0, 0.0).astype(BF16)
    sums = dot(stacked, upper, ((1,), (0,)))
    sub = lax.broadcasted_iota(jnp.int32, (8, CHUNK), 0)
    rate = jnp.zeros((8, CHUNK), F32)
    for head in range(heads):
        rate = jnp.where(sub == head, rates[head], rate)
    cums, mids, befores = [], [], []
    before = jnp.zeros((8, 1), F32)
    for j in range(chunks):
        part = sums[8 * j : 8 * j + 8, :]
        cum = LOG_ONE * part[6:7, :] + LOG_TWO * part[7:8, :] - rate * part
        cums.append(cum)
        mids.append(cum[:, CHUNK // 2 - 1 : CHUNK // 2])
        befores.append(before)
        before = before + cum[:, CHUNK - 1 : CHUNK]
    for j in range(chunks):
        at = slice(j * CHUNK, (j + 1) * CHUNK)
        size = steps[:, at]
        near_out[0:16, at] = split_two(jnp.exp(cums[j] - mids[j]))
        near_out[16:32, at] = split_two(jnp.exp(mids[j] - cums[j]) * size)
        front_out[:, at] = split_two(jnp.exp(befores[j] + cums[j]))
        far_out[:, at] = split_two(jnp.exp(before - befores[j] - cums[j]) * size)
    lead_pair[...] = split_two(jnp.exp(-jnp.maximum(cums[0], -8.0)) * steps[:, 0:CHUNK])
    pick = lax.broadcasted_iota(jnp.int32, (8, CHUNK), 0)
    place = lax.broadcasted_iota(jnp.int32, (8, CHUNK), 1)
    chosen = jnp.where((pick == 0) | ((pick == 1) & (place < CHUNK // 2)), 1.0, 0.0)
    flat = dot(chosen.astype(BF16), stacked, ((1,), (1,)))
    owner = lax.broadcasted_iota(jnp.int32, (chunks, 8 * chunks), 1) >> 3
    chunk_at = lax.broadcasted_iota(jnp.int32, (chunks, 8 * chunks), 0)
    lane_rate = per_lane(rates, heads, channels)
    kind = lax.broadcasted_iota(jnp.int32, (8 * chunks, channels), 0) & 7
    lane = lax.broadcasted_iota(jnp.int32, (8 * chunks, channels), 1)
    lane_head = head_of(lane, channels // heads)
    mixer = jnp.where(kind == lane_head, -lane_rate, 0.0)
    mixer = jnp.where(kind == 6, LOG_ONE, jnp.where(kind == 7, LOG_TWO, mixer))
    table = []
    for which in range(2):
        own = jnp.where(owner == chunk_at, flat[which : which + 1, :], 0.0)
        table.append(dot(own, mixer, ((1,), (0,)), HIGHEST))
    whole = jnp.exp(table[0])
    middle = jnp.exp(table[1])
    rest_of = jnp.exp(table[0] - table[1])
    logs_out[0] = whole
    logs_out[1] = middle
    logs_out[2] = rest_of
    decay = jnp.exp(jnp.sum(table[0], axis=0, keepdims=True))
    first = decay.astype(BF16).astype(F32)
    extra[...] = jnp.zeros_like(extra)
    extra[0:1, :] = first
    extra[1:2, :] = decay - first

    onehot = spread_matrix(heads, channels)
    lead_out[...] = spread(lead_pair[:, 0:16], onehot)
    gain_out[...] = jnp.broadcast_to(per_lane(gains, heads, channels), (8, channels))
    for copy in copies[4:7]:
        copy.wait()
    shift = back_shift()
    nothing = jnp.zeros((16, channels), BF16)
    for at in range(0, rows, CHUNK):
        both = slice(at, at + CHUNK)
        if at == 0:
            block = jnp.concatenate([nothing, inputs[both, :]], axis=0)
        else:
            block = inputs[at - 16 : at + CHUNK, :]
        moved = dot(shift, block, ((1,), (0,)))
        preact = taps[3:4, :] * inputs[both, :].astype(F32)
        for k in range(3):
            preact = preact + taps[k : k + 1, :] * moved[k * CHUNK : (k + 1) * CHUNK, :]
        sigma = 0.5 * jnp.tanh(0.5 * preact) + 0.5
        mixed = preact * sigma
        scale = spread(far_out[:, both], onehot)
        sigma_out[both, :] = sigma
        mixed_out[both, :] = mixed
        scaled[both, :] = (mixed * scale).astype(BF16)
        if at == 0:
            extra[11:14, :] = scale[0:3, :]
    state = dot(b_proj[...], scaled[...], ((0,), (0,))).astype(BF16)
    extra[2:5, :] = inputs[0:16, :].astype(F32)[0:3, :]
    extra[5:8, :] = inputs[rows - 16 : rows, :].astype(F32)[13:16, :]
    extra[8:11, 0:STATE] = b_proj[0:16, :].astype(F32)[0:3, :]
    for copy in copies[7:]:
        copy.wait()
    for at in range(0, rows, STEP_ROWS):
        both = slice(at, at + STEP_ROWS)
        scale = spread(front_out[:, both], onehot)
        scaled[both, :] = (grad[both, :].astype(F32) * scale).astype(BF16)
    adjoint = dot(c_proj[...], scaled[...], ((0,), (0,))).astype(BF16)
    me = lax.axis_index("seq")
    for distance in range(1, parts):
        pay = pays[distance - 1]
        pay[0:STATE, :] = jnp.where(partner(me, distance, parts) > me, state, adjoint)
        pay[STATE : STATE + 16, :] = extra[...].astype(BF16)


def back_shift():
    row = lax.broadcasted_iota(jnp.int32, (3 * CHUNK, CHUNK + 16), 0)
    col = lax.broadcasted_iota(jnp.int32, (3 * CHUNK, CHUNK + 16), 1)
    at = (row & (CHUNK - 1)) + 13 + (row >> 7)
    return jnp.where(col == at, 1.0, 0.0).astype(BF16)


def tail_rows(held, source):
    return held[source, STATE : STATE + 16, :].astype(F32)


def first_preact(taps, halo, first):
    joined = jnp.concatenate([halo[0:3, :], first[0:8, :]], axis=0)
    preact = taps[0:1, :] * joined[0:8, :]
    for k in range(1, 4):
        preact = preact + taps[k : k + 1, :] * joined[k : k + 8, :]
    return preact


def first_change(taps, halo, first):
    true = first_preact(taps, halo, first)
    bare = first_preact(taps, jnp.zeros_like(halo), first)
    change = true * (0.5 * jnp.tanh(0.5 * true) + 0.5) - bare * (0.5 * jnp.tanh(0.5 * bare) + 0.5)
    row = lax.broadcasted_iota(jnp.int32, change.shape, 0)
    change = jnp.where(row < 3, change, 0.0)
    return jnp.concatenate([change, jnp.zeros_like(change)], axis=0)


def lane_tiles(channels):
    return [slice(at, min(at + 128, channels)) for at in range(0, channels, 128)]


def partner(me, distance, parts):
    return (me ^ distance) if parts & (parts - 1) == 0 else (me + distance) % parts


def sender(me, distance, parts):
    return (me ^ distance) if parts & (parts - 1) == 0 else (me + parts - distance) % parts


def sort_blocks(parts, pays, held):
    me = lax.axis_index("seq")
    held[me] = jnp.zeros(held.shape[1:], BF16)
    for distance in range(1, parts):
        held[sender(me, distance, parts)] = pays[distance - 1][...]


def merged_adjoint(parts, held):
    me = lax.axis_index("seq")
    running = jnp.zeros((STATE, held.shape[2]), F32)
    for source in range(parts - 1, 0, -1):
        tail = tail_rows(held, source)
        decay = tail[0:1, :] + tail[1:2, :]
        block = held[source, 0:STATE, :].astype(F32)
        running = jnp.where(source > me, block + decay * running, running)
    return running.astype(BF16)


def own_halo(held):
    me = lax.axis_index("seq")
    return jnp.where(me > 0, tail_rows(held, jnp.maximum(me - 1, 0))[5:8, :], 0.0)


def merged_state(parts, taps, held):
    me = lax.axis_index("seq")
    channels = held.shape[2]
    running = jnp.zeros((STATE, channels), F32)
    blank = jnp.zeros((5, channels), F32)
    tails = [tail_rows(held, source) for source in range(parts - 1)]
    for source in range(parts - 1):
        tail = tails[source]
        state = held[source, 0:STATE, :].astype(F32)
        if source > 0:
            first = jnp.concatenate([tail[2:5, :], blank], axis=0)
            scale = jnp.concatenate([tail[11:14, :], blank, blank, blank[0:3, :]], axis=0)
            change = first_change(taps, tails[source - 1][5:8, :], first)
            change = (change * scale).astype(BF16)
            row = lax.broadcasted_iota(jnp.int32, (16, STATE), 0)
            lines = jnp.concatenate([tail[8:11, 0:STATE], blank[:, 0:STATE]], axis=0)
            lines = jnp.concatenate([lines, jnp.zeros_like(lines)], axis=0)
            lines = jnp.where(row < 3, lines, 0.0).astype(BF16)
            state = state + dot(lines, change, ((0,), (0,)))
        decay = tail[0:1, :] + tail[1:2, :]
        running = jnp.where(source < me, state + decay * running, running)
    return running


def inner_kernel(
    heads, gains, near, far, logs, grad, mixed, sigma, b_proj, c_proj,
    inputs, base_out, grad_base, grad_weight, first_out, moved_out,
    ahead_scores, behind_scores, mixed_scaled, mixed_low, grad_scaled, grad_low,
    mixed_fresh, grad_fresh,
):
    rows, channels = grad.shape
    chunks = rows // CHUNK
    blocks = [slice(j * CHUNK, (j + 1) * CHUNK) for j in range(chunks)]
    row = lax.broadcasted_iota(jnp.int32, (CHUNK, CHUNK), 0)
    col = lax.broadcasted_iota(jnp.int32, (CHUNK, CHUNK), 1)
    onehot = spread_matrix(heads, channels)
    gain = gains[0:1, :]
    for both in blocks:
        scale = spread(near[0:16, both], onehot)
        grad_scaled[both, :] = (grad[both, :].astype(F32) * scale).astype(BF16)
    for both in blocks:
        scale = spread(near[16:32, both], onehot)
        mixed_scaled[both, :] = (mixed[both, :] * scale).astype(BF16)
    for both in blocks:
        grad_fresh[both, :] = dot(c_proj[both, :], grad_scaled[both, :], ((0,), (0,)))
    for both in blocks:
        mixed_fresh[both, :] = dot(b_proj[both, :], mixed_scaled[both, :], ((0,), (0,)))
    for both in blocks:
        ahead = dot(c_proj[both, :], b_proj[both, :], ((1,), (1,)))
        ahead_scores[both, :] = jnp.where(row >= col, ahead, 0.0).astype(BF16)
    for both in blocks:
        behind = dot(b_proj[both, :], c_proj[both, :], ((1,), (1,)))
        behind_scores[both, :] = jnp.where(row <= col, behind, 0.0).astype(BF16)
    for lanes in lane_tiles(channels):
        adjoint = jnp.zeros((STATE, lanes.stop - lanes.start), F32)
        for j in range(chunks - 1, -1, -1):
            grad_low[blocks[j], lanes] = (adjoint * logs[2, j : j + 1, lanes]).astype(BF16)
            adjoint = logs[0, j : j + 1, lanes] * adjoint + (
                logs[1, j : j + 1, lanes] * grad_fresh[blocks[j], lanes]
            )
        state = jnp.zeros((STATE, lanes.stop - lanes.start), F32)
        for j in range(chunks):
            mixed_low[blocks[j], lanes] = (state * logs[1, j : j + 1, lanes]).astype(BF16)
            state = logs[0, j : j + 1, lanes] * state + (
                logs[2, j : j + 1, lanes] * mixed_fresh[blocks[j], lanes]
            )
    for both in blocks:
        inner = dot(
            jnp.concatenate([behind_scores[both, :], b_proj[both, :]], axis=1),
            jnp.concatenate([grad_scaled[both, :], grad_low[both, :]], axis=0),
            ((1,), (0,)),
        )
        slope = sigma[both, :] + mixed[both, :] * (1.0 - sigma[both, :])
        inner = gain * grad[both, :].astype(F32) + spread(near[16:32, both], onehot) * inner
        weight = spread(far[:, both], onehot)
        grad_base[both, :] = slope * inner
        grad_weight[both, :] = slope * weight
        if both.start == 0:
            first_out[0:8, :] = inner[0:8, :]
            first_out[8:16, :] = weight[0:8, :]
    for both in blocks:
        inner = dot(
            jnp.concatenate([ahead_scores[both, :], c_proj[both, :]], axis=1),
            jnp.concatenate([mixed_scaled[both, :], mixed_low[both, :]], axis=0),
            ((1,), (0,)),
        )
        base_out[both, :] = gain * mixed[both, :] + spread(near[0:16, both], onehot) * inner
    shift = back_shift()
    for both in blocks:
        if both.start == 0:
            nothing = jnp.zeros((16, channels), BF16)
            block = jnp.concatenate([nothing, inputs[both, :]], axis=0)
        else:
            block = inputs[both.start - 16 : both.stop, :]
        moved = dot(shift, block, ((1,), (0,)))
        for k in range(3):
            moved_out[k, both, :] = moved[k * CHUNK : (k + 1) * CHUNK, :].astype(BF16)


def gradient_kernel(parts, taps, base, weight, unscaled, inputs, moved, b_proj, *rest):
    pays = rest[: parts - 1]
    exact, window, tail_out, held, products = rest[parts - 1 :]
    rows, channels = base.shape
    chunks = rows // CHUNK
    sort_blocks(parts, pays, held)
    adjoint = merged_adjoint(parts, held)
    halo = own_halo(held)
    preact = first_preact(taps, halo, inputs[0:16, :].astype(F32))
    sigma = 0.5 * jnp.tanh(0.5 * preact) + 0.5
    slope = sigma + preact * sigma * (1.0 - sigma)
    window[rows : rows + 16, :] = jnp.zeros((16, channels), BF16)
    for j in range(chunks):
        both = slice(j * CHUNK, (j + 1) * CHUNK)
        carried = dot(b_proj[both, :], adjoint, ((1,), (0,)))
        grad_pre = base[both, :] + weight[both, :] * carried
        if j == 0:
            first = slope * (unscaled[0:8, :] + unscaled[8:16, :] * carried[0:8, :])
            grad_pre = jnp.concatenate([first, grad_pre[8:, :]], axis=0)
        exact[both, :] = grad_pre
        low = grad_pre.astype(BF16)
        window[both, :] = low
        for k in range(3):
            products[k, both, :] = low * moved[k, both, :]
        products[3, both, :] = low * inputs[both, :]
    ones = jnp.ones((8, rows), BF16)
    for k in range(4):
        tap = dot(ones, products[k], ((1,), (0,)))[0:1, :]
        for j in range(k, 3):
            tap = tap + first[j - k : j - k + 1, :] * halo[j : j + 1, :]
        tail_out[k : k + 1, :] = tap
    tail_out[4:7, :] = first[0:3, :]
    tail_out[7:8, :] = jnp.zeros((1, channels), F32)


def output_kernel(
    heads, parts, gains, taps, front, lead, base, inputs, b_proj, c_proj, exact, window, *rest
):
    pays = rest[: parts - 1]
    out_hbm, grad_hbm, edge_out, held, result_rows, grad_rows, sems = rest[parts - 1 :]
    rows, channels = base.shape
    sort_blocks(parts, pays, held)
    incoming = merged_state(parts, taps, held)
    onehot = spread_matrix(heads, channels)
    change = first_change(taps, own_halo(held), inputs[0:16, :].astype(F32))
    change_scaled = (change * lead[...]).astype(BF16)
    state = incoming + dot(b_proj[0:16, :], change_scaled, ((0,), (0,)))
    state = state.astype(BF16)
    row = lax.broadcasted_iota(jnp.int32, (16, 16), 0)
    col = lax.broadcasted_iota(jnp.int32, (16, 16), 1)
    scores = dot(c_proj[0:16, :], b_proj[0:16, :], ((1,), (1,)))
    scores = jnp.where(row >= col, scores, 0.0).astype(BF16)
    top = dot(c_proj[0:16, :], incoming.astype(BF16), ((1,), (0,)))
    top = top + dot(scores, change_scaled, ((1,), (0,)))
    top = top * spread(front[:, 0:16], onehot) + base[0:16, :]
    top = top + gains[0:1, :] * change
    row = lax.broadcasted_iota(jnp.int32, (3 * CHUNK, CHUNK + 16), 0)
    col = lax.broadcasted_iota(jnp.int32, (3 * CHUNK, CHUNK + 16), 1)
    shift = jnp.where(col == (row & (CHUNK - 1)) + 3 - (row >> 7), 1.0, 0.0).astype(BF16)
    for at in range(0, rows, CHUNK):
        both = slice(at, at + CHUNK)
        moved = dot(shift, window[at : at + CHUNK + 16, :], ((1,), (0,)))
        result = taps[3:4, :] * exact[both, :]
        for k in range(3):
            result = result + taps[k : k + 1, :] * moved[k * CHUNK : (k + 1) * CHUNK, :]
        grad_rows[both, :] = result.astype(BF16)
        if at + CHUNK == rows:
            edge_out[...] = result[CHUNK - 16 :, :]
    grad_copy = pltpu.make_async_copy(grad_rows, grad_hbm, sems.at[0])
    grad_copy.start()
    for at in range(0, rows, CHUNK):
        both = slice(at, at + CHUNK)
        carried = dot(c_proj[both, :], state, ((1,), (0,)))
        result = base[both, :] + spread(front[:, both], onehot) * carried
        result_rows[both, :] = result.astype(BF16)
        if at == 0:
            result_rows[0:16, :] = top.astype(BF16)
    out_copy = pltpu.make_async_copy(result_rows, out_hbm, sems.at[1])
    out_copy.start()
    grad_copy.wait()
    out_copy.wait()


def finish_kernel(parts, scale, taps, tail, edge, *rest):
    others = rest[: parts - 1]
    unused, grad_hbm, conv_out, rows_low, sem = rest[parts - 1 :]
    channels = tail.shape[1]
    me = lax.axis_index("seq")
    after = jnp.zeros(tail.shape, F32)
    for distance in range(1, parts):
        here = sender(me, distance, parts) == me + 1
        after = jnp.where(here, others[distance - 1][...], after)
    row = lax.broadcasted_iota(jnp.int32, (16, channels), 0)
    result = edge[...]
    for r in range(3):
        extra = jnp.zeros((1, channels), F32)
        for k in range(r + 1):
            extra = extra + taps[k : k + 1, :] * after[4 + r - k : 5 + r - k, :]
        result = jnp.where(row == 13 + r, result + extra, result)
    rows_low[...] = result.astype(BF16)
    rows = grad_hbm.shape[0]
    copy = pltpu.make_async_copy(rows_low, grad_hbm.at[pl.ds(rows - 16, 16)], sem)
    copy.start()
    total = tail[0:4, :]
    for other in others:
        total = total + other[0:4, :]
    conv_out[...] = total * scale
    copy.wait()


def rotated(block, axis, distance):
    size = lax.axis_size(axis)
    return lax.ppermute(block, axis, [(i, partner(i, distance, size)) for i in range(size)])


def shards(
    inputs,
    b_proj,
    c_proj,
    step_codes,
    gate_codes,
    decay_rates,
    skip_gain,
    conv_weight,
    out_cotangent,
):
    rows, channels = inputs.shape
    heads = decay_rates.shape[0]
    parts = lax.axis_size("seq")
    chunks = rows // CHUNK
    hbm = pl.BlockSpec(memory_space=pltpu.HBM)
    vmem = pl.BlockSpec(memory_space=pltpu.VMEM)
    shape = jax.ShapeDtypeStruct
    dma = pltpu.SemaphoreType.DMA
    big = rows * channels

    def call(kernel, in_specs, out_specs, out_shape, scratch, products, aliases=None):
        return pl.pallas_call(
            kernel,
            in_specs=in_specs,
            out_specs=out_specs,
            out_shape=out_shape,
            scratch_shapes=scratch,
            input_output_aliases=aliases or {},
            compiler_params=pltpu.CompilerParams(vmem_limit_bytes=VMEM_LIMIT),
            cost_estimate=pl.CostEstimate(
                flops=products * 2 * big * 128, bytes_accessed=6 * big, transcendentals=big
            ),
        )

    def stay(array):
        return pltpu.with_memory_space_constraint(array, pltpu.HBM)

    pay = shape((STATE + 16, channels), BF16)
    narrow = shape((rows, channels), BF16)
    broad = shape((rows, channels), F32)
    slim = shape((rows, STATE), BF16)

    outs = call(
        functools.partial(reduce_kernel, heads, parts),
        [hbm] * 9,
        [vmem] * (11 + parts),
        [
            shape((32, rows), BF16),
            shape((16, rows), BF16),
            shape((16, rows), BF16),
            shape((3, chunks, channels), F32),
            shape((16, channels), F32),
            shape((8, channels), F32),
            broad,
            broad,
            narrow,
            slim,
            narrow,
            slim,
        ]
        + [pay] * (parts - 1),
        [
            pltpu.SMEM((heads,), F32),
            pltpu.SMEM((heads,), F32),
            pltpu.VMEM((heads, rows), jnp.int32),
            pltpu.VMEM((1, rows), jnp.int32),
            pltpu.VMEM((4, channels), F32),
            pltpu.VMEM((8, rows), F32),
            pltpu.VMEM((rows, channels), BF16),
            pltpu.VMEM((16, CHUNK), BF16),
            pltpu.VMEM((16, channels), F32),
            dma((9,)),
        ],
        4,
    )(
        stay(decay_rates),
        stay(skip_gain),
        stay(step_codes),
        stay(gate_codes.reshape(1, rows)),
        stay(conv_weight),
        stay(inputs),
        stay(b_proj),
        stay(out_cotangent),
        stay(c_proj),
    )
    near, far, front, logs, lead, gain, mixed, sigma = outs[:8]
    inputs, b_proj, out_cotangent, c_proj = outs[8:12]
    pays = [rotated(send, "seq", distance + 1) for distance, send in enumerate(outs[12:])]

    tile = pltpu.VMEM((rows, CHUNK), BF16)
    low = pltpu.VMEM((rows, channels), BF16)
    high = pltpu.VMEM((rows, channels), F32)
    base, grad_base, grad_weight, unscaled, moved = call(
        functools.partial(inner_kernel, heads),
        [vmem] * 10,
        [vmem] * 5,
        [broad] * 3 + [shape((16, channels), F32), shape((3, rows, channels), BF16)],
        [tile, tile, low, low, low, low, high, high],
        10,
    )(gain, near, far, logs, out_cotangent, mixed, sigma, b_proj, c_proj, inputs)

    held = pltpu.VMEM((parts, STATE + 16, channels), BF16)
    exact, window, tail = call(
        functools.partial(gradient_kernel, parts),
        [vmem] * (6 + parts),
        [vmem] * 3,
        [broad, shape((rows + 16, channels), BF16), shape((8, channels), F32)],
        [held, pltpu.VMEM((4, rows, channels), BF16)],
        2,
    )(conv_weight, grad_base, grad_weight, unscaled, inputs, moved, b_proj, *pays)
    tails = [rotated(tail, "seq", distance) for distance in range(1, parts)]

    layer_out, grad_rows, edge = call(
        functools.partial(output_kernel, heads, parts),
        [vmem] * (9 + parts),
        [hbm, hbm, vmem],
        [narrow, narrow, shape((16, channels), F32)],
        [held, low, low, dma((2,))],
        4,
    )(gain, conv_weight, front, lead, base, inputs, b_proj, c_proj, exact, window, *pays)

    scale = float((rows * parts) ** -0.5)
    input_grad, conv_grad = call(
        functools.partial(finish_kernel, parts, scale),
        [vmem] * (2 + parts) + [hbm],
        [hbm, vmem],
        [narrow, shape((4, channels), F32)],
        [pltpu.VMEM((16, channels), BF16), dma],
        0,
        {parts + 2: 0},
    )(conv_weight, tail, edge, *tails, grad_rows)
    return layer_out, input_grad, conv_grad


def solution(mesh):
    in_specs = (
        P(("groups", "seq"), ("head", "sub")),
        P(("groups", "seq"), None),
        P(("groups", "seq"), None),
        P(("head", "sub"), ("groups", "seq")),
        P(("groups", "seq")),
        P(("head", "sub")),
        P(("head", "sub")),
        P(None, ("head", "sub")),
        P(("groups", "seq"), ("head", "sub")),
    )
    out_specs = (
        P(("groups", "seq"), ("head", "sub")),
        P(("groups", "seq"), ("head", "sub")),
        P("groups", ("head", "sub")),
    )
    return jax.shard_map(shards, mesh=mesh, in_specs=in_specs, out_specs=out_specs, check_vma=False)
```

```python
import functools

import jax
import jax.numpy as jnp
from jax import lax
from jax.experimental import pallas as pl
from jax.experimental.pallas import tpu as pltpu
from jax.sharding import PartitionSpec as P

CHUNK = 128
STATE = 128
STEP_ROWS = 512
LOG_ONE = -0.2876820724517809
LOG_TWO = -0.6931471805599453
F32 = jnp.float32
BF16 = jnp.bfloat16
HIGHEST = lax.Precision.HIGHEST
VMEM_LIMIT = 20 * 1024 * 1024


def dot(a, b, dims, precision=None):
    return lax.dot_general(a, b, (dims, ((), ())), preferred_element_type=F32, precision=precision)


def per_lane(scalars, count, channels):
    width = channels // count
    lane = lax.broadcasted_iota(jnp.int32, (1, channels), 1)
    row = jnp.zeros((1, channels), F32)
    for head in range(count):
        inside = (lane >= head * width) & (lane < (head + 1) * width)
        row = jnp.where(inside, scalars[head], row)
    return row


def split_two(value):
    high = value.astype(BF16)
    low = (value - high.astype(F32)).astype(BF16)
    return jnp.concatenate([high.astype(F32), low.astype(F32)], axis=0).astype(BF16)


def head_of(lane, width):
    if width & (width - 1) == 0:
        return lane >> (width.bit_length() - 1)
    return lane // width


def spread_matrix(count, channels):
    width = channels // count
    row = lax.broadcasted_iota(jnp.int32, (16, channels), 0)
    lane = lax.broadcasted_iota(jnp.int32, (16, channels), 1)
    return jnp.where((row & 7) == head_of(lane, width), 1.0, 0.0).astype(BF16)


def spread(pair, onehot):
    return dot(pair, onehot, ((0,), (0,)))


def reduce_kernel(
    heads, parts,
    rates_hbm, gains_hbm, codes_hbm, gates_hbm, taps_hbm, inputs_hbm, b_hbm, grad_hbm, c_hbm,
    near_out, far_out, front_out, logs_out, lead_out, gain_out, mixed_out, sigma_out,
    inputs, b_proj, grad, c_proj, *rest
):
    pays = rest[: parts - 1]
    rates, gains, codes, gates, taps, steps, scaled, lead_pair, extra, sems = rest[parts - 1 :]
    rows, channels = grad.shape
    chunks = rows // CHUNK
    sources = (
        rates_hbm, gains_hbm, codes_hbm, gates_hbm, taps_hbm, inputs_hbm, b_hbm, grad_hbm, c_hbm
    )
    targets = (rates, gains, codes, gates, taps, inputs, b_proj, grad, c_proj)
    copies = [
        pltpu.make_async_copy(source, target, sems.at[i])
        for i, (source, target) in enumerate(zip(sources, targets))
    ]
    for copy in copies:
        copy.start()
    for copy in copies[:4]:
        copy.wait()

    steps[...] = jnp.zeros_like(steps)
    steps[0:heads, :] = jnp.exp2(-codes[...].astype(F32))
    gate = gates[...]
    steps[6:7, :] = jnp.where(gate == 1, 1.0, 0.0).astype(F32)
    steps[7:8, :] = jnp.where(gate == 2, 1.0, 0.0).astype(F32)
    stacked = jnp.concatenate(
        [steps[:, j * CHUNK : (j + 1) * CHUNK] for j in range(chunks)], axis=0
    ).astype(BF16)
    row = lax.broadcasted_iota(jnp.int32, (CHUNK, CHUNK), 0)
    col = lax.broadcasted_iota(jnp.int32, (CHUNK, CHUNK), 1)
    upper = jnp.where(row <= col, 1.0, 0.0).astype(BF16)
    sums = dot(stacked, upper, ((1,), (0,)))
    sub = lax.broadcasted_iota(jnp.int32, (8, CHUNK), 0)
    rate = jnp.zeros((8, CHUNK), F32)
    for head in range(heads):
        rate = jnp.where(sub == head, rates[head], rate)
    cums, mids, befores = [], [], []
    before = jnp.zeros((8, 1), F32)
    for j in range(chunks):
        part = sums[8 * j : 8 * j + 8, :]
        cum = LOG_ONE * part[6:7, :] + LOG_TWO * part[7:8, :] - rate * part
        cums.append(cum)
        mids.append(cum[:, CHUNK // 2 - 1 : CHUNK // 2])
        befores.append(before)
        before = before + cum[:, CHUNK - 1 : CHUNK]
    for j in range(chunks):
        at = slice(j * CHUNK, (j + 1) * CHUNK)
        size = steps[:, at]
        near_out[0:16, at] = split_two(jnp.exp(cums[j] - mids[j]))
        near_out[16:32, at] = split_two(jnp.exp(mids[j] - cums[j]) * size)
        front_out[:, at] = split_two(jnp.exp(befores[j] + cums[j]))
        far_out[:, at] = split_two(jnp.exp(before - befores[j] - cums[j]) * size)
    lead_pair[...] = split_two(jnp.exp(-jnp.maximum(cums[0], -8.0)) * steps[:, 0:CHUNK])
    pick = lax.broadcasted_iota(jnp.int32, (8, CHUNK), 0)
    place = lax.broadcasted_iota(jnp.int32, (8, CHUNK), 1)
    chosen = jnp.where((pick == 0) | ((pick == 1) & (place < CHUNK // 2)), 1.0, 0.0)
    flat = dot(chosen.astype(BF16), stacked, ((1,), (1,)))
    owner = lax.broadcasted_iota(jnp.int32, (chunks, 8 * chunks), 1) >> 3
    chunk_at = lax.broadcasted_iota(jnp.int32, (chunks, 8 * chunks), 0)
    lane_rate = per_lane(rates, heads, channels)
    kind = lax.broadcasted_iota(jnp.int32, (8 * chunks, channels), 0) & 7
    lane = lax.broadcasted_iota(jnp.int32, (8 * chunks, channels), 1)
    lane_head = head_of(lane, channels // heads)
    mixer = jnp.where(kind == lane_head, -lane_rate, 0.0)
    mixer = jnp.where(kind == 6, LOG_ONE, jnp.where(kind == 7, LOG_TWO, mixer))
    table = []
    for which in range(2):
        own = jnp.where(owner == chunk_at, flat[which : which + 1, :], 0.0)
        table.append(dot(own, mixer, ((1,), (0,)), HIGHEST))
    whole = jnp.exp(table[0])
    middle = jnp.exp(table[1])
    rest_of = jnp.exp(table[0] - table[1])
    logs_out[0] = whole
    logs_out[1] = middle
    logs_out[2] = rest_of
    decay = jnp.exp(jnp.sum(table[0], axis=0, keepdims=True))
    first = decay.astype(BF16).astype(F32)
    extra[...] = jnp.zeros_like(extra)
    extra[0:1, :] = first
    extra[1:2, :] = decay - first

    onehot = spread_matrix(heads, channels)
    lead_out[...] = spread(lead_pair[:, 0:16], onehot)
    gain_out[...] = jnp.broadcast_to(per_lane(gains, heads, channels), (8, channels))
    for copy in copies[4:7]:
        copy.wait()
    shift = back_shift()
    nothing = jnp.zeros((16, channels), BF16)
    for at in range(0, rows, CHUNK):
        both = slice(at, at + CHUNK)
        if at == 0:
            block = jnp.concatenate([nothing, inputs[both, :]], axis=0)
        else:
            block = inputs[at - 16 : at + CHUNK, :]
        moved = dot(shift, block, ((1,), (0,)))
        preact = taps[3:4, :] * inputs[both, :].astype(F32)
        for k in range(3):
            preact = preact + taps[k : k + 1, :] * moved[k * CHUNK : (k + 1) * CHUNK, :]
        sigma = 0.5 * jnp.tanh(0.5 * preact) + 0.5
        mixed = preact * sigma
        scale = spread(far_out[:, both], onehot)
        sigma_out[both, :] = sigma
        mixed_out[both, :] = mixed
        scaled[both, :] = (mixed * scale).astype(BF16)
        if at == 0:
            extra[11:14, :] = scale[0:3, :]
    state = dot(b_proj[...], scaled[...], ((0,), (0,))).astype(BF16)
    extra[2:5, :] = inputs[0:16, :].astype(F32)[0:3, :]
    extra[5:8, :] = inputs[rows - 16 : rows, :].astype(F32)[13:16, :]
    extra[8:11, 0:STATE] = b_proj[0:16, :].astype(F32)[0:3, :]
    for copy in copies[7:]:
        copy.wait()
    for at in range(0, rows, STEP_ROWS):
        both = slice(at, at + STEP_ROWS)
        scale = spread(front_out[:, both], onehot)
        scaled[both, :] = (grad[both, :].astype(F32) * scale).astype(BF16)
    adjoint = dot(c_proj[...], scaled[...], ((0,), (0,))).astype(BF16)
    me = lax.axis_index("seq")
    for distance in range(1, parts):
        pay = pays[distance - 1]
        pay[0:STATE, :] = jnp.where(partner(me, distance, parts) > me, state, adjoint)
        pay[STATE : STATE + 16, :] = extra[...].astype(BF16)


def back_shift():
    row = lax.broadcasted_iota(jnp.int32, (3 * CHUNK, CHUNK + 16), 0)
    col = lax.broadcasted_iota(jnp.int32, (3 * CHUNK, CHUNK + 16), 1)
    at = (row & (CHUNK - 1)) + 13 + (row >> 7)
    return jnp.where(col == at, 1.0, 0.0).astype(BF16)


def tail_rows(held, source):
    return held[source, STATE : STATE + 16, :].astype(F32)


def first_preact(taps, halo, first):
    joined = jnp.concatenate([halo[0:3, :], first[0:8, :]], axis=0)
    preact = taps[0:1, :] * joined[0:8, :]
    for k in range(1, 4):
        preact = preact + taps[k : k + 1, :] * joined[k : k + 8, :]
    return preact


def first_change(taps, halo, first):
    true = first_preact(taps, halo, first)
    bare = first_preact(taps, jnp.zeros_like(halo), first)
    change = true * (0.5 * jnp.tanh(0.5 * true) + 0.5) - bare * (0.5 * jnp.tanh(0.5 * bare) + 0.5)
    row = lax.broadcasted_iota(jnp.int32, change.shape, 0)
    change = jnp.where(row < 3, change, 0.0)
    return jnp.concatenate([change, jnp.zeros_like(change)], axis=0)


def lane_tiles(channels):
    return [slice(at, min(at + 128, channels)) for at in range(0, channels, 128)]


def partner(me, distance, parts):
    return (me ^ distance) if parts & (parts - 1) == 0 else (me + distance) % parts


def sender(me, distance, parts):
    return (me ^ distance) if parts & (parts - 1) == 0 else (me + parts - distance) % parts


def sort_blocks(parts, pays, held):
    me = lax.axis_index("seq")
    held[me] = jnp.zeros(held.shape[1:], BF16)
    for distance in range(1, parts):
        held[sender(me, distance, parts)] = pays[distance - 1][...]


def merged_adjoint(parts, held):
    me = lax.axis_index("seq")
    running = jnp.zeros((STATE, held.shape[2]), F32)
    for source in range(parts - 1, 0, -1):
        tail = tail_rows(held, source)
        decay = tail[0:1, :] + tail[1:2, :]
        block = held[source, 0:STATE, :].astype(F32)
        running = jnp.where(source > me, block + decay * running, running)
    return running.astype(BF16)


def own_halo(held):
    me = lax.axis_index("seq")
    return jnp.where(me > 0, tail_rows(held, jnp.maximum(me - 1, 0))[5:8, :], 0.0)


def merged_state(parts, taps, held):
    me = lax.axis_index("seq")
    channels = held.shape[2]
    running = jnp.zeros((STATE, channels), F32)
    blank = jnp.zeros((5, channels), F32)
    tails = [tail_rows(held, source) for source in range(parts - 1)]
    for source in range(parts - 1):
        tail = tails[source]
        state = held[source, 0:STATE, :].astype(F32)
        if source > 0:
            first = jnp.concatenate([tail[2:5, :], blank], axis=0)
            scale = jnp.concatenate([tail[11:14, :], blank, blank, blank[0:3, :]], axis=0)
            change = first_change(taps, tails[source - 1][5:8, :], first)
            change = (change * scale).astype(BF16)
            row = lax.broadcasted_iota(jnp.int32, (16, STATE), 0)
            lines = jnp.concatenate([tail[8:11, 0:STATE], blank[:, 0:STATE]], axis=0)
            lines = jnp.concatenate([lines, jnp.zeros_like(lines)], axis=0)
            lines = jnp.where(row < 3, lines, 0.0).astype(BF16)
            state = state + dot(lines, change, ((0,), (0,)))
        decay = tail[0:1, :] + tail[1:2, :]
        running = jnp.where(source < me, state + decay * running, running)
    return running


def inner_kernel(
    heads, gains, near, far, logs, grad, mixed, sigma, b_proj, c_proj,
    base_out, grad_base, grad_weight, first_out,
    ahead_scores, behind_scores, mixed_scaled, mixed_low, grad_scaled, grad_low,
    mixed_fresh, grad_fresh,
):
    rows, channels = grad.shape
    chunks = rows // CHUNK
    blocks = [slice(j * CHUNK, (j + 1) * CHUNK) for j in range(chunks)]
    row = lax.broadcasted_iota(jnp.int32, (CHUNK, CHUNK), 0)
    col = lax.broadcasted_iota(jnp.int32, (CHUNK, CHUNK), 1)
    onehot = spread_matrix(heads, channels)
    gain = gains[0:1, :]
    for both in blocks:
        scale = spread(near[0:16, both], onehot)
        grad_scaled[both, :] = (grad[both, :].astype(F32) * scale).astype(BF16)
    for both in blocks:
        scale = spread(near[16:32, both], onehot)
        mixed_scaled[both, :] = (mixed[both, :] * scale).astype(BF16)
    for both in blocks:
        grad_fresh[both, :] = dot(c_proj[both, :], grad_scaled[both, :], ((0,), (0,)))
    for both in blocks:
        mixed_fresh[both, :] = dot(b_proj[both, :], mixed_scaled[both, :], ((0,), (0,)))
    for both in blocks:
        ahead = dot(c_proj[both, :], b_proj[both, :], ((1,), (1,)))
        ahead_scores[both, :] = jnp.where(row >= col, ahead, 0.0).astype(BF16)
    for both in blocks:
        behind = dot(b_proj[both, :], c_proj[both, :], ((1,), (1,)))
        behind_scores[both, :] = jnp.where(row <= col, behind, 0.0).astype(BF16)
    for lanes in lane_tiles(channels):
        adjoint = jnp.zeros((STATE, lanes.stop - lanes.start), F32)
        for j in range(chunks - 1, -1, -1):
            grad_low[blocks[j], lanes] = (adjoint * logs[2, j : j + 1, lanes]).astype(BF16)
            adjoint = logs[0, j : j + 1, lanes] * adjoint + (
                logs[1, j : j + 1, lanes] * grad_fresh[blocks[j], lanes]
            )
        state = jnp.zeros((STATE, lanes.stop - lanes.start), F32)
        for j in range(chunks):
            mixed_low[blocks[j], lanes] = (state * logs[1, j : j + 1, lanes]).astype(BF16)
            state = logs[0, j : j + 1, lanes] * state + (
                logs[2, j : j + 1, lanes] * mixed_fresh[blocks[j], lanes]
            )
    for both in blocks:
        inner = dot(
            jnp.concatenate([behind_scores[both, :], b_proj[both, :]], axis=1),
            jnp.concatenate([grad_scaled[both, :], grad_low[both, :]], axis=0),
            ((1,), (0,)),
        )
        slope = sigma[both, :] + mixed[both, :] * (1.0 - sigma[both, :])
        inner = gain * grad[both, :].astype(F32) + spread(near[16:32, both], onehot) * inner
        weight = spread(far[:, both], onehot)
        grad_base[both, :] = slope * inner
        grad_weight[both, :] = slope * weight
        if both.start == 0:
            first_out[0:8, :] = inner[0:8, :]
            first_out[8:16, :] = weight[0:8, :]
    for both in blocks:
        inner = dot(
            jnp.concatenate([ahead_scores[both, :], c_proj[both, :]], axis=1),
            jnp.concatenate([mixed_scaled[both, :], mixed_low[both, :]], axis=0),
            ((1,), (0,)),
        )
        base_out[both, :] = gain * mixed[both, :] + spread(near[0:16, both], onehot) * inner


def gradient_kernel(parts, taps, base, weight, unscaled, inputs, b_proj, *rest):
    pays = rest[: parts - 1]
    grad_out, tail_out, edge_out, window, exact, held = rest[parts - 1 :]
    rows, channels = base.shape
    chunks = rows // CHUNK
    sort_blocks(parts, pays, held)
    adjoint = merged_adjoint(parts, held)
    halo = own_halo(held)
    preact = first_preact(taps, halo, inputs[0:16, :].astype(F32))
    sigma = 0.5 * jnp.tanh(0.5 * preact) + 0.5
    slope = sigma + preact * sigma * (1.0 - sigma)
    window[rows : rows + 16, :] = jnp.zeros((16, channels), BF16)
    row = lax.broadcasted_iota(jnp.int32, (3 * CHUNK, CHUNK + 16), 0)
    col = lax.broadcasted_iota(jnp.int32, (3 * CHUNK, CHUNK + 16), 1)
    shift = jnp.where(col == (row & (CHUNK - 1)) + 3 - (row >> 7), 1.0, 0.0).astype(BF16)
    partial = [jnp.zeros((8, channels), F32) for _ in range(4)]
    for j in range(chunks):
        both = slice(j * CHUNK, (j + 1) * CHUNK)
        carried = dot(b_proj[both, :], adjoint, ((1,), (0,)))
        grad_pre = base[both, :] + weight[both, :] * carried
        if j == 0:
            first = slope * (unscaled[0:8, :] + unscaled[8:16, :] * carried[0:8, :])
            grad_pre = jnp.concatenate([first, grad_pre[8:, :]], axis=0)
        window[both, :] = grad_pre.astype(BF16)
        exact[both, :] = grad_pre
    for j in range(chunks):
        at = j * CHUNK
        both = slice(at, at + CHUNK)
        grad_pre = exact[both, :]
        moved = dot(shift, window[at : at + CHUNK + 16, :], ((1,), (0,)))
        x = inputs[both, :].astype(F32)
        result = taps[3:4, :] * grad_pre
        partial[3] = partial[3] + (grad_pre * x).reshape(CHUNK // 8, 8, channels).sum(axis=0)
        for k in range(3):
            part = moved[k * CHUNK : (k + 1) * CHUNK, :]
            result = result + taps[k : k + 1, :] * part
            partial[k] = partial[k] + (part * x).reshape(CHUNK // 8, 8, channels).sum(axis=0)
        grad_out[both, :] = result.astype(BF16)
        if j == chunks - 1:
            edge_out[...] = result[CHUNK - 16 :, :]
    for k in range(4):
        tap = jnp.sum(partial[k], axis=0, keepdims=True)
        for j in range(k, 3):
            tap = tap + first[j - k : j - k + 1, :] * halo[j : j + 1, :]
        tail_out[k : k + 1, :] = tap
    tail_out[4:7, :] = first[0:3, :]
    tail_out[7:8, :] = jnp.zeros((1, channels), F32)


def output_kernel(
    heads, parts, gains, taps, front, lead, base, inputs, b_proj, c_proj, grad_rows, *rest
):
    pays = rest[: parts - 1]
    out_hbm, grad_hbm, held, result_rows, sems = rest[parts - 1 :]
    rows, channels = base.shape
    grad_copy = pltpu.make_async_copy(grad_rows, grad_hbm, sems.at[0])
    grad_copy.start()
    sort_blocks(parts, pays, held)
    incoming = merged_state(parts, taps, held)
    onehot = spread_matrix(heads, channels)
    change = first_change(taps, own_halo(held), inputs[0:16, :].astype(F32))
    change_scaled = (change * lead[...]).astype(BF16)
    state = incoming + dot(b_proj[0:16, :], change_scaled, ((0,), (0,)))
    state = state.astype(BF16)
    row = lax.broadcasted_iota(jnp.int32, (16, 16), 0)
    col = lax.broadcasted_iota(jnp.int32, (16, 16), 1)
    scores = dot(c_proj[0:16, :], b_proj[0:16, :], ((1,), (1,)))
    scores = jnp.where(row >= col, scores, 0.0).astype(BF16)
    top = dot(c_proj[0:16, :], incoming.astype(BF16), ((1,), (0,)))
    top = top + dot(scores, change_scaled, ((1,), (0,)))
    top = top * spread(front[:, 0:16], onehot) + base[0:16, :]
    top = top + gains[0:1, :] * change
    for at in range(0, rows, CHUNK):
        both = slice(at, at + CHUNK)
        carried = dot(c_proj[both, :], state, ((1,), (0,)))
        result = base[both, :] + spread(front[:, both], onehot) * carried
        result_rows[both, :] = result.astype(BF16)
        if at == 0:
            result_rows[0:16, :] = top.astype(BF16)
    out_copy = pltpu.make_async_copy(result_rows, out_hbm, sems.at[1])
    out_copy.start()
    grad_copy.wait()
    out_copy.wait()


def finish_kernel(parts, scale, taps, tail, edge, *rest):
    others = rest[: parts - 1]
    unused, grad_hbm, conv_out, rows_low, sem = rest[parts - 1 :]
    channels = tail.shape[1]
    me = lax.axis_index("seq")
    after = jnp.zeros(tail.shape, F32)
    for distance in range(1, parts):
        here = sender(me, distance, parts) == me + 1
        after = jnp.where(here, others[distance - 1][...], after)
    row = lax.broadcasted_iota(jnp.int32, (16, channels), 0)
    result = edge[...]
    for r in range(3):
        extra = jnp.zeros((1, channels), F32)
        for k in range(r + 1):
            extra = extra + taps[k : k + 1, :] * after[4 + r - k : 5 + r - k, :]
        result = jnp.where(row == 13 + r, result + extra, result)
    rows_low[...] = result.astype(BF16)
    rows = grad_hbm.shape[0]
    copy = pltpu.make_async_copy(rows_low, grad_hbm.at[pl.ds(rows - 16, 16)], sem)
    copy.start()
    total = tail[0:4, :]
    for other in others:
        total = total + other[0:4, :]
    conv_out[...] = total * scale
    copy.wait()


def rotated(block, axis, distance):
    size = lax.axis_size(axis)
    return lax.ppermute(block, axis, [(i, partner(i, distance, size)) for i in range(size)])


def shards(
    inputs,
    b_proj,
    c_proj,
    step_codes,
    gate_codes,
    decay_rates,
    skip_gain,
    conv_weight,
    out_cotangent,
):
    rows, channels = inputs.shape
    heads = decay_rates.shape[0]
    parts = lax.axis_size("seq")
    chunks = rows // CHUNK
    hbm = pl.BlockSpec(memory_space=pltpu.HBM)
    vmem = pl.BlockSpec(memory_space=pltpu.VMEM)
    shape = jax.ShapeDtypeStruct
    dma = pltpu.SemaphoreType.DMA
    big = rows * channels

    def call(kernel, in_specs, out_specs, out_shape, scratch, products, aliases=None):
        return pl.pallas_call(
            kernel,
            in_specs=in_specs,
            out_specs=out_specs,
            out_shape=out_shape,
            scratch_shapes=scratch,
            input_output_aliases=aliases or {},
            compiler_params=pltpu.CompilerParams(vmem_limit_bytes=VMEM_LIMIT),
            cost_estimate=pl.CostEstimate(
                flops=products * 2 * big * 128, bytes_accessed=6 * big, transcendentals=big
            ),
        )

    def stay(array):
        return pltpu.with_memory_space_constraint(array, pltpu.HBM)

    pay = shape((STATE + 16, channels), BF16)
    narrow = shape((rows, channels), BF16)
    broad = shape((rows, channels), F32)
    slim = shape((rows, STATE), BF16)

    outs = call(
        functools.partial(reduce_kernel, heads, parts),
        [hbm] * 9,
        [vmem] * (11 + parts),
        [
            shape((32, rows), BF16),
            shape((16, rows), BF16),
            shape((16, rows), BF16),
            shape((3, chunks, channels), F32),
            shape((16, channels), F32),
            shape((8, channels), F32),
            broad,
            broad,
            narrow,
            slim,
            narrow,
            slim,
        ]
        + [pay] * (parts - 1),
        [
            pltpu.SMEM((heads,), F32),
            pltpu.SMEM((heads,), F32),
            pltpu.VMEM((heads, rows), jnp.int32),
            pltpu.VMEM((1, rows), jnp.int32),
            pltpu.VMEM((4, channels), F32),
            pltpu.VMEM((8, rows), F32),
            pltpu.VMEM((rows, channels), BF16),
            pltpu.VMEM((16, CHUNK), BF16),
            pltpu.VMEM((16, channels), F32),
            dma((9,)),
        ],
        4,
    )(
        stay(decay_rates),
        stay(skip_gain),
        stay(step_codes),
        stay(gate_codes.reshape(1, rows)),
        stay(conv_weight),
        stay(inputs),
        stay(b_proj),
        stay(out_cotangent),
        stay(c_proj),
    )
    near, far, front, logs, lead, gain, mixed, sigma = outs[:8]
    inputs, b_proj, out_cotangent, c_proj = outs[8:12]
    pays = [rotated(send, "seq", distance + 1) for distance, send in enumerate(outs[12:])]

    tile = pltpu.VMEM((rows, CHUNK), BF16)
    low = pltpu.VMEM((rows, channels), BF16)
    high = pltpu.VMEM((rows, channels), F32)
    base, grad_base, grad_weight, unscaled = call(
        functools.partial(inner_kernel, heads),
        [vmem] * 9,
        [vmem] * 4,
        [broad] * 3 + [shape((16, channels), F32)],
        [tile, tile, low, low, low, low, high, high],
        10,
    )(gain, near, far, logs, out_cotangent, mixed, sigma, b_proj, c_proj)

    held = pltpu.VMEM((parts, STATE + 16, channels), BF16)
    grad_rows, tail, edge = call(
        functools.partial(gradient_kernel, parts),
        [vmem] * (5 + parts),
        [vmem] * 3,
        [narrow, shape((8, channels), F32), shape((16, channels), F32)],
        [pltpu.VMEM((rows + 16, channels), BF16), high, held],
        2,
    )(conv_weight, grad_base, grad_weight, unscaled, inputs, b_proj, *pays)
    tails = [rotated(tail, "seq", distance) for distance in range(1, parts)]

    layer_out, grad_rows = call(
        functools.partial(output_kernel, heads, parts),
        [vmem] * (8 + parts),
        [hbm, hbm],
        [narrow, narrow],
        [held, low, dma((2,))],
        2,
    )(gain, conv_weight, front, lead, base, inputs, b_proj, c_proj, grad_rows, *pays)

    scale = float((rows * parts) ** -0.5)
    input_grad, conv_grad = call(
        functools.partial(finish_kernel, parts, scale),
        [vmem] * (2 + parts) + [hbm],
        [hbm, vmem],
        [narrow, shape((4, channels), F32)],
        [pltpu.VMEM((16, channels), BF16), dma],
        0,
        {parts + 2: 0},
    )(conv_weight, tail, edge, *tails, grad_rows)
    return layer_out, input_grad, conv_grad


def solution(mesh):
    in_specs = (
        P(("groups", "seq"), ("head", "sub")),
        P(("groups", "seq"), None),
        P(("groups", "seq"), None),
        P(("head", "sub"), ("groups", "seq")),
        P(("groups", "seq")),
        P(("head", "sub")),
        P(("head", "sub")),
        P(None, ("head", "sub")),
        P(("groups", "seq"), ("head", "sub")),
    )
    out_specs = (
        P(("groups", "seq"), ("head", "sub")),
        P(("groups", "seq"), ("head", "sub")),
        P("groups", ("head", "sub")),
    )
    return jax.shard_map(shards, mesh=mesh, in_specs=in_specs, out_specs=out_specs, check_vma=False)
```

```python
import functools

import jax
import jax.numpy as jnp
from jax import lax
from jax.experimental import pallas as pl
from jax.experimental.pallas import tpu as pltpu
from jax.sharding import PartitionSpec as P

CHUNK = 128
STATE = 128
STEP_ROWS = 512
LOG_ONE = -0.2876820724517809
LOG_TWO = -0.6931471805599453
F32 = jnp.float32
BF16 = jnp.bfloat16
HIGHEST = lax.Precision.HIGHEST
VMEM_LIMIT = 20 * 1024 * 1024


def dot(a, b, dims, precision=None):
    return lax.dot_general(a, b, (dims, ((), ())), preferred_element_type=F32, precision=precision)


def per_lane(scalars, count, channels):
    width = channels // count
    lane = lax.broadcasted_iota(jnp.int32, (1, channels), 1)
    row = jnp.zeros((1, channels), F32)
    for head in range(count):
        inside = (lane >= head * width) & (lane < (head + 1) * width)
        row = jnp.where(inside, scalars[head], row)
    return row


def split_two(value):
    high = value.astype(BF16)
    low = (value - high.astype(F32)).astype(BF16)
    return jnp.concatenate([high.astype(F32), low.astype(F32)], axis=0).astype(BF16)


def head_of(lane, width):
    if width & (width - 1) == 0:
        return lane >> (width.bit_length() - 1)
    return lane // width


def spread_matrix(count, channels):
    width = channels // count
    row = lax.broadcasted_iota(jnp.int32, (16, channels), 0)
    lane = lax.broadcasted_iota(jnp.int32, (16, channels), 1)
    return jnp.where((row & 7) == head_of(lane, width), 1.0, 0.0).astype(BF16)


def spread(pair, onehot):
    return dot(pair, onehot, ((0,), (0,)))


def reduce_kernel(
    heads, parts,
    rates_hbm, gains_hbm, codes_hbm, gates_hbm, taps_hbm, inputs_hbm, b_hbm, grad_hbm, c_hbm,
    near_out, far_out, front_out, logs_out, lead_out, gain_out, mixed_out, sigma_out,
    inputs, b_proj, grad, c_proj, *rest
):
    pays = rest[: parts - 1]
    rates, gains, codes, gates, taps, steps, scaled, grad_scaled, lead_pair, extra, sems = rest[
        parts - 1 :
    ]
    rows, channels = grad.shape
    chunks = rows // CHUNK
    sources = (
        rates_hbm, gains_hbm, codes_hbm, gates_hbm, taps_hbm, inputs_hbm, b_hbm, grad_hbm, c_hbm
    )
    targets = (rates, gains, codes, gates, taps, inputs, b_proj, grad, c_proj)
    copies = [
        pltpu.make_async_copy(source, target, sems.at[i])
        for i, (source, target) in enumerate(zip(sources, targets))
    ]
    for copy in copies:
        copy.start()
    for copy in copies[:4]:
        copy.wait()

    steps[...] = jnp.zeros_like(steps)
    steps[0:heads, :] = jnp.exp2(-codes[...].astype(F32))
    gate = gates[...]
    steps[6:7, :] = jnp.where(gate == 1, 1.0, 0.0).astype(F32)
    steps[7:8, :] = jnp.where(gate == 2, 1.0, 0.0).astype(F32)
    stacked = jnp.concatenate(
        [steps[:, j * CHUNK : (j + 1) * CHUNK] for j in range(chunks)], axis=0
    ).astype(BF16)
    row = lax.broadcasted_iota(jnp.int32, (CHUNK, CHUNK), 0)
    col = lax.broadcasted_iota(jnp.int32, (CHUNK, CHUNK), 1)
    upper = jnp.where(row <= col, 1.0, 0.0).astype(BF16)
    sums = dot(stacked, upper, ((1,), (0,)))
    sub = lax.broadcasted_iota(jnp.int32, (8, CHUNK), 0)
    rate = jnp.zeros((8, CHUNK), F32)
    for head in range(heads):
        rate = jnp.where(sub == head, rates[head], rate)
    cums, mids, befores = [], [], []
    before = jnp.zeros((8, 1), F32)
    for j in range(chunks):
        part = sums[8 * j : 8 * j + 8, :]
        cum = LOG_ONE * part[6:7, :] + LOG_TWO * part[7:8, :] - rate * part
        cums.append(cum)
        mids.append(cum[:, CHUNK // 2 - 1 : CHUNK // 2])
        befores.append(before)
        before = before + cum[:, CHUNK - 1 : CHUNK]
    for j in range(chunks):
        at = slice(j * CHUNK, (j + 1) * CHUNK)
        size = steps[:, at]
        near_out[0:16, at] = split_two(jnp.exp(cums[j] - mids[j]))
        near_out[16:32, at] = split_two(jnp.exp(mids[j] - cums[j]) * size)
        front_out[:, at] = split_two(jnp.exp(befores[j] + cums[j]))
        far_out[:, at] = split_two(jnp.exp(before - befores[j] - cums[j]) * size)
    lead_pair[...] = split_two(jnp.exp(-jnp.maximum(cums[0], -8.0)) * steps[:, 0:CHUNK])
    pick = lax.broadcasted_iota(jnp.int32, (8, CHUNK), 0)
    place = lax.broadcasted_iota(jnp.int32, (8, CHUNK), 1)
    chosen = jnp.where((pick == 0) | ((pick == 1) & (place < CHUNK // 2)), 1.0, 0.0)
    flat = dot(chosen.astype(BF16), stacked, ((1,), (1,)))
    owner = lax.broadcasted_iota(jnp.int32, (chunks, 8 * chunks), 1) >> 3
    chunk_at = lax.broadcasted_iota(jnp.int32, (chunks, 8 * chunks), 0)
    lane_rate = per_lane(rates, heads, channels)
    kind = lax.broadcasted_iota(jnp.int32, (8 * chunks, channels), 0) & 7
    lane = lax.broadcasted_iota(jnp.int32, (8 * chunks, channels), 1)
    lane_head = head_of(lane, channels // heads)
    mixer = jnp.where(kind == lane_head, -lane_rate, 0.0)
    mixer = jnp.where(kind == 6, LOG_ONE, jnp.where(kind == 7, LOG_TWO, mixer))
    table = []
    for which in range(2):
        own = jnp.where(owner == chunk_at, flat[which : which + 1, :], 0.0)
        table.append(dot(own, mixer, ((1,), (0,)), HIGHEST))
    whole = jnp.exp(table[0])
    middle = jnp.exp(table[1])
    rest_of = jnp.exp(table[0] - table[1])
    logs_out[0] = whole
    logs_out[1] = middle
    logs_out[2] = rest_of
    decay = jnp.exp(jnp.sum(table[0], axis=0, keepdims=True))
    first = decay.astype(BF16).astype(F32)
    extra[...] = jnp.zeros_like(extra)
    extra[0:1, :] = first
    extra[1:2, :] = decay - first

    onehot = spread_matrix(heads, channels)
    lead_out[...] = spread(lead_pair[:, 0:16], onehot)
    gain_out[...] = jnp.broadcast_to(per_lane(gains, heads, channels), (8, channels))
    for copy in copies[4:7]:
        copy.wait()
    shift = back_shift()
    nothing = jnp.zeros((16, channels), BF16)
    for at in range(0, rows, CHUNK):
        both = slice(at, at + CHUNK)
        if at == 0:
            block = jnp.concatenate([nothing, inputs[both, :]], axis=0)
        else:
            block = inputs[at - 16 : at + CHUNK, :]
        moved = dot(shift, block, ((1,), (0,)))
        preact = taps[3:4, :] * inputs[both, :].astype(F32)
        for k in range(3):
            preact = preact + taps[k : k + 1, :] * moved[k * CHUNK : (k + 1) * CHUNK, :]
        sigma = 0.5 * jnp.tanh(0.5 * preact) + 0.5
        mixed = preact * sigma
        scale = spread(far_out[:, both], onehot)
        sigma_out[both, :] = sigma
        mixed_out[both, :] = mixed
        scaled[both, :] = (mixed * scale).astype(BF16)
        if at == 0:
            extra[11:14, :] = scale[0:3, :]
    for copy in copies[7:]:
        copy.wait()
    state = dot(b_proj[...], scaled[...], ((0,), (0,))).astype(BF16)
    extra[2:5, :] = inputs[0:16, :].astype(F32)[0:3, :]
    extra[5:8, :] = inputs[rows - 16 : rows, :].astype(F32)[13:16, :]
    extra[8:11, 0:STATE] = b_proj[0:16, :].astype(F32)[0:3, :]
    for at in range(0, rows, STEP_ROWS):
        both = slice(at, at + STEP_ROWS)
        scale = spread(front_out[:, both], onehot)
        grad_scaled[both, :] = (grad[both, :].astype(F32) * scale).astype(BF16)
    adjoint = dot(c_proj[...], grad_scaled[...], ((0,), (0,))).astype(BF16)
    me = lax.axis_index("seq")
    for distance in range(1, parts):
        pay = pays[distance - 1]
        pay[0:STATE, :] = jnp.where(partner(me, distance, parts) > me, state, adjoint)
        pay[STATE : STATE + 16, :] = extra[...].astype(BF16)


def back_shift():
    row = lax.broadcasted_iota(jnp.int32, (3 * CHUNK, CHUNK + 16), 0)
    col = lax.broadcasted_iota(jnp.int32, (3 * CHUNK, CHUNK + 16), 1)
    at = (row & (CHUNK - 1)) + 13 + (row >> 7)
    return jnp.where(col == at, 1.0, 0.0).astype(BF16)


def tail_rows(held, source):
    return held[source, STATE : STATE + 16, :].astype(F32)


def first_preact(taps, halo, first):
    joined = jnp.concatenate([halo[0:3, :], first[0:8, :]], axis=0)
    preact = taps[0:1, :] * joined[0:8, :]
    for k in range(1, 4):
        preact = preact + taps[k : k + 1, :] * joined[k : k + 8, :]
    return preact


def first_change(taps, halo, first):
    true = first_preact(taps, halo, first)
    bare = first_preact(taps, jnp.zeros_like(halo), first)
    change = true * (0.5 * jnp.tanh(0.5 * true) + 0.5) - bare * (0.5 * jnp.tanh(0.5 * bare) + 0.5)
    row = lax.broadcasted_iota(jnp.int32, change.shape, 0)
    change = jnp.where(row < 3, change, 0.0)
    return jnp.concatenate([change, jnp.zeros_like(change)], axis=0)


def lane_tiles(channels):
    return [slice(at, min(at + 128, channels)) for at in range(0, channels, 128)]


def partner(me, distance, parts):
    return (me ^ distance) if parts & (parts - 1) == 0 else (me + distance) % parts


def sender(me, distance, parts):
    return (me ^ distance) if parts & (parts - 1) == 0 else (me + parts - distance) % parts


def sort_blocks(parts, pays, held):
    me = lax.axis_index("seq")
    held[me] = jnp.zeros(held.shape[1:], BF16)
    for distance in range(1, parts):
        held[sender(me, distance, parts)] = pays[distance - 1][...]


def merged_adjoint(parts, held):
    me = lax.axis_index("seq")
    running = jnp.zeros((STATE, held.shape[2]), F32)
    for source in range(parts - 1, 0, -1):
        tail = tail_rows(held, source)
        decay = tail[0:1, :] + tail[1:2, :]
        block = held[source, 0:STATE, :].astype(F32)
        running = jnp.where(source > me, block + decay * running, running)
    return running.astype(BF16)


def own_halo(held):
    me = lax.axis_index("seq")
    return jnp.where(me > 0, tail_rows(held, jnp.maximum(me - 1, 0))[5:8, :], 0.0)


def merged_state(parts, taps, held):
    me = lax.axis_index("seq")
    channels = held.shape[2]
    running = jnp.zeros((STATE, channels), F32)
    blank = jnp.zeros((5, channels), F32)
    tails = [tail_rows(held, source) for source in range(parts - 1)]
    for source in range(parts - 1):
        tail = tails[source]
        state = held[source, 0:STATE, :].astype(F32)
        if source > 0:
            first = jnp.concatenate([tail[2:5, :], blank], axis=0)
            scale = jnp.concatenate([tail[11:14, :], blank, blank, blank[0:3, :]], axis=0)
            change = first_change(taps, tails[source - 1][5:8, :], first)
            change = (change * scale).astype(BF16)
            row = lax.broadcasted_iota(jnp.int32, (16, STATE), 0)
            lines = jnp.concatenate([tail[8:11, 0:STATE], blank[:, 0:STATE]], axis=0)
            lines = jnp.concatenate([lines, jnp.zeros_like(lines)], axis=0)
            lines = jnp.where(row < 3, lines, 0.0).astype(BF16)
            state = state + dot(lines, change, ((0,), (0,)))
        decay = tail[0:1, :] + tail[1:2, :]
        running = jnp.where(source < me, state + decay * running, running)
    return running


def inner_kernel(
    heads, gains, near, far, logs, grad, mixed, sigma, b_proj, c_proj,
    base_out, grad_base, grad_weight, first_out,
    ahead_scores, behind_scores, mixed_scaled, mixed_low, grad_scaled, grad_low,
    mixed_fresh, grad_fresh,
):
    rows, channels = grad.shape
    chunks = rows // CHUNK
    blocks = [slice(j * CHUNK, (j + 1) * CHUNK) for j in range(chunks)]
    row = lax.broadcasted_iota(jnp.int32, (CHUNK, CHUNK), 0)
    col = lax.broadcasted_iota(jnp.int32, (CHUNK, CHUNK), 1)
    onehot = spread_matrix(heads, channels)
    gain = gains[0:1, :]
    for both in blocks:
        scale = spread(near[0:16, both], onehot)
        grad_scaled[both, :] = (grad[both, :].astype(F32) * scale).astype(BF16)
    for both in blocks:
        scale = spread(near[16:32, both], onehot)
        mixed_scaled[both, :] = (mixed[both, :] * scale).astype(BF16)
    for both in blocks:
        grad_fresh[both, :] = dot(c_proj[both, :], grad_scaled[both, :], ((0,), (0,)))
    for both in blocks:
        mixed_fresh[both, :] = dot(b_proj[both, :], mixed_scaled[both, :], ((0,), (0,)))
    for both in blocks:
        ahead = dot(c_proj[both, :], b_proj[both, :], ((1,), (1,)))
        ahead_scores[both, :] = jnp.where(row >= col, ahead, 0.0).astype(BF16)
    for both in blocks:
        behind = dot(b_proj[both, :], c_proj[both, :], ((1,), (1,)))
        behind_scores[both, :] = jnp.where(row <= col, behind, 0.0).astype(BF16)
    for lanes in lane_tiles(channels):
        adjoint = jnp.zeros((STATE, lanes.stop - lanes.start), F32)
        for j in range(chunks - 1, -1, -1):
            grad_low[blocks[j], lanes] = (adjoint * logs[2, j : j + 1, lanes]).astype(BF16)
            adjoint = logs[0, j : j + 1, lanes] * adjoint + (
                logs[1, j : j + 1, lanes] * grad_fresh[blocks[j], lanes]
            )
        state = jnp.zeros((STATE, lanes.stop - lanes.start), F32)
        for j in range(chunks):
            mixed_low[blocks[j], lanes] = (state * logs[1, j : j + 1, lanes]).astype(BF16)
            state = logs[0, j : j + 1, lanes] * state + (
                logs[2, j : j + 1, lanes] * mixed_fresh[blocks[j], lanes]
            )
    for both in blocks:
        inner = dot(
            jnp.concatenate([behind_scores[both, :], b_proj[both, :]], axis=1),
            jnp.concatenate([grad_scaled[both, :], grad_low[both, :]], axis=0),
            ((1,), (0,)),
        )
        slope = sigma[both, :] + mixed[both, :] * (1.0 - sigma[both, :])
        inner = gain * grad[both, :].astype(F32) + spread(near[16:32, both], onehot) * inner
        weight = spread(far[:, both], onehot)
        grad_base[both, :] = slope * inner
        grad_weight[both, :] = slope * weight
        if both.start == 0:
            first_out[0:8, :] = inner[0:8, :]
            first_out[8:16, :] = weight[0:8, :]
    for both in blocks:
        inner = dot(
            jnp.concatenate([ahead_scores[both, :], c_proj[both, :]], axis=1),
            jnp.concatenate([mixed_scaled[both, :], mixed_low[both, :]], axis=0),
            ((1,), (0,)),
        )
        base_out[both, :] = gain * mixed[both, :] + spread(near[0:16, both], onehot) * inner


def gradient_kernel(parts, taps, base, weight, unscaled, inputs, b_proj, *rest):
    pays = rest[: parts - 1]
    grad_out, tail_out, edge_out, window, exact, held = rest[parts - 1 :]
    rows, channels = base.shape
    chunks = rows // CHUNK
    sort_blocks(parts, pays, held)
    adjoint = merged_adjoint(parts, held)
    halo = own_halo(held)
    preact = first_preact(taps, halo, inputs[0:16, :].astype(F32))
    sigma = 0.5 * jnp.tanh(0.5 * preact) + 0.5
    slope = sigma + preact * sigma * (1.0 - sigma)
    window[rows : rows + 16, :] = jnp.zeros((16, channels), BF16)
    row = lax.broadcasted_iota(jnp.int32, (3 * CHUNK, CHUNK + 16), 0)
    col = lax.broadcasted_iota(jnp.int32, (3 * CHUNK, CHUNK + 16), 1)
    shift = jnp.where(col == (row & (CHUNK - 1)) + 3 - (row >> 7), 1.0, 0.0).astype(BF16)
    partial = [jnp.zeros((8, channels), F32) for _ in range(4)]
    for j in range(chunks):
        both = slice(j * CHUNK, (j + 1) * CHUNK)
        carried = dot(b_proj[both, :], adjoint, ((1,), (0,)))
        grad_pre = base[both, :] + weight[both, :] * carried
        if j == 0:
            first = slope * (unscaled[0:8, :] + unscaled[8:16, :] * carried[0:8, :])
            grad_pre = jnp.concatenate([first, grad_pre[8:, :]], axis=0)
        window[both, :] = grad_pre.astype(BF16)
        exact[both, :] = grad_pre
    for j in range(chunks):
        at = j * CHUNK
        both = slice(at, at + CHUNK)
        grad_pre = exact[both, :]
        moved = dot(shift, window[at : at + CHUNK + 16, :], ((1,), (0,)))
        x = inputs[both, :].astype(F32)
        result = taps[3:4, :] * grad_pre
        partial[3] = partial[3] + (grad_pre * x).reshape(CHUNK // 8, 8, channels).sum(axis=0)
        for k in range(3):
            part = moved[k * CHUNK : (k + 1) * CHUNK, :]
            result = result + taps[k : k + 1, :] * part
            partial[k] = partial[k] + (part * x).reshape(CHUNK // 8, 8, channels).sum(axis=0)
        grad_out[both, :] = result.astype(BF16)
        if j == chunks - 1:
            edge_out[...] = result[CHUNK - 16 :, :]
    for k in range(4):
        tap = jnp.sum(partial[k], axis=0, keepdims=True)
        for j in range(k, 3):
            tap = tap + first[j - k : j - k + 1, :] * halo[j : j + 1, :]
        tail_out[k : k + 1, :] = tap
    tail_out[4:7, :] = first[0:3, :]
    tail_out[7:8, :] = jnp.zeros((1, channels), F32)


def output_kernel(
    heads, parts, gains, taps, front, lead, base, inputs, b_proj, c_proj, grad_rows, *rest
):
    pays = rest[: parts - 1]
    out_hbm, grad_hbm, held, result_rows, sems = rest[parts - 1 :]
    rows, channels = base.shape
    grad_copy = pltpu.make_async_copy(grad_rows, grad_hbm, sems.at[0])
    grad_copy.start()
    sort_blocks(parts, pays, held)
    incoming = merged_state(parts, taps, held)
    onehot = spread_matrix(heads, channels)
    change = first_change(taps, own_halo(held), inputs[0:16, :].astype(F32))
    change_scaled = (change * lead[...]).astype(BF16)
    state = incoming + dot(b_proj[0:16, :], change_scaled, ((0,), (0,)))
    state = state.astype(BF16)
    row = lax.broadcasted_iota(jnp.int32, (16, 16), 0)
    col = lax.broadcasted_iota(jnp.int32, (16, 16), 1)
    scores = dot(c_proj[0:16, :], b_proj[0:16, :], ((1,), (1,)))
    scores = jnp.where(row >= col, scores, 0.0).astype(BF16)
    top = dot(c_proj[0:16, :], incoming.astype(BF16), ((1,), (0,)))
    top = top + dot(scores, change_scaled, ((1,), (0,)))
    top = top * spread(front[:, 0:16], onehot) + base[0:16, :]
    top = top + gains[0:1, :] * change
    for at in range(0, rows, CHUNK):
        both = slice(at, at + CHUNK)
        carried = dot(c_proj[both, :], state, ((1,), (0,)))
        result = base[both, :] + spread(front[:, both], onehot) * carried
        result_rows[both, :] = result.astype(BF16)
        if at == 0:
            result_rows[0:16, :] = top.astype(BF16)
    out_copy = pltpu.make_async_copy(result_rows, out_hbm, sems.at[1])
    out_copy.start()
    grad_copy.wait()
    out_copy.wait()


def finish_kernel(parts, scale, taps, tail, edge, *rest):
    others = rest[: parts - 1]
    unused, grad_hbm, conv_out, rows_low, sem = rest[parts - 1 :]
    channels = tail.shape[1]
    me = lax.axis_index("seq")
    after = jnp.zeros(tail.shape, F32)
    for distance in range(1, parts):
        here = sender(me, distance, parts) == me + 1
        after = jnp.where(here, others[distance - 1][...], after)
    row = lax.broadcasted_iota(jnp.int32, (16, channels), 0)
    result = edge[...]
    for r in range(3):
        extra = jnp.zeros((1, channels), F32)
        for k in range(r + 1):
            extra = extra + taps[k : k + 1, :] * after[4 + r - k : 5 + r - k, :]
        result = jnp.where(row == 13 + r, result + extra, result)
    rows_low[...] = result.astype(BF16)
    rows = grad_hbm.shape[0]
    copy = pltpu.make_async_copy(rows_low, grad_hbm.at[pl.ds(rows - 16, 16)], sem)
    copy.start()
    total = tail[0:4, :]
    for other in others:
        total = total + other[0:4, :]
    conv_out[...] = total * scale
    copy.wait()


def rotated(block, axis, distance):
    size = lax.axis_size(axis)
    return lax.ppermute(block, axis, [(i, partner(i, distance, size)) for i in range(size)])


def shards(
    inputs,
    b_proj,
    c_proj,
    step_codes,
    gate_codes,
    decay_rates,
    skip_gain,
    conv_weight,
    out_cotangent,
):
    rows, channels = inputs.shape
    heads = decay_rates.shape[0]
    parts = lax.axis_size("seq")
    chunks = rows // CHUNK
    hbm = pl.BlockSpec(memory_space=pltpu.HBM)
    vmem = pl.BlockSpec(memory_space=pltpu.VMEM)
    shape = jax.ShapeDtypeStruct
    dma = pltpu.SemaphoreType.DMA
    big = rows * channels

    def call(kernel, in_specs, out_specs, out_shape, scratch, products, aliases=None):
        return pl.pallas_call(
            kernel,
            in_specs=in_specs,
            out_specs=out_specs,
            out_shape=out_shape,
            scratch_shapes=scratch,
            input_output_aliases=aliases or {},
            compiler_params=pltpu.CompilerParams(vmem_limit_bytes=VMEM_LIMIT),
            cost_estimate=pl.CostEstimate(
                flops=products * 2 * big * 128, bytes_accessed=6 * big, transcendentals=big
            ),
        )

    def stay(array):
        return pltpu.with_memory_space_constraint(array, pltpu.HBM)

    pay = shape((STATE + 16, channels), BF16)
    narrow = shape((rows, channels), BF16)
    broad = shape((rows, channels), F32)
    slim = shape((rows, STATE), BF16)

    outs = call(
        functools.partial(reduce_kernel, heads, parts),
        [hbm] * 9,
        [vmem] * (11 + parts),
        [
            shape((32, rows), BF16),
            shape((16, rows), BF16),
            shape((16, rows), BF16),
            shape((3, chunks, channels), F32),
            shape((16, channels), F32),
            shape((8, channels), F32),
            broad,
            broad,
            narrow,
            slim,
            narrow,
            slim,
        ]
        + [pay] * (parts - 1),
        [
            pltpu.SMEM((heads,), F32),
            pltpu.SMEM((heads,), F32),
            pltpu.VMEM((heads, rows), jnp.int32),
            pltpu.VMEM((1, rows), jnp.int32),
            pltpu.VMEM((4, channels), F32),
            pltpu.VMEM((8, rows), F32),
            pltpu.VMEM((rows, channels), BF16),
            pltpu.VMEM((rows, channels), BF16),
            pltpu.VMEM((16, CHUNK), BF16),
            pltpu.VMEM((16, channels), F32),
            dma((9,)),
        ],
        4,
    )(
        stay(decay_rates),
        stay(skip_gain),
        stay(step_codes),
        stay(gate_codes.reshape(1, rows)),
        stay(conv_weight),
        stay(inputs),
        stay(b_proj),
        stay(out_cotangent),
        stay(c_proj),
    )
    near, far, front, logs, lead, gain, mixed, sigma = outs[:8]
    inputs, b_proj, out_cotangent, c_proj = outs[8:12]
    pays = [rotated(send, "seq", distance + 1) for distance, send in enumerate(outs[12:])]

    tile = pltpu.VMEM((rows, CHUNK), BF16)
    low = pltpu.VMEM((rows, channels), BF16)
    high = pltpu.VMEM((rows, channels), F32)
    base, grad_base, grad_weight, unscaled = call(
        functools.partial(inner_kernel, heads),
        [vmem] * 9,
        [vmem] * 4,
        [broad] * 3 + [shape((16, channels), F32)],
        [tile, tile, low, low, low, low, high, high],
        10,
    )(gain, near, far, logs, out_cotangent, mixed, sigma, b_proj, c_proj)

    held = pltpu.VMEM((parts, STATE + 16, channels), BF16)
    grad_rows, tail, edge = call(
        functools.partial(gradient_kernel, parts),
        [vmem] * (5 + parts),
        [vmem] * 3,
        [narrow, shape((8, channels), F32), shape((16, channels), F32)],
        [pltpu.VMEM((rows + 16, channels), BF16), high, held],
        2,
    )(conv_weight, grad_base, grad_weight, unscaled, inputs, b_proj, *pays)
    tails = [rotated(tail, "seq", distance) for distance in range(1, parts)]

    layer_out, grad_rows = call(
        functools.partial(output_kernel, heads, parts),
        [vmem] * (8 + parts),
        [hbm, hbm],
        [narrow, narrow],
        [held, low, dma((2,))],
        2,
    )(gain, conv_weight, front, lead, base, inputs, b_proj, c_proj, grad_rows, *pays)

    scale = float((rows * parts) ** -0.5)
    input_grad, conv_grad = call(
        functools.partial(finish_kernel, parts, scale),
        [vmem] * (2 + parts) + [hbm],
        [hbm, vmem],
        [narrow, shape((4, channels), F32)],
        [pltpu.VMEM((16, channels), BF16), dma],
        0,
        {parts + 2: 0},
    )(conv_weight, tail, edge, *tails, grad_rows)
    return layer_out, input_grad, conv_grad


def solution(mesh):
    in_specs = (
        P(("groups", "seq"), ("head", "sub")),
        P(("groups", "seq"), None),
        P(("groups", "seq"), None),
        P(("head", "sub"), ("groups", "seq")),
        P(("groups", "seq")),
        P(("head", "sub")),
        P(("head", "sub")),
        P(None, ("head", "sub")),
        P(("groups", "seq"), ("head", "sub")),
    )
    out_specs = (
        P(("groups", "seq"), ("head", "sub")),
        P(("groups", "seq"), ("head", "sub")),
        P("groups", ("head", "sub")),
    )
    return jax.shard_map(shards, mesh=mesh, in_specs=in_specs, out_specs=out_specs, check_vma=False)
```
